32 devices in a mesh: rep: 8 (over z, x), fsdp: 4 (over y, core).
Axes of the slice: x: 2, y: 2, z: 4, core: 2. Of those that a mesh axis runs over, the one named last changes fastest.
Arguments:
- images: bfloat16 [512, 197, 384], P(('rep', 'fsdp')), may hold values from -6 to 6
- cotangent: bfloat16 [512, 197, 384], P(('rep', 'fsdp')), may hold values from -6 to 6
- counts: int32 [32], P(('rep', 'fsdp')), may hold values from 1 to 16, as said below
- w_qkv: float32 [384, 1152], P('fsdp'), may hold values from -0.3125 to 0.3125
- w_proj: float32 [384, 384], P('fsdp'), may hold values from -2.5 to 2.5
- w_fc1: float32 [384, 1536], P('fsdp'), may hold values from -0.3125 to 0.3125
- w_fc2: float32 [1536, 384], P(None, 'fsdp'), may hold values from -0.15625 to 0.15625
- gains: float32 [2, 384], P(None, 'fsdp'), may hold values from 0.1 to 1.9
- biases: float32 [10, 384], P(None, 'fsdp'), may hold values from -3 to 3
- mom_qkv: float32 [384, 1152], P('fsdp'), may hold values from -10 to 10
- mom_proj: float32 [384, 384], P('fsdp'), may hold values from -1.75 to 1.75
- mom_fc1: float32 [384, 1536], P('fsdp'), may hold values from -5 to 5
- mom_fc2: float32 [1536, 384], P(None, 'fsdp'), may hold values from -8 to 8
- gains_first: float32 [2, 384], P(None, 'fsdp'), may hold values from -6 to 6
- gains_second: float32 [2, 384], P(None, 'fsdp'), may hold values from 0.985 to 9.85
- biases_first: float32 [10, 384], P(None, 'fsdp'), may hold values from -6 to 6
- biases_second: float32 [10, 384], P(None, 'fsdp'), may hold values from 0.985 to 9.85
Outputs:
- block_output: bfloat16 [512, 197, 384], P(('rep', 'fsdp'))
- input_grad: bfloat16 [512, 197, 384], P(('rep', 'fsdp'))
- grad_qkv: float32 [384, 1152], P('fsdp')
- grad_proj: float32 [384, 384], P('fsdp')
- grad_fc1: float32 [384, 1536], P('fsdp')
- grad_fc2: float32 [1536, 384], P(None, 'fsdp')
- grad_gains: float32 [2, 384], P(None, 'fsdp')
- grad_biases: float32 [10, 384], P(None, 'fsdp')
- new_qkv: float32 [384, 1152], P('fsdp')
- new_proj: float32 [384, 384], P('fsdp')
- new_fc1: float32 [384, 1536], P('fsdp')
- new_fc2: float32 [1536, 384], P(None, 'fsdp')
- new_gains: float32 [2, 384], P(None, 'fsdp')
- new_biases: float32 [10, 384], P(None, 'fsdp')
- next_mom_qkv: float32 [384, 1152], P('fsdp')
- next_mom_proj: float32 [384, 384], P('fsdp')
- next_mom_fc1: float32 [384, 1536], P('fsdp')
- next_mom_fc2: float32 [1536, 384], P(None, 'fsdp')
- next_gains_first: float32 [2, 384], P(None, 'fsdp')
- next_gains_second: float32 [2, 384], P(None, 'fsdp')
- next_biases_first: float32 [10, 384], P(None, 'fsdp')
- next_biases_second: float32 [10, 384], P(None, 'fsdp')
The draws below stay inside these ranges and needn't reach their ends.
Inputs may be any that keep to these rules, and one draw needn't show every extreme that they name: counts[d] of device d's 16 slots, the first ones, hold images; at least one device holds 16.
All inputs are finite; a program needn't handle non-finite values.
Results may differ from the reference program's by a relative error of at most 0.0095.
The reference program's roundings to bfloat16 on the way count: a program that leaves them out, or rounds other values in their place, can miss the bound.
Values may be sent and summed in bfloat16 or wider, within the bound.
No kernel may reach another device: no remote copies, remote signals or barrier semaphores. Data moves between devices by JAX's collectives and lax.ppermute only.
A program may use at most 320 MiB of HBM per device.

```python
import math
import jax
import jax.numpy as jnp
from jax import lax

D = 384
H = 6
HD = 64
F = 1536
TOKS = 197
SLOTS = 16
NS_ITERS = 5
ADAM_STEP = 3
SHARDS = 32
IMAGES = 512


def draw_counts(key, part):
    key_first, key_second, key_third = jax.random.split(jax.random.fold_in(key, 7), 3)
    lower_draw = jax.random.randint(key_first, (SHARDS,), 1, SLOTS + 1)
    upper_draw = jax.random.randint(key_second, (SHARDS,), 1, SLOTS + 1)
    chosen = jax.random.randint(key_third, (), 0, SHARDS)
    device_loads = jnp.minimum(lower_draw, upper_draw)
    return jnp.where(jnp.arange(SHARDS) == chosen, SLOTS, device_loads).astype(jnp.int32)


def block_levels(own_key, shape, cuts, least, high):
    level = 1.0
    for position, parts in cuts:
        heights = jax.random.uniform(jax.random.fold_in(jax.random.fold_in(own_key, 6), position), (parts,), jnp.float32, least / len(cuts), high / len(cuts))
        level = level * jnp.repeat(jnp.exp(heights), shape[position] // parts).reshape((-1,) + (1,) * (len(shape) - 1 - position))
    return level


def bell_draw(key, shape, spread, limit, shards=(), kind=jnp.bfloat16):
    values = spread * jax.random.normal(key, shape, jnp.float32)
    if shards:
        values = values * block_levels(key, shape, shards, -0.22, 0.18)
    return jnp.clip(values, -limit, limit).astype(kind)


def setup_inputs(seed: int = 0) -> dict:
    arg_keys = jax.random.split(jax.random.key(seed), 18)
    return {
        "images": bell_draw(arg_keys[0], (IMAGES, TOKS, D), 1.0, 6.0, ((0, 32),)),
        "cotangent": bell_draw(arg_keys[1], (IMAGES, TOKS, D), 1.0, 6.0, ((0, 32),)),
        "counts": draw_counts(jax.random.fold_in(arg_keys[17], 71), 0),
        "w_qkv": bell_draw(arg_keys[3], (D, 3 * D), D ** -0.5, 0.3125, ((0, 4),), jnp.float32),
        "w_proj": bell_draw(arg_keys[4], (D, D), H ** -0.5, 2.5, ((0, 4),), jnp.float32),
        "w_fc1": bell_draw(arg_keys[5], (D, F), D ** -0.5, 0.3125, ((0, 4),), jnp.float32),
        "w_fc2": bell_draw(arg_keys[6], (F, D), F ** -0.5, 0.15625, ((1, 4),), jnp.float32),
        "gains": jnp.clip(1.0 + 0.18 * jax.random.normal(arg_keys[7], (2, D), jnp.float32), 0.1, 1.9),
        "biases": bell_draw(arg_keys[8], (6 + F // D, D), 0.5, 3.0, ((1, 4),), jnp.float32),
        "mom_qkv": bell_draw(arg_keys[9], (D, 3 * D), (0.3 * (SLOTS * TOKS) ** 0.5 * (3 * SHARDS) ** -0.5), 10.0, ((0, 4),), jnp.float32),
        "mom_proj": bell_draw(arg_keys[10], (D, D), (0.05 * (SLOTS * TOKS) ** 0.5 * (3 * SHARDS) ** -0.5), 1.75, ((0, 4),), jnp.float32),
        "mom_fc1": bell_draw(arg_keys[11], (D, F), (0.15 * (SLOTS * TOKS) ** 0.5 * (3 * SHARDS) ** -0.5), 5.0, ((0, 4),), jnp.float32),
        "mom_fc2": bell_draw(arg_keys[12], (F, D), (0.25 * (SLOTS * TOKS) ** 0.5 * (3 * SHARDS) ** -0.5), 8.0, ((1, 4),), jnp.float32),
        "gains_first": bell_draw(arg_keys[13], (2, D), (0.1 * (SLOTS * TOKS) ** 0.5 * SHARDS ** -0.5), 6.0, ((1, 4),), jnp.float32),
        "gains_second": jnp.clip(jnp.exp(math.log(9.85) - 2.3025851 * jax.random.uniform(arg_keys[14], (2, D), jnp.float32) ** block_levels(arg_keys[14], (2, D), ((1, 4),), -0.2, 0.2)), 0.985, 9.85),
        "biases_first": bell_draw(arg_keys[15], (6 + F // D, D), (0.1 * (SLOTS * TOKS) ** 0.5 * SHARDS ** -0.5), 6.0, ((1, 4),), jnp.float32),
        "biases_second": jnp.clip(jnp.exp(math.log(9.85) - 2.3025851 * jax.random.uniform(arg_keys[16], (6 + F // D, D), jnp.float32) ** block_levels(arg_keys[16], (6 + F // D, D), ((1, 4),), -0.2, 0.2)), 0.985, 9.85),
    }


NORM_EPSILON = 1e-06
ORTHO_EPSILON = 1e-07
COEFF_FIRST = 3.4445
COEFF_SECOND = -4.775
COEFF_THIRD = 2.0315
MUON_RATE = 0.3
MUON_MOMENTUM = 0.95
ADAM_RATE = 0.2
ADAM_FIRST = 0.9
ADAM_SECOND = 0.95
ADAM_EPSILON = 1e-08
ADAM_DECAY = 0.25

def layer_norm(values, gain, shift):
    centred = values - lax.optimization_barrier(jnp.mean(values, axis=-1, keepdims=True))
    inverse = lax.rsqrt(lax.optimization_barrier(jnp.mean(centred * centred, axis=-1, keepdims=True)) + NORM_EPSILON)
    normed = centred * inverse
    return (normed * gain + shift, normed, inverse)

def norm_back(grad_out, normed, inverse, gain):
    scaled = grad_out * gain
    return inverse * (scaled - lax.optimization_barrier(jnp.mean(scaled, axis=-1, keepdims=True)) - normed * lax.optimization_barrier(jnp.mean(scaled * normed, axis=-1, keepdims=True)))

def normal_cdf(pre_act):
    return 0.5 * (1.0 + lax.erf(pre_act * (1.0 / math.sqrt(2.0))))

def gelu_value(pre_act):
    return pre_act * normal_cdf(pre_act)

def gelu_slope(pre_act):
    density = jnp.exp(-0.5 * pre_act * pre_act) * (1.0 / math.sqrt(2.0 * math.pi))
    return normal_cdf(pre_act) + pre_act * density

def make_live(live_count, slot_count, tokens):
    live_slots = jnp.arange(slot_count, dtype=jnp.int32) < live_count
    return jnp.broadcast_to(live_slots[:, None], (slot_count, tokens)).reshape(slot_count * tokens, 1)

def forward_pass(images, live_rows, params):
    w_qkv, w_proj, w_fc1, w_fc2, gains, biases = params
    slot_count, tokens, model_width = images.shape
    row_count = slot_count * tokens
    hidden = w_fc1.shape[1]
    gain_vec = gains.astype(jnp.float32)
    shift_vec = biases.astype(jnp.float32)
    inputs = images.astype(jnp.float32).reshape(row_count, model_width)
    normed_in, norm_one, inv_one = layer_norm(inputs, gain_vec[0], shift_vec[0])
    attn_in = normed_in.astype(jnp.bfloat16)
    qkv_shift = jnp.concatenate([shift_vec[1], jnp.zeros_like(shift_vec[1]), shift_vec[2]])
    projected = (jnp.dot(attn_in, w_qkv, preferred_element_type=jnp.float32) + qkv_shift).astype(jnp.bfloat16)
    projected = projected.reshape(slot_count, tokens, 3, H, HD)
    query_h = projected[:, :, 0]
    key_h = projected[:, :, 1]
    value_h = projected[:, :, 2]
    score_scale = 1.0 / math.sqrt(HD)
    scores = jnp.einsum('bshd,bthd->bhst', query_h.astype(jnp.float32), key_h.astype(jnp.float32)) * score_scale
    log_total = jnp.log(lax.optimization_barrier(jnp.sum(jnp.exp(scores), axis=-1, keepdims=True)))
    probs_b = jnp.exp(scores - log_total).astype(jnp.bfloat16)
    attended = jnp.einsum('bhst,bthd->bshd', probs_b.astype(jnp.float32), value_h.astype(jnp.float32))
    attended = attended.astype(jnp.bfloat16).reshape(row_count, model_width)
    residual = inputs + jnp.dot(attended, w_proj, preferred_element_type=jnp.float32) + shift_vec[3]
    normed_mid, norm_two, inv_two = layer_norm(residual, gain_vec[1], shift_vec[4])
    mlp_in = normed_mid.astype(jnp.bfloat16)
    pre_act = jnp.dot(mlp_in, w_fc1, preferred_element_type=jnp.float32) + shift_vec[6:].reshape(hidden)
    activated = gelu_value(pre_act).astype(jnp.bfloat16)
    outputs = residual + jnp.dot(activated, w_fc2, preferred_element_type=jnp.float32) + shift_vec[5]
    block_out = jnp.where(live_rows, outputs, 0.0).astype(jnp.bfloat16).reshape(slot_count, tokens, model_width)
    saved = (norm_one, inv_one, attn_in, query_h, key_h, value_h, log_total, attended, norm_two, inv_two, mlp_in, pre_act, activated)
    return (block_out, saved)

def backward_pass(cotangent, live_rows, saved, params):
    w_qkv, w_proj, w_fc1, w_fc2, gains, biases = params
    norm_one, inv_one, attn_in, query_h, key_h, value_h, log_total, attended, norm_two, inv_two, mlp_in, pre_act, activated = saved
    slot_count, tokens, model_width = cotangent.shape
    row_count = slot_count * tokens
    hidden = w_fc1.shape[1]
    gain_vec = gains.astype(jnp.float32)
    out_grad = jnp.where(live_rows, cotangent.reshape(row_count, model_width), jnp.zeros((), jnp.bfloat16))
    out_float = out_grad.astype(jnp.float32)
    grad_fc2 = jnp.dot(activated.T, out_grad, preferred_element_type=jnp.float32)
    pre_grad = jnp.dot(out_grad, w_fc2.T, preferred_element_type=jnp.float32) * gelu_slope(pre_act)
    pre_grad_b = pre_grad.astype(jnp.bfloat16)
    grad_fc1 = jnp.dot(mlp_in.T, pre_grad_b, preferred_element_type=jnp.float32)
    mid_grad = jnp.dot(pre_grad_b, w_fc1.T, preferred_element_type=jnp.float32)
    resid_grad = out_float + norm_back(mid_grad, norm_two, inv_two, gain_vec[1])
    resid_grad_b = resid_grad.astype(jnp.bfloat16)
    grad_proj = jnp.dot(attended.T, resid_grad_b, preferred_element_type=jnp.float32)
    attn_grad = jnp.dot(resid_grad_b, w_proj.T, preferred_element_type=jnp.float32).astype(jnp.bfloat16)
    attn_grad = attn_grad.reshape(slot_count, tokens, H, HD)
    score_scale = 1.0 / math.sqrt(HD)
    scores = jnp.einsum('bshd,bthd->bhst', query_h.astype(jnp.float32), key_h.astype(jnp.float32)) * score_scale
    attn_probs = jnp.exp(scores - log_total)
    probs_b = attn_probs.astype(jnp.bfloat16)
    value_grad = jnp.einsum('bhst,bshd->bthd', probs_b.astype(jnp.float32), attn_grad.astype(jnp.float32))
    prob_grad = jnp.einsum('bshd,bthd->bhst', attn_grad.astype(jnp.float32), value_h.astype(jnp.float32))
    inner_sum = lax.optimization_barrier(jnp.sum(attn_probs * prob_grad, axis=-1, keepdims=True))
    score_grad = (attn_probs * (prob_grad - inner_sum) * score_scale).astype(jnp.bfloat16)
    query_grad = jnp.einsum('bhst,bthd->bshd', score_grad.astype(jnp.float32), key_h.astype(jnp.float32))
    key_grad = jnp.einsum('bhst,bshd->bthd', score_grad.astype(jnp.float32), query_h.astype(jnp.float32))
    qkv_grad = jnp.stack([query_grad, key_grad, value_grad], axis=2).reshape(row_count, 3 * model_width)
    qkv_grad_b = qkv_grad.astype(jnp.bfloat16)
    grad_qkv = jnp.dot(attn_in.T, qkv_grad_b, preferred_element_type=jnp.float32)
    in_grad = jnp.dot(qkv_grad_b, w_qkv.T, preferred_element_type=jnp.float32)
    input_grad = (resid_grad + norm_back(in_grad, norm_one, inv_one, gain_vec[0])).astype(jnp.bfloat16)
    input_grad = input_grad.reshape(slot_count, tokens, model_width)
    grad_gains = jnp.stack([lax.optimization_barrier(jnp.sum(in_grad * norm_one, axis=0)), lax.optimization_barrier(jnp.sum(mid_grad * norm_two, axis=0))])
    vector_rows = jnp.stack([lax.optimization_barrier(jnp.sum(in_grad, axis=0)), lax.optimization_barrier(jnp.sum(query_grad.reshape(row_count, model_width), axis=0)), lax.optimization_barrier(jnp.sum(value_grad.reshape(row_count, model_width), axis=0)), lax.optimization_barrier(jnp.sum(resid_grad, axis=0)), lax.optimization_barrier(jnp.sum(mid_grad, axis=0)), lax.optimization_barrier(jnp.sum(out_float, axis=0))])
    grad_biases = jnp.concatenate([vector_rows, lax.optimization_barrier(jnp.sum(pre_grad, axis=0)).reshape(hidden // model_width, model_width)], axis=0)
    return (input_grad, (grad_qkv, grad_proj, grad_fc1, grad_fc2, grad_gains, grad_biases))

def orthogonalize(matrix):
    norm_value = jnp.sqrt(jnp.sum(matrix * matrix))
    current = matrix / (norm_value + ORTHO_EPSILON)
    for iteration in range(NS_ITERS):
        square = jnp.dot(current, current.T, precision=lax.Precision.HIGHEST)
        polynomial = COEFF_SECOND * square + COEFF_THIRD * jnp.dot(square, square, precision=lax.Precision.HIGHEST)
        current = COEFF_FIRST * current + jnp.dot(polynomial, current, precision=lax.Precision.HIGHEST)
    return current

def adam_update(parameter, gradient, first_state, second_state):
    next_first = ADAM_FIRST * first_state + (1.0 - ADAM_FIRST) * gradient
    next_second = ADAM_SECOND * second_state + (1.0 - ADAM_SECOND) * gradient * gradient
    first_hat = next_first / (1.0 - ADAM_FIRST ** ADAM_STEP)
    second_hat = next_second / (1.0 - ADAM_SECOND ** ADAM_STEP)
    updated = parameter - ADAM_RATE * (first_hat / (jnp.sqrt(second_hat) + ADAM_EPSILON) + ADAM_DECAY * parameter)
    return (updated, next_first, next_second)

def muon_factor(row_total, column_total):
    return math.sqrt(max(1.0, row_total / column_total))

def reference(images, cotangent, counts, w_qkv, w_proj, w_fc1, w_fc2, gains, biases, mom_qkv, mom_proj, mom_fc1, mom_fc2, gains_first, gains_second, biases_first, biases_second):
    params = (w_qkv.astype(jnp.bfloat16), w_proj.astype(jnp.bfloat16), w_fc1.astype(jnp.bfloat16), w_fc2.astype(jnp.bfloat16), gains.astype(jnp.bfloat16), biases.astype(jnp.bfloat16))
    image_blocks = images.reshape(SHARDS, SLOTS, TOKS, D)
    cot_blocks = cotangent.reshape(SHARDS, SLOTS, TOKS, D)

    def device_step(totals, inputs):
        block_images, block_cot, live_count = inputs
        live_rows = make_live(live_count, SLOTS, TOKS)
        block_out, saved = forward_pass(block_images, live_rows, params)
        input_grad, block_grads = backward_pass(block_cot, live_rows, saved, params)
        totals = jax.tree.map(lambda left_side, right_side: left_side + right_side, totals, block_grads)
        return (totals, (block_out, input_grad))
    initial = (jnp.zeros((D, 3 * D), jnp.float32), jnp.zeros((D, D), jnp.float32), jnp.zeros((D, F), jnp.float32), jnp.zeros((F, D), jnp.float32), jnp.zeros((2, D), jnp.float32), jnp.zeros((6 + F // D, D), jnp.float32))
    totals, (out_blocks, grad_blocks) = lax.scan(device_step, initial, (image_blocks, cot_blocks, counts))
    block_output = out_blocks.reshape(IMAGES, TOKS, D)
    input_grad = grad_blocks.reshape(IMAGES, TOKS, D)
    grad_qkv, grad_proj, grad_fc1, grad_fc2, grad_gains, grad_biases = tuple((item / SHARDS for item in totals))
    next_qkv = MUON_MOMENTUM * mom_qkv + grad_qkv
    next_proj = MUON_MOMENTUM * mom_proj + grad_proj
    next_fc1 = MUON_MOMENTUM * mom_fc1 + grad_fc1
    next_fc2 = MUON_MOMENTUM * mom_fc2 + grad_fc2
    new_qkv = w_qkv - MUON_RATE * muon_factor(D, 3 * D) * orthogonalize(next_qkv)
    new_proj = w_proj - MUON_RATE * muon_factor(D, D) * orthogonalize(next_proj)
    new_fc1 = w_fc1 - MUON_RATE * muon_factor(D, F) * orthogonalize(next_fc1)
    new_fc2 = w_fc2 - MUON_RATE * muon_factor(F, D) * orthogonalize(next_fc2.T).T
    new_gains, next_gains_first, next_gains_second = adam_update(gains, grad_gains, gains_first, gains_second)
    new_biases, next_biases_first, next_biases_second = adam_update(biases, grad_biases, biases_first, biases_second)
    return (block_output, input_grad, grad_qkv, grad_proj, grad_fc1, grad_fc2, grad_gains, grad_biases, new_qkv, new_proj, new_fc1, new_fc2, new_gains, new_biases, next_qkv, next_proj, next_fc1, next_fc2, next_gains_first, next_gains_second, next_biases_first, next_biases_second)
```

```python
import functools, math
import jax, jax.numpy as jnp
from jax import lax
from jax.experimental import pallas as pl
from jax.experimental.pallas import tpu as pltpu


from jax.sharding import PartitionSpec as P

NS_ITERS = 5
ADAM_STEP = 3
ORTHO_EPSILON = 1e-07
COEFF_FIRST = 3.4445
COEFF_SECOND = -4.775
COEFF_THIRD = 2.0315
MUON_RATE = 0.3
MUON_MOMENTUM = 0.95
ADAM_RATE = 0.2
ADAM_FIRST = 0.9
ADAM_SECOND = 0.95
ADAM_EPSILON = 1e-08
ADAM_DECAY = 0.25

D=384; H=6; HD=64; F=1536; T=197; TP=208
EPS=1e-6
f32=jnp.float32; bf16=jnp.bfloat16
C2=(1.0/math.sqrt(HD))*math.log2(math.e)

def dot(a,b): return jnp.dot(a,b,preferred_element_type=f32)
def dot_nt(a,b): return lax.dot_general(a,b,(((1,),(1,)),((),())),preferred_element_type=f32)
def dot_tn(a,b): return lax.dot_general(a,b,(((0,),(0,)),((),())),preferred_element_type=f32)

def pad_rows(v):
    return jnp.concatenate([v, jnp.zeros((TP-T,)+v.shape[1:], v.dtype)], axis=0)

def norm(x):
    mu=jnp.mean(x,axis=-1,keepdims=True)
    xc=x-mu
    r=lax.rsqrt(jnp.mean(xc*xc,axis=-1,keepdims=True)+EPS)
    return xc*r, r

def col8(v):
    return jnp.sum(v.reshape(v.shape[0]//8,8,v.shape[1]),axis=0)

def kA(n_ref, *refs):
    @pl.when(pl.program_id(0) < n_ref[0])
    def _():
        kA_step(*refs)


def kA_step(x_ref, w_ref, g_ref, b_ref, qb_ref, qkv_ref, o_ref, lse_ref):
    x=pad_rows(x_ref[0].astype(f32))
    n1,_=norm(x)
    a=(n1*g_ref[...]+b_ref[...]).astype(bf16)
    qkv=(dot(a,w_ref[...])+qb_ref[...]).astype(bf16)
    qkv_ref[0]=qkv
    lane=lax.broadcasted_iota(jnp.int32,(TP,128),1)
    lo=lane<HD
    colm=lax.broadcasted_iota(jnp.int32,(TP,TP),1)<T
    lse=jnp.zeros((TP,128),f32)
    for hp in range(H//2):
        q=qkv[:,hp*128:(hp+1)*128]; k=qkv[:,D+hp*128:D+(hp+1)*128]; v=qkv[:,2*D+hp*128:2*D+(hp+1)*128]
        o=None
        for s_ in range(2):
            sel=lo if s_==0 else jnp.logical_not(lo)
            qm=jnp.where(sel,q,jnp.zeros_like(q)); vm=jnp.where(sel,v,jnp.zeros_like(v))
            t=jnp.where(colm,dot_nt(qm,k)*C2,-1e30)
            e=jnp.exp2(t)
            l2=jnp.log2(jnp.sum(e,axis=-1,keepdims=True))
            p=jnp.exp2(t-l2).astype(bf16)
            po=dot(p,vm)
            o=po if o is None else o+po
            lse=jnp.where(lane==hp*2+s_,l2,lse)
        o_ref[0,:,hp*128:(hp+1)*128]=o.astype(bf16)
    lse_ref[0]=lse

PHI_T = 0.28
PHI_C = (0.11652077999788102, 0.06749674653879187, 0.2689101818992952,
         -0.2369935012534717, 0.38987403003604115, -0.10580824648054844)
HALF_LOG2E = -0.5 * math.log2(math.e)
DENSITY = 1.0 / math.sqrt(2.0 * math.pi)


def gelu_parts(z):
    t = 1.0 / (1.0 + PHI_T * jnp.abs(z))
    bell = jnp.exp2((z * z) * HALF_LOG2E)
    poly = PHI_C[5] * t + PHI_C[4]
    for k in (3, 2, 1, 0):
        poly = poly * t + PHI_C[k]
    tail = (poly * t) * bell
    cdf = jnp.where(z < 0.0, tail, 1.0 - tail)
    return z * cdf, cdf + (z * DENSITY) * bell


FC=512
def kB(n_ref, *refs):
    @pl.when(pl.program_id(0) < n_ref[0])
    def _():
        kB_step(*refs)


def kB_step(x_ref, o_ref, cot_ref, wp_ref, w1_ref, w2_ref, vec_ref, bu_ref,
       out_ref, dh_ref, do_ref, gp_ref, g1_ref, g2t_ref, vg_ref, gbu_ref):
    i=pl.program_id(0)
    @pl.when(i==0)
    def _():
        gp_ref[...]=jnp.zeros_like(gp_ref); g1_ref[...]=jnp.zeros_like(g1_ref); g2t_ref[...]=jnp.zeros_like(g2t_ref)
        vg_ref[...]=jnp.zeros_like(vg_ref); gbu_ref[...]=jnp.zeros_like(gbu_ref)
    bo=vec_ref[0:1,:]; g2=vec_ref[1:2,:]; b2=vec_ref[2:3,:]; bd=vec_ref[3:4,:]
    x=pad_rows(x_ref[0].astype(f32))
    o=o_ref[0]
    h=x+dot(o,wp_ref[...])+bo
    n2,r2=norm(h)
    c=(n2*g2+b2).astype(bf16)
    dyf=pad_rows(cot_ref[0].astype(f32))
    dy=dyf.astype(bf16)
    cT=c.T; dyT=dy.T
    acc=None; dc=None
    for j in range(F//FC):
        sl=slice(j*FC,(j+1)*FC)
        w1=w1_ref[:,sl]; w2=w2_ref[sl,:]
        z=dot(c,w1)+bu_ref[:,sl]
        u,slope=gelu_parts(z)
        u=u.astype(bf16)
        t=dot(u,w2); acc=t if acc is None else acc+t
        dz=dot_nt(dy,w2)*slope
        dzb=dz.astype(bf16)
        t=dot_nt(dzb,w1); dc=t if dc is None else dc+t
        g1_ref[:,sl]+=dot(cT,dzb)
        g2t_ref[:,sl]+=dot(dyT,u)
        gbu_ref[:,sl]+=col8(dz)
    out_ref[0]=(h+acc+bd)[:T].astype(bf16)
    e2=dc*g2
    dh=dyf+r2*(e2-jnp.mean(e2,axis=-1,keepdims=True)-n2*jnp.mean(e2*n2,axis=-1,keepdims=True))
    dh_ref[0]=dh
    dhb=dh.astype(bf16)
    gp_ref[...]+=dot(o.T,dhb)
    do_ref[0]=dot_nt(dhb,wp_ref[...]).astype(bf16)
    vg_ref[0:8]+=col8(dc*n2); vg_ref[8:16]+=col8(dh); vg_ref[16:24]+=col8(dc); vg_ref[24:32]+=col8(dyf)

def kC(n_ref, *refs):
    @pl.when(pl.program_id(0) < n_ref[0])
    def _():
        kC_step(*refs)


def kC_step(x_ref, qkv_ref, lse_ref, do_ref, dh_ref, w_ref, g_ref, b_ref,
       ig_ref, gq_ref, vg_ref, dqkv_s):
    i=pl.program_id(0)
    @pl.when(i==0)
    def _():
        gq_ref[...]=jnp.zeros_like(gq_ref); vg_ref[...]=jnp.zeros_like(vg_ref)
    x=pad_rows(x_ref[0].astype(f32))
    n1,r1=norm(x)
    a=(n1*g_ref[...]+b_ref[...]).astype(bf16)
    aT=a.T
    lane=lax.broadcasted_iota(jnp.int32,(TP,128),1)
    lo=lane<HD
    colm=lax.broadcasted_iota(jnp.int32,(TP,TP),1)<T
    lse=lse_ref[0]
    for hp in range(H//2):
        pr=slice(hp*128,(hp+1)*128); kr=slice(D+hp*128,D+(hp+1)*128); vr=slice(2*D+hp*128,2*D+(hp+1)*128)
        q=qkv_ref[0,:,pr]; k=qkv_ref[0,:,kr]; v=qkv_ref[0,:,vr]; do=do_ref[0,:,pr]
        dq=dk=dv=None
        for s_ in range(2):
            sel=lo if s_==0 else jnp.logical_not(lo)
            z=jnp.zeros_like(q)
            qm=jnp.where(sel,q,z); km=jnp.where(sel,k,z); dom=jnp.where(sel,do,z)
            hh=hp*2+s_
            t=jnp.where(colm,dot_nt(qm,k)*C2,-1e30)
            p=jnp.exp2(t-lse[:,hh:hh+1])
            pb=p.astype(bf16)
            dp=dot_nt(dom,v)
            delta=jnp.sum(p*dp,axis=-1,keepdims=True)
            ds=(p*(dp-delta)*(1.0/math.sqrt(HD))).astype(bf16)
            a1=dot(ds,km); a2=dot_tn(ds,qm); a3=dot_tn(pb,dom)
            dq=a1 if dq is None else dq+a1
            dk=a2 if dk is None else dk+a2
            dv=a3 if dv is None else dv+a3
        dqkv_s[:,pr]=dq.astype(bf16); dqkv_s[:,kr]=dk.astype(bf16); dqkv_s[:,vr]=dv.astype(bf16)
        vg_ref[16:24,pr]+=col8(dq); vg_ref[24:32,pr]+=col8(dv)
    dqkv=dqkv_s[...]
    gq_ref[...]+=dot(aT,dqkv)
    da=dot_nt(dqkv,w_ref[...])
    e1=da*g_ref[...]
    ig=dh_ref[0]+r1*(e1-jnp.mean(e1,axis=-1,keepdims=True)-n1*jnp.mean(e1*n1,axis=-1,keepdims=True))
    ig_ref[0]=ig[:T].astype(bf16)
    vg_ref[0:8]+=col8(da*n1); vg_ref[8:16]+=col8(da)


def dot3(a, b):
    ah = a.astype(bf16); al = (a - ah.astype(f32)).astype(bf16)
    bh = b.astype(bf16); bl = (b - bh.astype(f32)).astype(bf16)
    return dot(ah, bh) + (dot(ah, bl) + dot(al, bh))


def kNS(f_ref, m_ref, o_ref, q_s):
    m = m_ref[...]
    a = dot_nt(m, m)
    ri = lax.broadcasted_iota(jnp.int32, (D, D), 0)
    ci = lax.broadcasted_iota(jnp.int32, (D, D), 1)
    diag = ri == ci
    ssq = jnp.sum(jnp.where(diag, a, 0.0))
    s = 1.0 / (jnp.sqrt(jnp.full((1, 1), ssq, f32)) + ORTHO_EPSILON)
    a = a * (s * s)
    eye = jnp.where(diag, 1.0, 0.0).astype(f32)
    q = None
    for k in range(NS_ITERS):
        p = COEFF_FIRST * eye + COEFF_SECOND * a + COEFF_THIRD * dot3(a, a)
        q = p if q is None else dot3(p, q)
        if k < NS_ITERS - 1:
            a = dot3(dot3(p, a), p)
    q_s[...] = q * s
    rows = o_ref.shape[0]
    qr = q_s[pl.ds(pl.multiple_of(f_ref[0] * rows, rows), rows), :]
    qh = qr.astype(bf16)
    ql = (qr - qh.astype(f32)).astype(bf16)
    o_ref[...] = dot(qh, m) + dot(ql, m)


VL = 60 * 1024 * 1024
S = jax.ShapeDtypeStruct


def orth_rows(f_idx, m, parts):
    n = m.shape[1]
    rows = D // parts
    return pl.pallas_call(
        kNS, out_shape=S((rows, n), f32),
        grid_spec=pltpu.PrefetchScalarGridSpec(
            num_scalar_prefetch=1, grid=(1,),
            in_specs=[pl.BlockSpec((D, n), lambda i, f: (0, 0))],
            out_specs=pl.BlockSpec((rows, n), lambda i, f: (0, 0)),
            scratch_shapes=[pltpu.VMEM((D, D), f32)]),
        compiler_params=pltpu.CompilerParams(vmem_limit_bytes=VL),
        cost_estimate=pl.CostEstimate(flops=30 * 2 * D * D * D, bytes_accessed=4 * D * n, transcendentals=0),
        name="orth")(f_idx, m)


def whole(shape):
    return pl.BlockSpec(shape, lambda i, n: (0,) * len(shape))


def img(rows, cols):
    return pl.BlockSpec((1, rows, cols), lambda i, n: (jnp.minimum(i, n[0] - 1), 0, 0))


def slot(rows, cols):
    def at(i, n):
        j = jnp.minimum(i, n[0] - 1)
        return (jnp.where(j < n[1], j, n[2] + j - n[1]), 0, 0)

    return pl.BlockSpec((1, rows, cols), at)


def call(k, n, ins, in_specs, outs, out_specs, scratch, name, flops):
    return pl.pallas_call(
        k, out_shape=outs,
        grid_spec=pltpu.PrefetchScalarGridSpec(
            num_scalar_prefetch=1, grid=(ins[0].shape[0],), in_specs=in_specs, out_specs=out_specs,
            scratch_shapes=list(scratch)),
        compiler_params=pltpu.CompilerParams(dimension_semantics=("arbitrary",), vmem_limit_bytes=VL),
        cost_estimate=pl.CostEstimate(flops=flops, bytes_accessed=20_000_000, transcendentals=0),
        name=name)(n, *ins)


def run_A(n, x, wqkv, g1, b1, qb):
    N = x.shape[0]
    return call(kA, n, (x, wqkv, g1, b1, qb),
                [slot(T, D), whole((D, 3 * D)), whole((1, D)), whole((1, D)), whole((1, 3 * D))],
                (S((N, TP, 3 * D), bf16), S((N, TP, D), bf16), S((N, TP, 128), f32)),
                [img(TP, 3 * D), img(TP, D), img(TP, 128)], (), "attn_fwd", 10_000_000_000)


def run_B(n, x, o, cot, wp, w1, w2, vec, bu):
    N = x.shape[0]
    return call(kB, n, (x, o, cot, wp, w1, w2, vec, bu),
                [slot(T, D), img(TP, D), slot(T, D), whole((D, D)), whole((D, F)), whole((F, D)),
                 whole((4, D)), whole((1, F))],
                (S((N, T, D), bf16), S((N, TP, D), f32), S((N, TP, D), bf16), S((D, D), f32),
                 S((D, F), f32), S((D, F), f32), S((32, D), f32), S((8, F), f32)),
                [slot(T, D), img(TP, D), img(TP, D), whole((D, D)), whole((D, F)), whole((D, F)),
                 whole((32, D)), whole((8, F))], (), "mlp", 25_000_000_000)


def run_C(n, x, qkv, lse, do, dh, wqkv, g1, b1):
    N = x.shape[0]
    return call(kC, n, (x, qkv, lse, do, dh, wqkv, g1, b1),
                [slot(T, D), img(TP, 3 * D), img(TP, 128), img(TP, D), img(TP, D),
                 whole((D, 3 * D)), whole((1, D)), whole((1, D))],
                (S((N, T, D), bf16), S((D, 3 * D), f32), S((32, D), f32)),
                [slot(T, D), whole((D, 3 * D)), whole((32, D))],
                (pltpu.VMEM((TP, 3 * D), bf16),), "attn_bwd", 20_000_000_000)


def xor_perm(size, k):
    return [(i, i ^ k) for i in range(size)]


def swap(v, axis, k):
    return lax.ppermute(v, axis, xor_perm(lax.axis_size(axis), k))


def bits_of(axis):
    idx = lax.axis_index(axis)
    return [(idx >> b) & 1 for b in range(lax.axis_size(axis).bit_length() - 1)]


def gather_rows(v, axis):
    size = lax.axis_size(axis)
    cur = v[None]
    for b in reversed(range(size.bit_length() - 1)):
        bit = (lax.axis_index(axis) >> b) & 1
        got = swap(cur, axis, 1 << b)
        first = jnp.where(bit == 0, cur, got)
        second = jnp.where(bit == 0, got, cur)
        cur = jnp.stack([first, second], axis=1).reshape((-1,) + v.shape)
    return cur.reshape((-1,) + v.shape[1:])


def scatter_sum(v, axis):
    size = lax.axis_size(axis)
    cur = v
    nb = size.bit_length() - 1
    cur = v.reshape((2,) * nb + (v.shape[0] // size,) + v.shape[1:])
    for b in range(nb):
        bit = (lax.axis_index(axis) >> b) & 1
        ax = nb - 1 - b
        lo = lax.index_in_dim(cur, 0, ax, keepdims=False)
        hi = lax.index_in_dim(cur, 1, ax, keepdims=False)
        got = swap(jnp.where(bit == 0, hi, lo).astype(bf16), axis, 1 << b)
        cur = jnp.where(bit == 0, lo, hi) + got.astype(f32)
    return cur


def all_sum(v, axis):
    size = lax.axis_size(axis)
    nb = size.bit_length() - 1
    cur = v
    for b in range(nb):
        bit = (lax.axis_index(axis) >> b) & 1
        half = cur.shape[0] // 2
        lo, hi = cur[:half], cur[half:]
        got = swap(jnp.where(bit == 0, hi, lo).astype(bf16), axis, 1 << b)
        cur = jnp.where(bit == 0, lo, hi) + got.astype(f32)
    cur = cur.astype(bf16)
    for b in reversed(range(nb)):
        bit = (lax.axis_index(axis) >> b) & 1
        got = swap(cur, axis, 1 << b)
        cur = jnp.concatenate([jnp.where(bit == 0, cur, got), jnp.where(bit == 0, got, cur)], axis=0)
    return cur


def split_hi_lo(v):
    hi = v.astype(bf16)
    return hi, (v - hi.astype(f32)).astype(bf16)


def adam_update(parameter, gradient, first_state, second_state):
    next_first = ADAM_FIRST * first_state + (1.0 - ADAM_FIRST) * gradient
    next_second = ADAM_SECOND * second_state + (1.0 - ADAM_SECOND) * gradient * gradient
    first_hat = next_first / (1.0 - ADAM_FIRST**ADAM_STEP)
    second_hat = next_second / (1.0 - ADAM_SECOND**ADAM_STEP)
    updated = parameter - ADAM_RATE * (
        first_hat / (jnp.sqrt(second_hat) + ADAM_EPSILON) + ADAM_DECAY * parameter
    )
    return (updated, next_first, next_second)


def muon_factor(row_total, column_total):
    return math.sqrt(max(1.0, row_total / column_total))


def body(images, cotangent, counts, w_qkv, w_proj, w_fc1, w_fc2, gains, biases,
         mom_qkv, mom_proj, mom_fc1, mom_fc2, gains_first, gains_second, biases_first, biases_second):
    slots = images.shape[0]
    half = slots // 2
    own = w_qkv.shape[0]
    parts = lax.axis_size("fsdp")
    devices = lax.axis_size("rep") * parts
    f_idx = lax.axis_index("fsdp").reshape(1).astype(jnp.int32)
    count = counts[0]
    other = swap(counts, "fsdp", 1)[0]
    n_own = (count + 1) // 2
    n_other = other // 2
    nlist = jnp.stack([n_own + n_other, n_own, jnp.int32(half)]).astype(jnp.int32)

    def pool(v):
        v = v.reshape((half, 2) + v.shape[1:])
        return jnp.concatenate([v[:, 0], swap(v[:, 1], "fsdp", 1)], axis=0)

    live = (jnp.arange(slots, dtype=jnp.int32) < count)[:, None, None]

    def unpool(v):
        back = swap(v[half:], "fsdp", 1)
        full = jnp.stack([v[:half], back], axis=1).reshape(v.shape)
        return jnp.where(live, full, jnp.zeros_like(full))

    vecs = jnp.concatenate([gains, biases], axis=0).astype(bf16).T
    nvec = vecs.shape[1]
    first = jnp.concatenate([w_qkv.astype(bf16), jnp.pad(vecs, ((0, 0), (0, 128 - nvec)))], axis=1)
    first = gather_rows(first, "fsdp")
    xw = pool(images)
    wqkv = first[:, : 3 * D]
    vecs = first[:, 3 * D : 3 * D + nvec].astype(f32).T
    gv, bv = vecs[:2], vecs[2:]
    rest = jnp.concatenate([w_proj.astype(bf16), w_fc1.astype(bf16), w_fc2.astype(bf16).T], axis=1)
    rest = gather_rows(rest, "fsdp")
    wp, w1, w2 = rest[:, :D], rest[:, D : D + F], rest[:, D + F :].T
    cw = pool(cotangent)

    qb = jnp.concatenate([bv[1], jnp.zeros_like(bv[1]), bv[2]])[None]
    qkv, o, lse = run_A(nlist, xw, wqkv, gv[0:1], bv[0:1], qb)
    vec = jnp.stack([bv[3], gv[1], bv[4], bv[5]])
    out, dh, do, gp, g1, g2t, vgB, gbu = run_B(nlist, xw, o, cw, wp, w1, w2, vec, bv[6:].reshape(1, F))
    block_out = unpool(out)
    mid = all_sum(scatter_sum(jnp.concatenate([gp, g1, g2t], axis=1), "fsdp"), "rep")
    ig, gq, vgC = run_C(nlist, xw, qkv, lse, do, dh, wqkv, gv[0:1], bv[0:1])
    sB = vgB.reshape(4, 8, D).sum(1)
    sC = vgC.reshape(4, 8, D).sum(1)
    vg = jnp.concatenate([jnp.stack([sC[0], sB[0], sC[1], sC[2], sC[3], sB[1], sB[2], sB[3]]),
                          gbu.sum(0).reshape(F // D, D)]).T
    lastg = scatter_sum(jnp.concatenate([gq, jnp.pad(vg, ((0, 0), (0, 128 - nvec)))], axis=1), "fsdp")
    last = all_sum(lastg, "rep").astype(f32) * (1.0 / devices)
    input_grad = unpool(ig)
    mid = mid.astype(f32) * (1.0 / devices)
    grad_proj, grad_fc1, grad_fc2t = mid[:, :D], mid[:, D : D + F], mid[:, D + F :]
    grad_qkv = last[:, : 3 * D]
    gvec = last[:, 3 * D : 3 * D + nvec].T
    grad_gains, grad_biases = gvec[:2], gvec[2:]
    next_qkv = MUON_MOMENTUM * mom_qkv + grad_qkv
    next_proj = MUON_MOMENTUM * mom_proj + grad_proj
    next_fc1 = MUON_MOMENTUM * mom_fc1 + grad_fc1
    next_fc2t = MUON_MOMENTUM * mom_fc2.T + grad_fc2t
    m_mid = gather_rows(jnp.concatenate([next_proj, next_fc1, next_fc2t], axis=1).astype(bf16), "fsdp")
    m_qkv = gather_rows(next_qkv.astype(bf16), "fsdp")
    orth_proj = orth_rows(f_idx, m_mid[:, :D], parts)
    orth_fc1 = orth_rows(f_idx, m_mid[:, D : D + F], parts)
    orth_fc2t = orth_rows(f_idx, m_mid[:, D + F :], parts)
    orth_qkv = orth_rows(f_idx, m_qkv, parts)
    new_qkv = w_qkv - MUON_RATE * muon_factor(D, 3 * D) * orth_qkv
    new_proj = w_proj - MUON_RATE * muon_factor(D, D) * orth_proj
    new_fc1 = w_fc1 - MUON_RATE * muon_factor(D, F) * orth_fc1
    new_fc2 = w_fc2 - MUON_RATE * muon_factor(F, D) * orth_fc2t.T
    new_gains, next_gains_first, next_gains_second = adam_update(gains, grad_gains, gains_first, gains_second)
    new_biases, next_biases_first, next_biases_second = adam_update(biases, grad_biases, biases_first, biases_second)
    return (block_out, input_grad, grad_qkv, grad_proj, grad_fc1, grad_fc2t.T, grad_gains, grad_biases,
            new_qkv, new_proj, new_fc1, new_fc2, new_gains, new_biases,
            next_qkv, next_proj, next_fc1, next_fc2t.T,
            next_gains_first, next_gains_second, next_biases_first, next_biases_second)


def solution(mesh):
    in_specs = (
        P(("rep", "fsdp"), None, None),
        P(("rep", "fsdp"), None, None),
        P(("rep", "fsdp")),
        P("fsdp", None),
        P("fsdp", None),
        P("fsdp", None),
        P(None, "fsdp"),
        P(None, "fsdp"),
        P(None, "fsdp"),
        P("fsdp", None),
        P("fsdp", None),
        P("fsdp", None),
        P(None, "fsdp"),
        P(None, "fsdp"),
        P(None, "fsdp"),
        P(None, "fsdp"),
        P(None, "fsdp"),
    )
    out_specs = (
        P(("rep", "fsdp"), None, None),
        P(("rep", "fsdp"), None, None),
        P("fsdp", None),
        P("fsdp", None),
        P("fsdp", None),
        P(None, "fsdp"),
        P(None, "fsdp"),
        P(None, "fsdp"),
        P("fsdp", None),
        P("fsdp", None),
        P("fsdp", None),
        P(None, "fsdp"),
        P(None, "fsdp"),
        P(None, "fsdp"),
        P("fsdp", None),
        P("fsdp", None),
        P("fsdp", None),
        P(None, "fsdp"),
        P(None, "fsdp"),
        P(None, "fsdp"),
        P(None, "fsdp"),
        P(None, "fsdp"),
    )
    return jax.shard_map(body, mesh=mesh, in_specs=in_specs, out_specs=out_specs, check_vma=False)
```

```python
import math

import jax
import jax.numpy as jnp
from jax import lax
from jax.experimental import pallas as pl
from jax.experimental.pallas import tpu as pltpu
from jax.sharding import PartitionSpec as P


NS_ITERS = 5
ADAM_STEP = 3
ORTHO_EPSILON = 1e-07
COEFF_FIRST = 3.4445
COEFF_SECOND = -4.775
COEFF_THIRD = 2.0315
MUON_RATE = 0.3
MUON_MOMENTUM = 0.95
ADAM_RATE = 0.2
ADAM_FIRST = 0.9
ADAM_SECOND = 0.95
ADAM_EPSILON = 1e-08
ADAM_DECAY = 0.25

D = 384
H = 6
HD = 64
F = 1536
T = 197
TP = 208
TC = T // 16 * 16
EPS = 1e-6
NV = 12
Q_COLS = 3 * D + 128
R_COLS = D + 2 * F
F2 = F // 2
M_HALF = 256 + F
Q_HALF = Q_COLS // 2
f32 = jnp.float32
bf16 = jnp.bfloat16
SCALE = 1.0 / math.sqrt(HD)
SCALE_LOG2E = SCALE * math.log2(math.e)
VMEM_LIMIT = 60 * 1024 * 1024
S = jax.ShapeDtypeStruct
ANY = pl.BlockSpec(memory_space=pl.ANY)


def dot(a, b):
    return jnp.dot(a, b, preferred_element_type=f32)


def dot_nt(a, b):
    return lax.dot_general(a, b, (((1,), (1,)), ((), ())), preferred_element_type=f32)


def dot_tn(a, b):
    return lax.dot_general(a, b, (((0,), (0,)), ((), ())), preferred_element_type=f32)


def norm(x):
    xc = x - jnp.mean(x, axis=-1, keepdims=True)
    r = lax.rsqrt(jnp.mean(xc * xc, axis=-1, keepdims=True) + EPS)
    return xc * r, r


def norm_back(e, n, r):
    return r * (e - jnp.mean(e, axis=-1, keepdims=True) - n * jnp.mean(e * n, axis=-1, keepdims=True))


def col8(v):
    return jnp.sum(v.reshape(v.shape[0] // 8, 8, v.shape[1]), axis=0)


def total(v):
    return jnp.sum(v, axis=0, keepdims=True)


PHI_T = 0.28
PHI_C = (0.11652077999788102, 0.06749674653879187, 0.2689101818992952,
         -0.2369935012534717, 0.38987403003604115, -0.10580824648054844)
HALF_LOG2E = -0.5 * math.log2(math.e)
DENSITY = 1.0 / math.sqrt(2.0 * math.pi)


def gelu_parts(z):
    t = 1.0 / (1.0 + PHI_T * jnp.abs(z))
    bell = jnp.exp2((z * z) * HALF_LOG2E)
    poly = PHI_C[5] * t + PHI_C[4]
    for k in (3, 2, 1, 0):
        poly = poly * t + PHI_C[k]
    tail = (poly * t) * bell
    cdf = jnp.where(z < 0.0, tail, 1.0 - tail)
    return z * cdf, cdf + (z * DENSITY) * bell


def slot_of(n_ref):
    i = pl.program_id(0)
    return jnp.where(i < n_ref[1], 2 * i, 2 * (i - n_ref[1]) + 1)


def fill_pool(own_ref, got_ref, pool):
    rows = own_ref.shape[0]
    odd = lax.broadcasted_iota(jnp.int32, (rows, 128), 0) & 1
    for j in range(D // 128):
        cols = slice(128 * j, 128 * j + 128)
        pool[j, :rows] = jnp.where(odd == 0, own_ref[:, cols].astype(f32), got_ref[:, cols].astype(f32))
        pool[j, rows:] = jnp.zeros((pool.shape[1] - rows, 128), f32)


def load_image(n_ref, pool):
    rows = pl.ds(slot_of(n_ref), TP, stride=pool.shape[1] // TP)
    return jnp.concatenate([pool[j, rows, :] for j in range(D // 128)], axis=1)


def store_image(n_ref, pool, value):
    rows = pl.ds(slot_of(n_ref), TP, stride=pool.shape[1] // TP)
    for j in range(D // 128):
        pool[j, rows, :] = value[:, 128 * j : 128 * j + 128]


def empty_pool(pool, out_ref):
    for j in range(D // 128):
        out_ref[:, 128 * j : 128 * j + 128] = pool[j, : out_ref.shape[0]].astype(bf16)


def fetch(n_ref, pieces, buf, sems):
    rows = pieces[0].shape[0]
    copies = []
    for k, piece in enumerate(pieces):
        at = pl.multiple_of((n_ref[2] ^ k) * rows, 32)
        copies.append(pltpu.make_async_copy(piece, buf.at[pl.ds(at, rows)], sems.at[k]))
    for c in copies:
        c.start()
    for c in copies:
        c.wait()


def flush(n_ref, acc, send_ref, keep_ref):
    pairs, rows = keep_ref.shape[0], keep_ref.shape[1]
    me = n_ref[2] & 1
    for y in range(pairs):
        mine = pl.multiple_of((2 * y + me) * rows, 32)
        theirs = pl.multiple_of((2 * y + 1 - me) * rows, 32)
        keep_ref[y] = acc[pl.ds(mine, rows), :]
        send_ref[y] = acc[pl.ds(theirs, rows), :].astype(bf16)


def live_step(n_ref, step):
    pl.when(pl.program_id(0) < n_ref[0])(step)


def attn_fwd_kernel(parts, n_ref, xo_ref, xg_ref, *rest):
    pieces = rest[:parts]
    x_ref, qkv_ref, o_ref, lse_ref, vec_ref, w, pool, sems = rest[parts:]

    @pl.when(pl.program_id(0) == 0)
    def _():
        fetch(n_ref, pieces, w, sems)
        vec_ref[...] = w[:, 3 * D :].astype(f32).T[:16]
        fill_pool(xo_ref, xg_ref, pool)

    def step():
        x = load_image(n_ref, pool)
        x_ref[0] = x.astype(bf16)
        n1, _ = norm(x)
        a = (n1 * vec_ref[0:1] + vec_ref[2:3]).astype(bf16)
        qb = jnp.concatenate([vec_ref[3:4], jnp.zeros((1, D), f32), vec_ref[4:5]], axis=1)
        qkv = (dot(a, w[:, : 3 * D]) + qb).astype(bf16)
        real = lax.broadcasted_iota(jnp.int32, (TP - TC, 3 * D), 0) < T - TC
        qkv_ref[0, :TC] = qkv[:TC]
        qkv_ref[0, TC:] = jnp.where(real, qkv[TC:], jnp.zeros_like(qkv[TC:]))
        lane = lax.broadcasted_iota(jnp.int32, (TP, 128), 1)
        low = lane < HD
        key = lax.broadcasted_iota(jnp.int32, (TP, TP), 1) < T
        lse = jnp.zeros((TP, 128), f32)
        for pair in range(H // 2):
            at = pair * 128
            q, k, v = (qkv_ref[0, :, off + at : off + at + 128] for off in (0, D, 2 * D))
            zero = jnp.zeros_like(q)
            o = None
            for side in range(2):
                sel = low if side == 0 else jnp.logical_not(low)
                s = jnp.where(key, dot_nt(jnp.where(sel, q, zero), k) * SCALE_LOG2E, -1e30)
                l2 = jnp.log2(jnp.sum(jnp.exp2(s), axis=-1, keepdims=True))
                p = jnp.exp2(s - l2).astype(bf16)
                part = dot(p, jnp.where(sel, v, zero))
                o = part if o is None else o + part
                lse = jnp.where(lane == pair * 2 + side, l2, lse)
            o_ref[0, :, at : at + 128] = o.astype(bf16)
        lse_ref[0] = lse

    live_step(n_ref, step)


FC = 256


def mlp_kernel(parts, n_ref, x_ref, co_ref, cg_ref, o_ref, vec_ref, *rest):
    pieces = rest[:parts]
    out_ref, dh_ref, do_ref, send_ref, keep_ref, vb_ref, w, acc, vg, gbu, cpool, opool, bu_s, c_s, dy_s, ct_s, dyt_s, zb, db, ub, eb, out_s, dc_s, sems = rest[parts:]

    @pl.when(pl.program_id(0) == 0)
    def _():
        fetch(n_ref, pieces, w, sems)
        acc[...] = jnp.zeros_like(acc)
        vg[...] = jnp.zeros_like(vg)
        gbu[...] = jnp.zeros_like(gbu)
        fill_pool(co_ref, cg_ref, cpool)
        bu_s[...] = jnp.concatenate([vec_ref[8 + j : 9 + j] for j in range(F // D)], axis=1)

    def step():
        g2, b2, bo, bd = vec_ref[1:2], vec_ref[6:7], vec_ref[5:6], vec_ref[7:8]
        x = x_ref[0].astype(f32)
        o = o_ref[0]
        h = x + dot(o, w[:, :D]) + bo
        n2, r2 = norm(h)
        c = (n2 * g2 + b2).astype(bf16)
        dyf = load_image(n_ref, cpool)
        dy = dyf.astype(bf16)
        steps = F // FC
        c_s[...] = c
        dy_s[...] = dy
        ct_s[...] = c.T
        dyt_s[...] = dy.T

        def cols(base, j):
            return slice(base + j * FC, base + j * FC + FC)

        def produce(j, slot):
            zb[slot] = dot(c_s[...], w[:, cols(D, j)])
            db[slot] = dot(dy_s[...], w[:, cols(D + F, j)])

        def middle(j, slot):
            u, slope = gelu_parts(zb[slot] + bu_s[:, cols(0, j)])
            dz = db[slot] * slope
            gbu[:, cols(0, j)] += col8(dz)
            ub[slot] = u.astype(bf16)
            eb[slot] = dz.astype(bf16)

        def consume(j, slot, first=False):
            u, dzb = ub[slot], eb[slot]
            o1, d1 = dot_nt(u, w[:, cols(D + F, j)]), dot_nt(dzb, w[:, cols(D, j)])
            out_s[...] = o1 if first else out_s[...] + o1
            dc_s[...] = d1 if first else dc_s[...] + d1
            base = M_HALF * (j // (steps // 2)) + 256
            acc[:, cols(base, j % (steps // 2))] += dot(ct_s[...], dzb)
            acc[:, cols(base + F2, j % (steps // 2))] += dot(dyt_s[...], u)

        produce(0, 0)
        produce(1, 1)
        middle(0, 0)
        for j in range(1, steps):
            if j + 1 < steps:
                produce(j + 1, (j + 1) % 3)
            consume(j - 1, (j - 1) % 3, j == 1)
            middle(j, j % 3)
        consume(steps - 1, (steps - 1) % 3)
        out, dc = out_s[...], dc_s[...]
        store_image(n_ref, opool, h + out + bd)
        dh = dyf + norm_back(dc * g2, n2, r2)
        dh_ref[0] = dh
        dhb = dh.astype(bf16)
        ot = o.T
        acc[:, :256] += dot(ot, dhb[:, :256])
        acc[:, M_HALF : M_HALF + 128] += dot(ot, dhb[:, 256:])
        do_ref[0] = dot_nt(dhb, w[:, :D]).astype(bf16)
        vg[0:8] += col8(dc * n2)
        vg[8:16] += col8(dh)
        vg[16:24] += col8(dc)
        vg[24:32] += col8(dyf)

    live_step(n_ref, step)

    @pl.when(pl.program_id(0) == n_ref[0] - 1)
    def _():
        empty_pool(opool, out_ref)
        flush(n_ref, acc, send_ref, keep_ref)
        rows = [total(vg[8 * k : 8 * k + 8]) for k in range(4)]
        rows += [total(gbu[:, k * D : (k + 1) * D]) for k in range(F // D)]
        vb_ref[...] = jnp.concatenate(rows, axis=0)


def attn_bwd_kernel(parts, n_ref, x_ref, qkv_ref, lse_ref, do_ref, dh_ref, vec_ref, vb_ref, *rest):
    pieces = rest[:parts]
    out_ref, send_ref, keep_ref, w, acc, vg, dqkv, opool, sb, db, pb, gb, tb, sems = rest[parts:]

    @pl.when(pl.program_id(0) == 0)
    def _():
        fetch(n_ref, pieces, w, sems)
        acc[...] = jnp.zeros_like(acc)
        vg[...] = jnp.zeros_like(vg)

    def step():
        g1, b1 = vec_ref[0:1], vec_ref[2:3]
        x = x_ref[0].astype(f32)
        n1, r1 = norm(x)
        at_ = (n1 * g1 + b1).astype(bf16).T
        low = lax.broadcasted_iota(jnp.int32, (TP, 128), 1) < HD
        real = lax.broadcasted_iota(jnp.int32, (TP - TC, 128), 0) < T - TC

        def mask(h, v):
            return jnp.where(low if h % 2 == 0 else jnp.logical_not(low), v, jnp.zeros_like(v))

        def lanes(h, off=0):
            return slice(off + (h // 2) * 128, off + (h // 2) * 128 + 128)

        def produce(h):
            sb[h % 3] = dot_nt(mask(h, qkv_ref[0, :, lanes(h)]), qkv_ref[0, :, lanes(h, D)])
            db[h % 3] = dot_nt(mask(h, do_ref[0, :, lanes(h)]), qkv_ref[0, :, lanes(h, 2 * D)])

        def middle(h):
            p = jnp.exp2(sb[h % 3] * SCALE_LOG2E - lse_ref[0, :, h : h + 1])
            dp = db[h % 3]
            pb[h % 2] = p.astype(bf16)
            delta = jnp.sum(p * dp, axis=-1, keepdims=True)
            gb[h % 2] = (p * (dp - delta) * SCALE).astype(bf16)

        def consume(h):
            ds = gb[h % 2]
            part = (dot(ds, mask(h, qkv_ref[0, :, lanes(h, D)])),
                    dot_tn(ds, mask(h, qkv_ref[0, :, lanes(h)])),
                    dot_tn(pb[h % 2], mask(h, do_ref[0, :, lanes(h)])))
            if h % 2 == 0:
                for k in range(3):
                    tb[k] = part[k]
                return
            dq, dk, dv = (tb[k] + part[k] for k in range(3))
            dqkv[:, lanes(h)] = dq.astype(bf16)
            for v, off in ((dk, D), (dv, 2 * D)):
                v_b = v.astype(bf16)
                dqkv[:TC, lanes(h, off)] = v_b[:TC]
                dqkv[TC:, lanes(h, off)] = jnp.where(real, v_b[TC:], jnp.zeros_like(v_b[TC:]))
            vg[16:24, lanes(h)] += col8(dq)
            vg[24:32, lanes(h)] += col8(dv[:TC]) + col8(jnp.where(real, dv[TC:], 0.0))

        produce(0)
        produce(1)
        middle(0)
        for h in range(1, H):
            if h + 1 < H:
                produce(h + 1)
            consume(h - 1)
            middle(h)
        consume(H - 1)
        dqkv_b = dqkv[...]
        acc[:, : 3 * D] += dot(at_, dqkv_b)
        da = dot_nt(dqkv_b, w[:, : 3 * D])
        store_image(n_ref, opool, dh_ref[0] + norm_back(da * g1, n1, r1))
        vg[0:8] += col8(da * n1)
        vg[8:16] += col8(da)

    live_step(n_ref, step)

    @pl.when(pl.program_id(0) == n_ref[0] - 1)
    def _():
        empty_pool(opool, out_ref)
        mine = [total(vg[8 * k : 8 * k + 8]) for k in range(4)]
        vb = vb_ref[...]
        rows = jnp.concatenate([mine[0], vb[0:1], mine[1], mine[2], mine[3], vb[1:8], jnp.zeros((116, D), f32)], axis=0)
        acc[:, 3 * D :] = rows.T
        flush(n_ref, acc, send_ref, keep_ref)


def whole(shape):
    return pl.BlockSpec(shape, lambda i, n: (0,) * len(shape))


def item(rows, cols):
    return pl.BlockSpec((1, rows, cols), lambda i, n: (jnp.minimum(i, n[0] - 1), 0, 0))


def layer_call(kernel, n, slots, ins, in_specs, pieces, outs, out_specs, scratch, flops):
    parts = len(pieces)
    return pl.pallas_call(
        lambda *refs: kernel(parts, *refs),
        out_shape=outs,
        grid_spec=pltpu.PrefetchScalarGridSpec(
            num_scalar_prefetch=1, grid=(slots,), in_specs=list(in_specs) + [ANY] * parts,
            out_specs=out_specs, scratch_shapes=list(scratch) + [pltpu.SemaphoreType.DMA((parts,))]),
        compiler_params=pltpu.CompilerParams(
            dimension_semantics=("arbitrary",), vmem_limit_bytes=VMEM_LIMIT),
        cost_estimate=pl.CostEstimate(flops=flops, bytes_accessed=20_000_000, transcendentals=0))(n, *ins, *pieces)


def once(shape):
    return pl.BlockSpec(shape, lambda i, n: (0,) * len(shape), pipeline_mode=pl.Buffered(1))


def attn_fwd(n, slots, x_own, x_got, pieces):
    rows = x_own.shape[0]
    return layer_call(
        attn_fwd_kernel, n, slots, (x_own, x_got), (once((rows, D)), once((rows, D))), pieces,
        (S((slots, TP, D), bf16), S((slots, TP, 3 * D), bf16), S((slots, TP, D), bf16), S((slots, TP, 128), f32),
         S((16, D), f32)),
        (item(TP, D), item(TP, 3 * D), item(TP, D), item(TP, 128), whole((16, D))),
        (pltpu.VMEM((D, Q_COLS), bf16), pltpu.VMEM((D // 128, TP * slots, 128), f32)), 10_000_000_000)


def reduced(parts, cols):
    shape = (parts // 2, D // parts, cols)
    return (S(shape, bf16), S(shape, f32)), (once(shape), once(shape))


def mlp(n, slots, x, c_own, c_got, o, vec, pieces):
    rows = c_own.shape[0]
    r_shape, r_spec = reduced(len(pieces), 2 * M_HALF)
    return layer_call(
        mlp_kernel, n, slots, (x, c_own, c_got, o, vec),
        (item(TP, D), once((rows, D)), once((rows, D)), item(TP, D), whole((16, D))), pieces,
        (S((rows, D), bf16), S((slots, TP, D), f32), S((slots, TP, D), bf16)) + r_shape + (S((8, D), f32),),
        (once((rows, D)), item(TP, D), item(TP, D)) + r_spec + (whole((8, D)),),
        (pltpu.VMEM((D, R_COLS), bf16), pltpu.VMEM((D, 2 * M_HALF), f32), pltpu.VMEM((32, D), f32),
         pltpu.VMEM((8, F), f32), pltpu.VMEM((D // 128, TP * slots, 128), f32), pltpu.VMEM((D // 128, TP * slots, 128), f32),
         pltpu.VMEM((1, F), f32), pltpu.VMEM((TP, D), bf16), pltpu.VMEM((TP, D), bf16), pltpu.VMEM((D, TP), bf16),
         pltpu.VMEM((D, TP), bf16), pltpu.VMEM((3, TP, FC), f32), pltpu.VMEM((3, TP, FC), f32),
         pltpu.VMEM((3, TP, FC), bf16), pltpu.VMEM((3, TP, FC), bf16), pltpu.VMEM((TP, D), f32),
         pltpu.VMEM((TP, D), f32)),
        25_000_000_000)


def attn_bwd(n, slots, x, qkv, lse, do, dh, vec, vb, pieces, rows):
    r_shape, r_spec = reduced(len(pieces), Q_COLS)
    return layer_call(
        attn_bwd_kernel, n, slots, (x, qkv, lse, do, dh, vec, vb),
        (item(TP, D), item(TP, 3 * D), item(TP, 128), item(TP, D), item(TP, D),
         whole((16, D)), whole((8, D))), pieces,
        (S((rows, D), bf16),) + r_shape, (once((rows, D)),) + r_spec,
        (pltpu.VMEM((D, Q_COLS), bf16), pltpu.VMEM((D, Q_COLS), f32), pltpu.VMEM((32, D), f32),
         pltpu.VMEM((TP, 3 * D), bf16), pltpu.VMEM((D // 128, TP * slots, 128), f32), pltpu.VMEM((3, TP, TP), f32),
         pltpu.VMEM((3, TP, TP), f32), pltpu.VMEM((2, TP, TP), bf16), pltpu.VMEM((2, TP, TP), bf16),
         pltpu.VMEM((3, TP, 128), f32)), 20_000_000_000)


def pack_first_kernel(w_ref, g_ref, b_ref, o_ref):
    rows = w_ref.shape[0]
    vec = jnp.concatenate([g_ref[...], b_ref[...], jnp.zeros((128 - NV, rows), f32)], axis=0)
    o_ref[:, : 3 * D] = w_ref[...].astype(bf16)
    o_ref[:, 3 * D :] = vec.T.astype(bf16)


def pack_rest_kernel(p_ref, a_ref, b_ref, o_ref):
    o_ref[:, :D] = p_ref[...].astype(bf16)
    o_ref[:, D : D + F] = a_ref[...].astype(bf16)
    o_ref[:, D + F : D + 2 * F] = b_ref[...].astype(bf16)


def split3(a):
    hi = a.astype(bf16)
    return hi, (a - hi.astype(f32)).astype(bf16)


def dot3(a, b):
    return dot(jnp.concatenate([a[0], a[1], a[0]], axis=1), jnp.concatenate([b[0], b[0], b[1]], axis=0))


def orth_rows(m, q_s, at, rows):
    a = dot_nt(m, m)
    diag = lax.broadcasted_iota(jnp.int32, (D, D), 0) == lax.broadcasted_iota(jnp.int32, (D, D), 1)
    ssq = jnp.sum(jnp.where(diag, a, 0.0), axis=(0, 1), keepdims=True)
    s = 1.0 / (jnp.sqrt(ssq) + ORTHO_EPSILON)
    a = a * (s * s)
    eye = jnp.where(diag, COEFF_FIRST, 0.0)
    q = None
    for k in range(NS_ITERS - 1):
        a_s = split3(a)
        p = eye + COEFF_SECOND * a + COEFF_THIRD * dot3(a_s, a_s)
        p_s = split3(p)
        if k == 0:
            q_s[...] = p
            q = q_s[pl.ds(at, rows), :]
        else:
            q = dot3(split3(q), p_s)
        if k < NS_ITERS - 2:
            a = dot3(split3(dot3(p_s, a_s)), p_s)

    def times_last(v):
        return dot3(split3(dot3(split3(dot3(split3(v), p_s)), a_s)), p_s)

    qa = times_last(q)
    q = COEFF_FIRST * q + COEFF_SECOND * qa + COEFF_THIRD * times_last(qa)
    hi, lo = split3(q * s)
    return dot(hi, m) + dot(lo, m)


def fetch_momenta(n_ref, pieces, buf, sems, plan):
    rows = pieces[0].shape[1]

    def start(x):
        copies = []
        for k in range(2):
            own, near, far = pieces[3 * k : 3 * k + 3]
            for off, src, h in ((0, own.at[0], 0), (0, own.at[1], 1), (2, near, x), (2, far, 1 - x)):
                col, width, to = plan(h)
                at = pl.multiple_of((n_ref[0] ^ (k + off)) * rows, 32)
                copies.append(pltpu.make_async_copy(
                    src.at[:, pl.ds(col, width)], buf.at[pl.ds(at, rows), pl.ds(to, width)], sems.at[len(copies)]))
        for c in copies:
            c.start()
        for c in copies:
            c.wait()

    for x in range(2):
        pl.when(n_ref[1] == x)(lambda x=x: start(x))


def orth_both(n_ref, mine_ref, theirs_ref, m, q_s, o_s):
    rows = mine_ref.shape[0]
    core = n_ref[0] & 1
    at = pl.multiple_of((n_ref[0] - core) * rows, 32)
    o_s[...] = orth_rows(m[...], q_s, at, 2 * rows)
    mine_ref[...] = o_s[pl.ds(pl.multiple_of(core * rows, 32), rows), :]
    theirs_ref[...] = o_s[pl.ds(pl.multiple_of((1 - core) * rows, 32), rows), :]


def orth_mlp_kernel(n_ref, *rest):
    pieces = rest[:6]
    mine_ref, theirs_ref, m, q_s, o_s, sems = rest[6:]
    at = pl.multiple_of(256 + (n_ref[0] & 1) * F2, 128)
    fetch_momenta(n_ref, pieces, m, sems, lambda h: (at, F2, h * F2))
    orth_both(n_ref, mine_ref, theirs_ref, m, q_s, o_s)


def orth_attn_kernel(n_ref, *rest):
    pieces, others = rest[:6], rest[6:12]
    mine_ref, theirs_ref, m, q_s, o_s, sems = rest[12:]

    @pl.when(n_ref[0] & 1 == 0)
    def _():
        fetch_momenta(n_ref, pieces, m, sems, lambda h: (0, 3 * D - Q_HALF if h else Q_HALF, h * Q_HALF))

    @pl.when(n_ref[0] & 1 == 1)
    def _():
        m[:, D:] = jnp.zeros((D, 2 * D), bf16)
        fetch_momenta(n_ref, others, m, sems, lambda h: (0, D - 256 if h else 256, h * 256))

    orth_both(n_ref, mine_ref, theirs_ref, m, q_s, o_s)


def orth_call(kernel, at, pieces, cols):
    rows = pieces[0].shape[1]
    spec = pl.BlockSpec((rows, cols), lambda i, n: (0, 0))
    return pl.pallas_call(
        kernel, out_shape=(S((rows, cols), f32),) * 2,
        grid_spec=pltpu.PrefetchScalarGridSpec(
            num_scalar_prefetch=1, grid=(1,), in_specs=[ANY] * len(pieces), out_specs=(spec,) * 2,
            scratch_shapes=[pltpu.VMEM((D, cols), bf16), pltpu.VMEM((D, D), f32), pltpu.VMEM((2 * rows, cols), f32),
                            pltpu.SemaphoreType.DMA((8,))]),
        compiler_params=pltpu.CompilerParams(vmem_limit_bytes=VMEM_LIMIT),
        cost_estimate=pl.CostEstimate(flops=8_000_000_000, bytes_accessed=4_000_000, transcendentals=0))(at, *pieces)


def step_call(kernel, at, ins, outs, scratch):
    full = [pl.BlockSpec(v.shape, lambda i, n, r=len(v.shape): (0,) * r) for v in ins]
    return pl.pallas_call(
        kernel, out_shape=outs,
        grid_spec=pltpu.PrefetchScalarGridSpec(
            num_scalar_prefetch=1, grid=(1,), in_specs=full,
            out_specs=tuple(pl.BlockSpec(v.shape, lambda i, n, r=len(v.shape): (0,) * r) for v in outs),
            scratch_shapes=scratch),
        compiler_params=pltpu.CompilerParams(vmem_limit_bytes=VMEM_LIMIT),
        cost_estimate=pl.CostEstimate(flops=1_000_000, bytes_accessed=1_000_000, transcendentals=0))(at, *ins)


def split_xy_kernel(n_ref, keep_ref, got_ref, own_ref, x_ref, y_ref, xy_ref):
    half = own_ref.shape[1]

    def term(dy, dx):
        y, at = n_ref[0] >> 1 ^ dy, pl.multiple_of((n_ref[1] ^ dx) * half, 128)
        return keep_ref[y, :, pl.ds(at, half)] + got_ref[y, :, pl.ds(at, half)].astype(f32)

    own_ref[...] = term(0, 0)
    x_ref[...] = term(0, 1).astype(bf16)
    y_ref[...] = term(1, 0).astype(bf16)
    xy_ref[...] = term(1, 1).astype(bf16)


def split_z_kernel(n_ref, own_ref, a_ref, b_ref, c_ref, keep_ref, *rest):
    sends, t = rest[:3], rest[3]
    t[...] = own_ref[...] + (a_ref[...].astype(f32) + b_ref[...].astype(f32) + c_ref[...].astype(f32))
    rows = keep_ref.shape[0]
    keep_ref[...] = t[pl.ds(pl.multiple_of(n_ref[2] * rows, 8), rows), :]
    for k, ref in enumerate(sends):
        ref[...] = t[pl.ds(pl.multiple_of((n_ref[2] ^ (k + 1)) * rows, 8), rows), :].astype(bf16)


def sum_z_kernel(n_ref, own_ref, a_ref, b_ref, c_ref, o_ref):
    t = own_ref[...] + (a_ref[...].astype(f32) + b_ref[...].astype(f32) + c_ref[...].astype(f32))
    o_ref[...] = t.astype(o_ref.dtype)


def momentum(g, mom, scale):
    return MUON_MOMENTUM * mom + g.astype(f32) * scale


def momenta_kernel(scale, plan, n_ref, own_ref, a_ref, b_ref, c_ref, *rest):
    moms, (g_ref, m_ref) = rest[:-2], rest[-2:]
    rows = own_ref.shape[0]
    for k, ref in enumerate((own_ref, a_ref, b_ref, c_ref)):
        g_ref[pl.ds(pl.multiple_of((n_ref[2] ^ k) * rows, 8), rows), :] = ref[...]
    m_ref[...] = jnp.zeros_like(m_ref)

    def fill(h):
        for which, col, width, at in plan(h):
            m_ref[:, at : at + width] = momentum(
                g_ref[:, at : at + width], moms[which][:, col : col + width], scale).astype(bf16)

    for h in range(2):
        pl.when(n_ref[1] == h)(lambda h=h: fill(h))


def results_kernel(scale, plan, count, n_ref, own_ref, got_ref, *rest):
    moms, grads, nexts, m_ref = rest[:count], rest[count : 2 * count], rest[2 * count : 3 * count], rest[3 * count]
    m_ref[...] = jnp.zeros_like(m_ref)

    def fill(x):
        for h in range(2):
            src = own_ref if h == x else got_ref
            for which, col, width, at in plan(h):
                g = src[:, at : at + width]
                m = momentum(g, moms[which][:, col : col + width], scale)
                grads[which][:, col : col + width] = g.astype(f32) * scale
                nexts[which][:, col : col + width] = m
                m_ref[h, :, at : at + width] = m.astype(bf16)

    for x in range(2):
        pl.when(n_ref[1] == x)(lambda x=x: fill(x))


def mlp_plan(h):
    return ((0, 256 * h, D - 256 if h else 256, 0), (1, F2 * h, F2, 256), (2, F2 * h, F2, 256 + F2))


def attn_plan(h):
    return ((0, Q_HALF * h, 3 * D - Q_HALF if h else Q_HALF, 0),)


def send(v, rep, fsdp):
    parts = lax.axis_size("fsdp")
    pairs = [(r * parts + f, (r ^ rep) * parts + (f ^ fsdp)) for r in range(lax.axis_size("rep")) for f in range(parts)]
    return lax.ppermute(v, ("rep", "fsdp"), pairs)


def spread_xy(at, sent, keep):
    got = send(sent, 0, 1)
    half = S((keep.shape[1], keep.shape[2] // 2), bf16)
    own, to_x, to_y, to_xy = step_call(
        split_xy_kernel, at, (keep, got), (S(half.shape, f32), half, half, half), [])
    return own, send(to_x, 1, 0), send(to_y, 0, 2), send(to_xy, 1, 2)


def sum_all(at, terms, moms, plan, scale):
    rows, half = terms[0].shape
    z = S((rows // 4, half), bf16)
    out = step_call(split_z_kernel, at, terms, (S(z.shape, f32), z, z, z), [pltpu.VMEM((rows, half), f32)])
    got = [send(v, 2 * (k + 1), 0) for k, v in enumerate(out[1:])]
    more = range(3, lax.axis_size("rep").bit_length() - 1)
    (g,) = step_call(sum_z_kernel, at, (out[0], *got), (S(z.shape, f32 if more else bf16),), [])
    for b in more:
        g = g.astype(bf16).astype(f32) + send(g.astype(bf16), 1 << b, 0).astype(f32)
    g = g.astype(bf16)
    got = [send(g, 2 * k, 0) for k in range(1, 4)]
    both = S((rows, half), bf16)
    g, m = step_call(lambda *refs: momenta_kernel(scale, plan, *refs), at, (g, *got, *moms), (both, both), [])
    near, far, g_x = send(m, 0, 2), send(m, 1, 2), send(g, 1, 0)
    count = len(moms)
    full = tuple(S(v.shape, f32) for v in moms)
    out = step_call(lambda *refs: results_kernel(scale, plan, count, *refs), at, (g, g_x, *moms),
                    full + full + (S((2, rows, half), bf16),), [])
    own = out[-1]
    pieces = [own, near, far] + [send(v, 0, 1) for v in (own, near, far)]
    return g, g_x, out[:count], out[count : 2 * count], pieces


def swap(v, axis, k):
    return lax.ppermute(v, axis, [(i, i ^ k) for i in range(lax.axis_size(axis))])


def bits(axis):
    return range(lax.axis_size(axis).bit_length() - 1)


def all_pieces(v, axis):
    pieces = {0: v}
    for b in reversed(bits(axis)):
        pieces.update({k ^ (1 << b): swap(p, axis, 1 << b) for k, p in list(pieces.items())})
    return [pieces[k] for k in range(lax.axis_size(axis))]


def unpool_kernel(slots, n_ref, own_ref, got_ref, o_ref):
    row = pl.program_id(0) * own_ref.shape[0] + lax.broadcasted_iota(jnp.int32, own_ref.shape, 0)
    slot = row & (slots - 1)
    v = jnp.where(slot & 1 == 0, own_ref[...].astype(f32), got_ref[...].astype(f32))
    o_ref[...] = jnp.where(slot < n_ref[0], v, 0.0).astype(bf16)


def unpool_call(count, slots, own, got):
    rows = own.shape[0]
    block = rows // 2 if rows % 16 == 0 else rows
    spec = pl.BlockSpec((block, D), lambda i, n: (i, 0))
    return pl.pallas_call(
        lambda *refs: unpool_kernel(slots, *refs), out_shape=S(own.shape, bf16),
        grid_spec=pltpu.PrefetchScalarGridSpec(
            num_scalar_prefetch=1, grid=(rows // block,), in_specs=[spec, spec], out_specs=spec),
        cost_estimate=pl.CostEstimate(flops=1_000_000, bytes_accessed=7_000_000, transcendentals=0))(count, own, got)


def adam_kernel(scale, n_ref, own_ref, got_ref, *refs):
    ins, outs = refs[:6], refs[6:]
    g = jnp.where(n_ref[1] == 1, own_ref[...], got_ref[...])
    g = (g.astype(f32) * scale).T
    for k, (lo, hi) in enumerate(((0, 2), (2, NV))):
        gradient, parameter = g[lo:hi], ins[k][...]
        first = ADAM_FIRST * ins[2 + 2 * k][...] + (1.0 - ADAM_FIRST) * gradient
        second = ADAM_SECOND * ins[3 + 2 * k][...] + (1.0 - ADAM_SECOND) * gradient * gradient
        first_hat = first / (1.0 - ADAM_FIRST**ADAM_STEP)
        second_hat = second / (1.0 - ADAM_SECOND**ADAM_STEP)
        outs[k][...] = gradient
        outs[2 + k][...] = parameter - ADAM_RATE * (
            first_hat / (jnp.sqrt(second_hat) + ADAM_EPSILON) + ADAM_DECAY * parameter)
        outs[4 + 2 * k][...] = first
        outs[5 + 2 * k][...] = second


def adam(at, own, got, devices, *states):
    full = [pl.BlockSpec(v.shape, lambda i, n: (0, 0)) for v in states]
    one, two = S(states[0].shape, f32), S(states[1].shape, f32)
    last = pl.BlockSpec((own.shape[0], 128), lambda i, n: (0, Q_HALF // 128 - 1))
    return pl.pallas_call(
        lambda *refs: adam_kernel(1.0 / devices, *refs),
        out_shape=(one, two, one, two, one, one, two, two),
        grid_spec=pltpu.PrefetchScalarGridSpec(
            num_scalar_prefetch=1, grid=(1,), in_specs=[last, last] + full,
            out_specs=tuple(full[k] for k in (0, 1, 0, 1, 2, 3, 4, 5))), name="adam")(at, own, got, *states)


def muon_factor(row_total, column_total):
    return math.sqrt(max(1.0, row_total / column_total))


def body(images, cotangent, counts, w_qkv, w_proj, w_fc1, w_fc2, gains, biases,
         mom_qkv, mom_proj, mom_fc1, mom_fc2, gains_first, gains_second, biases_first, biases_second):
    slots = images.shape[0]
    rows = w_qkv.shape[0]
    devices = lax.axis_size("rep") * lax.axis_size("fsdp")
    me = lax.axis_index("fsdp").astype(jnp.int32)

    first = pl.pallas_call(pack_first_kernel, out_shape=S((rows, Q_COLS), bf16), name="pack_first")(w_qkv, gains, biases)
    q_pieces = all_pieces(first, "fsdp")

    count = counts[0]
    other = swap(counts, "fsdp", 1)[0]
    x_own = images.transpose(1, 0, 2).reshape(-1, D)
    x_got = swap(x_own, "fsdp", 1)
    c_own = cotangent.transpose(1, 0, 2).reshape(-1, D)
    c_got = swap(c_own, "fsdp", 1)
    n_own, n_got = (count + 1) >> 1, other >> 1
    n = jnp.stack([n_own + n_got, n_own, me]).astype(jnp.int32)

    def unpool(v):
        full = unpool_call(count.reshape(1), slots, v, swap(v, "fsdp", 1))
        return full.reshape(-1, slots, D).transpose(1, 0, 2)

    rest = pl.pallas_call(pack_rest_kernel, out_shape=S((rows, R_COLS), bf16), name="pack_rest")(w_proj, w_fc1, w_fc2.T)
    r_pieces = all_pieces(rest, "fsdp")

    rep_at = lax.axis_index("rep").astype(jnp.int32)
    at = jnp.stack([me, rep_at & 1, (rep_at >> 1) & 3])
    x, qkv, o, lse, vec = attn_fwd(n, slots, x_own, x_got, q_pieces)
    out, dh, do, r_send, r_keep, vb = mlp(n, slots, x, c_own, c_got, o, vec, r_pieces)
    terms = spread_xy(at, r_send, r_keep)
    in_grad, q_send, q_keep = attn_bwd(n, slots, x, qkv, lse, do, dh, vec, vb, q_pieces, x_own.shape[0])
    scale = 1.0 / devices
    _, _, mid_grads, mid_nexts, mid_pieces = sum_all(
        at, terms, (mom_proj, mom_fc1, mom_fc2.T), mlp_plan, scale)
    g, g_x, (grad_qkv,), (next_qkv,), qkv_pieces = sum_all(
        at, spread_xy(at, q_send, q_keep), (mom_qkv,), attn_plan, scale)
    block_out = unpool(out)
    input_grad = unpool(in_grad)
    vectors = adam(at, g, g_x, devices, gains, biases, gains_first, gains_second, biases_first, biases_second)
    grad_proj, grad_fc1, grad_fc2t = mid_grads
    next_proj, next_fc1, next_fc2t = mid_nexts

    core = me & 1
    mine, theirs = orth_call(orth_mlp_kernel, at, mid_pieces, F)
    got = send(theirs, 0, 1)
    orth_fc1, orth_fc2t = jnp.where(core == 0, mine, got), jnp.where(core == 0, got, mine)
    mine, theirs = orth_call(orth_attn_kernel, at, qkv_pieces + mid_pieces, 3 * D)
    got = send(theirs, 0, 1)
    orth_qkv, orth_proj = jnp.where(core == 0, mine, got), jnp.where(core == 0, got, mine)[:, :D]
    new_qkv = w_qkv - MUON_RATE * muon_factor(D, 3 * D) * orth_qkv
    new_proj = w_proj - MUON_RATE * muon_factor(D, D) * orth_proj
    new_fc1 = w_fc1 - MUON_RATE * muon_factor(D, F) * orth_fc1
    new_fc2t = w_fc2.T - MUON_RATE * muon_factor(F, D) * orth_fc2t
    grad_gains, grad_biases, new_gains, new_biases = vectors[:4]
    return (block_out, input_grad, grad_qkv, grad_proj, grad_fc1, grad_fc2t.T, grad_gains, grad_biases,
            new_qkv, new_proj, new_fc1, new_fc2t.T, new_gains, new_biases,
            next_qkv, next_proj, next_fc1, next_fc2t.T) + tuple(vectors[4:])


def solution(mesh):
    in_specs = (
        P(("rep", "fsdp"), None, None),
        P(("rep", "fsdp"), None, None),
        P(("rep", "fsdp")),
        P("fsdp", None),
        P("fsdp", None),
        P("fsdp", None),
        P(None, "fsdp"),
        P(None, "fsdp"),
        P(None, "fsdp"),
        P("fsdp", None),
        P("fsdp", None),
        P("fsdp", None),
        P(None, "fsdp"),
        P(None, "fsdp"),
        P(None, "fsdp"),
        P(None, "fsdp"),
        P(None, "fsdp"),
    )
    out_specs = (
        P(("rep", "fsdp"), None, None),
        P(("rep", "fsdp"), None, None),
        P("fsdp", None),
        P("fsdp", None),
        P("fsdp", None),
        P(None, "fsdp"),
        P(None, "fsdp"),
        P(None, "fsdp"),
        P("fsdp", None),
        P("fsdp", None),
        P("fsdp", None),
        P(None, "fsdp"),
        P(None, "fsdp"),
        P(None, "fsdp"),
        P("fsdp", None),
        P("fsdp", None),
        P("fsdp", None),
        P(None, "fsdp"),
        P(None, "fsdp"),
        P(None, "fsdp"),
        P(None, "fsdp"),
        P(None, "fsdp"),
    )
    return jax.shard_map(body, mesh=mesh, in_specs=in_specs, out_specs=out_specs, check_vma=False)
```

```python
import math

import jax
import jax.numpy as jnp
from jax import lax
from jax.experimental import pallas as pl
from jax.experimental.pallas import tpu as pltpu
from jax.sharding import PartitionSpec as P


NS_ITERS = 5
ADAM_STEP = 3
ORTHO_EPSILON = 1e-07
COEFF_FIRST = 3.4445
COEFF_SECOND = -4.775
COEFF_THIRD = 2.0315
MUON_RATE = 0.3
MUON_MOMENTUM = 0.95
ADAM_RATE = 0.2
ADAM_FIRST = 0.9
ADAM_SECOND = 0.95
ADAM_EPSILON = 1e-08
ADAM_DECAY = 0.25

D = 384
H = 6
HD = 64
F = 1536
T = 197
TP = 208
TC = T // 16 * 16
EPS = 1e-6
NV = 12
Q_COLS = 3 * D + 128
R_COLS = D + 2 * F + 128
f32 = jnp.float32
bf16 = jnp.bfloat16
SCALE = 1.0 / math.sqrt(HD)
SCALE_LOG2E = SCALE * math.log2(math.e)
VMEM_LIMIT = 60 * 1024 * 1024
S = jax.ShapeDtypeStruct
ANY = pl.BlockSpec(memory_space=pl.ANY)


def dot(a, b):
    return jnp.dot(a, b, preferred_element_type=f32)


def dot_nt(a, b):
    return lax.dot_general(a, b, (((1,), (1,)), ((), ())), preferred_element_type=f32)


def dot_tn(a, b):
    return lax.dot_general(a, b, (((0,), (0,)), ((), ())), preferred_element_type=f32)


def norm(x):
    xc = x - jnp.mean(x, axis=-1, keepdims=True)
    r = lax.rsqrt(jnp.mean(xc * xc, axis=-1, keepdims=True) + EPS)
    return xc * r, r


def norm_back(e, n, r):
    return r * (e - jnp.mean(e, axis=-1, keepdims=True) - n * jnp.mean(e * n, axis=-1, keepdims=True))


def col8(v):
    return jnp.sum(v.reshape(v.shape[0] // 8, 8, v.shape[1]), axis=0)


def total(v):
    return jnp.sum(v, axis=0, keepdims=True)


PHI_T = 0.28
PHI_C = (0.11652077999788102, 0.06749674653879187, 0.2689101818992952,
         -0.2369935012534717, 0.38987403003604115, -0.10580824648054844)
HALF_LOG2E = -0.5 * math.log2(math.e)
DENSITY = 1.0 / math.sqrt(2.0 * math.pi)


def gelu_parts(z):
    t = 1.0 / (1.0 + PHI_T * jnp.abs(z))
    bell = jnp.exp2((z * z) * HALF_LOG2E)
    poly = PHI_C[5] * t + PHI_C[4]
    for k in (3, 2, 1, 0):
        poly = poly * t + PHI_C[k]
    tail = (poly * t) * bell
    cdf = jnp.where(z < 0.0, tail, 1.0 - tail)
    return z * cdf, cdf + (z * DENSITY) * bell


def slot_of(n_ref):
    i = pl.program_id(0)
    return jnp.where(i < n_ref[1], 2 * i, 2 * (i - n_ref[1]) + 1)


def fill_pool(own_ref, got_ref, pool):
    rows = own_ref.shape[0]
    odd = lax.broadcasted_iota(jnp.int32, (rows, 128), 0) & 1
    for j in range(D // 128):
        cols = slice(128 * j, 128 * j + 128)
        pool[j, :rows] = jnp.where(odd == 0, own_ref[:, cols].astype(f32), got_ref[:, cols].astype(f32))
        pool[j, rows:] = jnp.zeros((pool.shape[1] - rows, 128), f32)


def load_image(n_ref, pool):
    rows = pl.ds(slot_of(n_ref), TP, stride=pool.shape[1] // TP)
    return jnp.concatenate([pool[j, rows, :] for j in range(D // 128)], axis=1)


def store_image(n_ref, pool, value):
    rows = pl.ds(slot_of(n_ref), TP, stride=pool.shape[1] // TP)
    for j in range(D // 128):
        pool[j, rows, :] = value[:, 128 * j : 128 * j + 128]


def empty_pool(pool, out_ref):
    for j in range(D // 128):
        out_ref[:, 128 * j : 128 * j + 128] = pool[j, : out_ref.shape[0]].astype(bf16)


def fetch(n_ref, pieces, buf, sems):
    rows = pieces[0].shape[0]
    copies = []
    for k, piece in enumerate(pieces):
        at = pl.multiple_of((n_ref[2] ^ k) * rows, 32)
        copies.append(pltpu.make_async_copy(piece, buf.at[pl.ds(at, rows)], sems.at[k]))
    for c in copies:
        c.start()
    for c in copies:
        c.wait()


def flush(n_ref, acc, send_ref, keep_ref):
    pairs, rows = keep_ref.shape[0], keep_ref.shape[1]
    me = n_ref[2] & 1
    for y in range(pairs):
        mine = pl.multiple_of((2 * y + me) * rows, 32)
        theirs = pl.multiple_of((2 * y + 1 - me) * rows, 32)
        keep_ref[y] = acc[pl.ds(mine, rows), :]
        send_ref[y] = acc[pl.ds(theirs, rows), :].astype(bf16)


def live_step(n_ref, step):
    pl.when(pl.program_id(0) < n_ref[0])(step)


def attn_fwd_kernel(parts, n_ref, xo_ref, xg_ref, *rest):
    pieces = rest[:parts]
    x_ref, qkv_ref, o_ref, lse_ref, vec_ref, w, pool, sems = rest[parts:]

    @pl.when(pl.program_id(0) == 0)
    def _():
        fetch(n_ref, pieces, w, sems)
        vec_ref[...] = w[:, 3 * D :].astype(f32).T[:16]
        fill_pool(xo_ref, xg_ref, pool)

    def step():
        x = load_image(n_ref, pool)
        x_ref[0] = x.astype(bf16)
        n1, _ = norm(x)
        a = (n1 * vec_ref[0:1] + vec_ref[2:3]).astype(bf16)
        qb = jnp.concatenate([vec_ref[3:4], jnp.zeros((1, D), f32), vec_ref[4:5]], axis=1)
        qkv = (dot(a, w[:, : 3 * D]) + qb).astype(bf16)
        real = lax.broadcasted_iota(jnp.int32, (TP - TC, 3 * D), 0) < T - TC
        qkv_ref[0, :TC] = qkv[:TC]
        qkv_ref[0, TC:] = jnp.where(real, qkv[TC:], jnp.zeros_like(qkv[TC:]))
        lane = lax.broadcasted_iota(jnp.int32, (TP, 128), 1)
        low = lane < HD
        key = lax.broadcasted_iota(jnp.int32, (TP, TP), 1) < T
        lse = jnp.zeros((TP, 128), f32)
        for pair in range(H // 2):
            at = pair * 128
            q, k, v = (qkv_ref[0, :, off + at : off + at + 128] for off in (0, D, 2 * D))
            zero = jnp.zeros_like(q)
            o = None
            for side in range(2):
                sel = low if side == 0 else jnp.logical_not(low)
                s = jnp.where(key, dot_nt(jnp.where(sel, q, zero), k) * SCALE_LOG2E, -1e30)
                l2 = jnp.log2(jnp.sum(jnp.exp2(s), axis=-1, keepdims=True))
                p = jnp.exp2(s - l2).astype(bf16)
                part = dot(p, jnp.where(sel, v, zero))
                o = part if o is None else o + part
                lse = jnp.where(lane == pair * 2 + side, l2, lse)
            o_ref[0, :, at : at + 128] = o.astype(bf16)
        lse_ref[0] = lse

    live_step(n_ref, step)


FC = 256


def mlp_kernel(parts, n_ref, x_ref, co_ref, cg_ref, o_ref, vec_ref, *rest):
    pieces = rest[:parts]
    out_ref, dh_ref, do_ref, send_ref, keep_ref, vb_ref, w, acc, vg, gbu, cpool, opool, bu_s, c_s, dy_s, ct_s, dyt_s, zb, db, ub, eb, out_s, dc_s, sems = rest[parts:]

    @pl.when(pl.program_id(0) == 0)
    def _():
        fetch(n_ref, pieces, w, sems)
        acc[...] = jnp.zeros_like(acc)
        vg[...] = jnp.zeros_like(vg)
        gbu[...] = jnp.zeros_like(gbu)
        fill_pool(co_ref, cg_ref, cpool)
        bu_s[...] = jnp.concatenate([vec_ref[8 + j : 9 + j] for j in range(F // D)], axis=1)

    def step():
        g2, b2, bo, bd = vec_ref[1:2], vec_ref[6:7], vec_ref[5:6], vec_ref[7:8]
        x = x_ref[0].astype(f32)
        o = o_ref[0]
        h = x + dot(o, w[:, :D]) + bo
        n2, r2 = norm(h)
        c = (n2 * g2 + b2).astype(bf16)
        dyf = load_image(n_ref, cpool)
        dy = dyf.astype(bf16)
        steps = F // FC
        c_s[...] = c
        dy_s[...] = dy
        ct_s[...] = c.T
        dyt_s[...] = dy.T

        def cols(base, j):
            return slice(base + j * FC, base + j * FC + FC)

        def produce(j, slot):
            zb[slot] = dot(c_s[...], w[:, cols(D, j)])
            db[slot] = dot(dy_s[...], w[:, cols(D + F, j)])

        def middle(j, slot):
            u, slope = gelu_parts(zb[slot] + bu_s[:, cols(0, j)])
            dz = db[slot] * slope
            gbu[:, cols(0, j)] += col8(dz)
            ub[slot] = u.astype(bf16)
            eb[slot] = dz.astype(bf16)

        def consume(j, slot, first=False):
            u, dzb = ub[slot], eb[slot]
            o1, d1 = dot_nt(u, w[:, cols(D + F, j)]), dot_nt(dzb, w[:, cols(D, j)])
            out_s[...] = o1 if first else out_s[...] + o1
            dc_s[...] = d1 if first else dc_s[...] + d1
            acc[:, cols(D, j)] += dot(ct_s[...], dzb)
            acc[:, cols(D + F, j)] += dot(dyt_s[...], u)

        produce(0, 0)
        produce(1, 1)
        middle(0, 0)
        for j in range(1, steps):
            if j + 1 < steps:
                produce(j + 1, (j + 1) % 3)
            consume(j - 1, (j - 1) % 3, j == 1)
            middle(j, j % 3)
        consume(steps - 1, (steps - 1) % 3)
        out, dc = out_s[...], dc_s[...]
        store_image(n_ref, opool, h + out + bd)
        dh = dyf + norm_back(dc * g2, n2, r2)
        dh_ref[0] = dh
        dhb = dh.astype(bf16)
        acc[:, :D] += dot(o.T, dhb)
        do_ref[0] = dot_nt(dhb, w[:, :D]).astype(bf16)
        vg[0:8] += col8(dc * n2)
        vg[8:16] += col8(dh)
        vg[16:24] += col8(dc)
        vg[24:32] += col8(dyf)

    live_step(n_ref, step)

    @pl.when(pl.program_id(0) == n_ref[0] - 1)
    def _():
        empty_pool(opool, out_ref)
        flush(n_ref, acc, send_ref, keep_ref)
        rows = [total(vg[8 * k : 8 * k + 8]) for k in range(4)]
        rows += [total(gbu[:, k * D : (k + 1) * D]) for k in range(F // D)]
        vb_ref[...] = jnp.concatenate(rows, axis=0)


def attn_bwd_kernel(parts, n_ref, x_ref, qkv_ref, lse_ref, do_ref, dh_ref, vec_ref, vb_ref, *rest):
    pieces = rest[:parts]
    out_ref, send_ref, keep_ref, w, acc, vg, dqkv, opool, sb, db, pb, gb, tb, sems = rest[parts:]

    @pl.when(pl.program_id(0) == 0)
    def _():
        fetch(n_ref, pieces, w, sems)
        acc[...] = jnp.zeros_like(acc)
        vg[...] = jnp.zeros_like(vg)

    def step():
        g1, b1 = vec_ref[0:1], vec_ref[2:3]
        x = x_ref[0].astype(f32)
        n1, r1 = norm(x)
        at_ = (n1 * g1 + b1).astype(bf16).T
        low = lax.broadcasted_iota(jnp.int32, (TP, 128), 1) < HD
        real = lax.broadcasted_iota(jnp.int32, (TP - TC, 128), 0) < T - TC

        def mask(h, v):
            return jnp.where(low if h % 2 == 0 else jnp.logical_not(low), v, jnp.zeros_like(v))

        def lanes(h, off=0):
            return slice(off + (h // 2) * 128, off + (h // 2) * 128 + 128)

        def produce(h):
            sb[h % 3] = dot_nt(mask(h, qkv_ref[0, :, lanes(h)]), qkv_ref[0, :, lanes(h, D)])
            db[h % 3] = dot_nt(mask(h, do_ref[0, :, lanes(h)]), qkv_ref[0, :, lanes(h, 2 * D)])

        def middle(h):
            p = jnp.exp2(sb[h % 3] * SCALE_LOG2E - lse_ref[0, :, h : h + 1])
            dp = db[h % 3]
            pb[h % 2] = p.astype(bf16)
            delta = jnp.sum(p * dp, axis=-1, keepdims=True)
            gb[h % 2] = (p * (dp - delta) * SCALE).astype(bf16)

        def consume(h):
            ds = gb[h % 2]
            part = (dot(ds, mask(h, qkv_ref[0, :, lanes(h, D)])),
                    dot_tn(ds, mask(h, qkv_ref[0, :, lanes(h)])),
                    dot_tn(pb[h % 2], mask(h, do_ref[0, :, lanes(h)])))
            if h % 2 == 0:
                for k in range(3):
                    tb[k] = part[k]
                return
            dq, dk, dv = (tb[k] + part[k] for k in range(3))
            dqkv[:, lanes(h)] = dq.astype(bf16)
            for v, off in ((dk, D), (dv, 2 * D)):
                v_b = v.astype(bf16)
                dqkv[:TC, lanes(h, off)] = v_b[:TC]
                dqkv[TC:, lanes(h, off)] = jnp.where(real, v_b[TC:], jnp.zeros_like(v_b[TC:]))
            vg[16:24, lanes(h)] += col8(dq)
            vg[24:32, lanes(h)] += col8(dv[:TC]) + col8(jnp.where(real, dv[TC:], 0.0))

        produce(0)
        produce(1)
        middle(0)
        for h in range(1, H):
            if h + 1 < H:
                produce(h + 1)
            consume(h - 1)
            middle(h)
        consume(H - 1)
        dqkv_b = dqkv[...]
        acc[:, : 3 * D] += dot(at_, dqkv_b)
        da = dot_nt(dqkv_b, w[:, : 3 * D])
        store_image(n_ref, opool, dh_ref[0] + norm_back(da * g1, n1, r1))
        vg[0:8] += col8(da * n1)
        vg[8:16] += col8(da)

    live_step(n_ref, step)

    @pl.when(pl.program_id(0) == n_ref[0] - 1)
    def _():
        empty_pool(opool, out_ref)
        mine = [total(vg[8 * k : 8 * k + 8]) for k in range(4)]
        vb = vb_ref[...]
        rows = jnp.concatenate([mine[0], vb[0:1], mine[1], mine[2], mine[3], vb[1:8], jnp.zeros((116, D), f32)], axis=0)
        acc[:, 3 * D :] = rows.T
        flush(n_ref, acc, send_ref, keep_ref)


def whole(shape):
    return pl.BlockSpec(shape, lambda i, n: (0,) * len(shape))


def item(rows, cols):
    return pl.BlockSpec((1, rows, cols), lambda i, n: (jnp.minimum(i, n[0] - 1), 0, 0))


def layer_call(kernel, n, slots, ins, in_specs, pieces, outs, out_specs, scratch, flops):
    parts = len(pieces)
    return pl.pallas_call(
        lambda *refs: kernel(parts, *refs),
        out_shape=outs,
        grid_spec=pltpu.PrefetchScalarGridSpec(
            num_scalar_prefetch=1, grid=(slots,), in_specs=list(in_specs) + [ANY] * parts,
            out_specs=out_specs, scratch_shapes=list(scratch) + [pltpu.SemaphoreType.DMA((parts,))]),
        compiler_params=pltpu.CompilerParams(
            dimension_semantics=("arbitrary",), vmem_limit_bytes=VMEM_LIMIT),
        cost_estimate=pl.CostEstimate(flops=flops, bytes_accessed=20_000_000, transcendentals=0))(n, *ins, *pieces)


def once(shape):
    return pl.BlockSpec(shape, lambda i, n: (0,) * len(shape), pipeline_mode=pl.Buffered(1))


def attn_fwd(n, slots, x_own, x_got, pieces):
    rows = x_own.shape[0]
    return layer_call(
        attn_fwd_kernel, n, slots, (x_own, x_got), (once((rows, D)), once((rows, D))), pieces,
        (S((slots, TP, D), bf16), S((slots, TP, 3 * D), bf16), S((slots, TP, D), bf16), S((slots, TP, 128), f32),
         S((16, D), f32)),
        (item(TP, D), item(TP, 3 * D), item(TP, D), item(TP, 128), whole((16, D))),
        (pltpu.VMEM((D, Q_COLS), bf16), pltpu.VMEM((D // 128, TP * slots, 128), f32)), 10_000_000_000)


def reduced(parts, cols):
    shape = (parts // 2, D // parts, cols)
    return (S(shape, bf16), S(shape, f32)), (once(shape), once(shape))


def mlp(n, slots, x, c_own, c_got, o, vec, pieces):
    rows = c_own.shape[0]
    r_shape, r_spec = reduced(len(pieces), R_COLS)
    return layer_call(
        mlp_kernel, n, slots, (x, c_own, c_got, o, vec),
        (item(TP, D), once((rows, D)), once((rows, D)), item(TP, D), whole((16, D))), pieces,
        (S((rows, D), bf16), S((slots, TP, D), f32), S((slots, TP, D), bf16)) + r_shape + (S((8, D), f32),),
        (once((rows, D)), item(TP, D), item(TP, D)) + r_spec + (whole((8, D)),),
        (pltpu.VMEM((D, R_COLS), bf16), pltpu.VMEM((D, R_COLS), f32), pltpu.VMEM((32, D), f32),
         pltpu.VMEM((8, F), f32), pltpu.VMEM((D // 128, TP * slots, 128), f32), pltpu.VMEM((D // 128, TP * slots, 128), f32),
         pltpu.VMEM((1, F), f32), pltpu.VMEM((TP, D), bf16), pltpu.VMEM((TP, D), bf16), pltpu.VMEM((D, TP), bf16),
         pltpu.VMEM((D, TP), bf16), pltpu.VMEM((3, TP, FC), f32), pltpu.VMEM((3, TP, FC), f32),
         pltpu.VMEM((3, TP, FC), bf16), pltpu.VMEM((3, TP, FC), bf16), pltpu.VMEM((TP, D), f32),
         pltpu.VMEM((TP, D), f32)),
        25_000_000_000)


def attn_bwd(n, slots, x, qkv, lse, do, dh, vec, vb, pieces, rows):
    r_shape, r_spec = reduced(len(pieces), Q_COLS)
    return layer_call(
        attn_bwd_kernel, n, slots, (x, qkv, lse, do, dh, vec, vb),
        (item(TP, D), item(TP, 3 * D), item(TP, 128), item(TP, D), item(TP, D),
         whole((16, D)), whole((8, D))), pieces,
        (S((rows, D), bf16),) + r_shape, (once((rows, D)),) + r_spec,
        (pltpu.VMEM((D, Q_COLS), bf16), pltpu.VMEM((D, Q_COLS), f32), pltpu.VMEM((32, D), f32),
         pltpu.VMEM((TP, 3 * D), bf16), pltpu.VMEM((D // 128, TP * slots, 128), f32), pltpu.VMEM((3, TP, TP), f32),
         pltpu.VMEM((3, TP, TP), f32), pltpu.VMEM((2, TP, TP), bf16), pltpu.VMEM((2, TP, TP), bf16),
         pltpu.VMEM((3, TP, 128), f32)), 20_000_000_000)


def pack_first_kernel(w_ref, g_ref, b_ref, o_ref):
    rows = w_ref.shape[0]
    vec = jnp.concatenate([g_ref[...], b_ref[...], jnp.zeros((128 - NV, rows), f32)], axis=0)
    o_ref[:, : 3 * D] = w_ref[...].astype(bf16)
    o_ref[:, 3 * D :] = vec.T.astype(bf16)


def pack_rest_kernel(p_ref, a_ref, b_ref, o_ref):
    o_ref[:, :D] = p_ref[...].astype(bf16)
    o_ref[:, D : D + F] = a_ref[...].astype(bf16)
    o_ref[:, D + F : D + 2 * F] = b_ref[...].astype(bf16)
    o_ref[:, D + 2 * F :] = jnp.zeros((o_ref.shape[0], R_COLS - D - 2 * F), bf16)


def split3(a):
    hi = a.astype(bf16)
    return hi, (a - hi.astype(f32)).astype(bf16)


def dot3(a, b):
    return dot(jnp.concatenate([a[0], a[1], a[0]], axis=1), jnp.concatenate([b[0], b[0], b[1]], axis=0))


def dot3_sym(a, b):
    left = jnp.concatenate([a[0], a[1], a[0]], axis=1)
    right = jnp.concatenate([b[0], b[0], b[1]], axis=0)
    wide = dot(left, right[:, :256])
    corner = dot(left[256:], right[:, 256:])
    return jnp.concatenate([wide, jnp.concatenate([wide[256:].T, corner], axis=0)], axis=1)


def orth_rows(m, q_s, at, rows):
    a = dot_nt(m, m)
    diag = lax.broadcasted_iota(jnp.int32, (D, D), 0) == lax.broadcasted_iota(jnp.int32, (D, D), 1)
    ssq = jnp.sum(jnp.where(diag, a, 0.0), axis=(0, 1), keepdims=True)
    s = 1.0 / (jnp.sqrt(ssq) + ORTHO_EPSILON)
    a = a * (s * s)
    eye = jnp.where(diag, COEFF_FIRST, 0.0)
    q = None
    for k in range(NS_ITERS - 1):
        a_s = split3(a)
        p = eye + COEFF_SECOND * a + COEFF_THIRD * dot3_sym(a_s, a_s)
        p_s = split3(p)
        if k == 0:
            q_s[...] = p
            q = q_s[pl.ds(at, rows), :]
        else:
            q = dot3(split3(q), p_s)
        if k < NS_ITERS - 2:
            a = dot3_sym(split3(dot3_sym(p_s, a_s)), p_s)

    def times_last(v):
        return dot3(split3(dot3(split3(dot3(split3(v), p_s)), a_s)), p_s)

    qa = times_last(q)
    q = COEFF_FIRST * q + COEFF_SECOND * qa + COEFF_THIRD * times_last(qa)
    hi, lo = split3(q * s)
    return dot(hi, m) + dot(lo, m)


def fetch_cols(n_ref, pieces, buf, sems, at_col, cols):
    rows = pieces[0].shape[0]
    copies = []
    for k, piece in enumerate(pieces):
        at = pl.multiple_of((n_ref[0] ^ k) * rows, 32)
        copies.append(pltpu.make_async_copy(
            piece.at[:, pl.ds(at_col, cols)], buf.at[pl.ds(at, rows), pl.ds(0, cols)], sems.at[k]))
    for c in copies:
        c.start()
    for c in copies:
        c.wait()


def orth_both(n_ref, mine_ref, theirs_ref, m, q_s, o_s):
    rows = mine_ref.shape[0]
    core = n_ref[0] & 1
    at = pl.multiple_of((n_ref[0] - core) * rows, 32)
    o_s[...] = orth_rows(m[...], q_s, at, 2 * rows)
    mine_ref[...] = o_s[pl.ds(pl.multiple_of(core * rows, 32), rows), :]
    theirs_ref[...] = o_s[pl.ds(pl.multiple_of((1 - core) * rows, 32), rows), :]


def orth_mlp_kernel(parts, n_ref, *rest):
    pieces = rest[:parts]
    mine_ref, theirs_ref, m, q_s, o_s, sems = rest[parts:]
    fetch_cols(n_ref, pieces, m, sems, pl.multiple_of(D + (n_ref[0] & 1) * F, 128), F)
    orth_both(n_ref, mine_ref, theirs_ref, m, q_s, o_s)


def orth_attn_kernel(parts, n_ref, *rest):
    pieces, others = rest[:parts], rest[parts : 2 * parts]
    mine_ref, theirs_ref, m, q_s, o_s, sems = rest[2 * parts :]

    @pl.when(n_ref[0] & 1 == 0)
    def _():
        fetch_cols(n_ref, pieces, m, sems, 0, 3 * D)

    @pl.when(n_ref[0] & 1 == 1)
    def _():
        m[:, D:] = jnp.zeros((D, 2 * D), bf16)
        fetch_cols(n_ref, others, m, sems, 0, D)

    orth_both(n_ref, mine_ref, theirs_ref, m, q_s, o_s)


def orth_call(kernel, me, pieces, more, cols):
    parts = len(pieces)
    rows = pieces[0].shape[0]
    spec = pl.BlockSpec((rows, cols), lambda i, n: (0, 0))
    return pl.pallas_call(
        lambda *refs: kernel(parts, *refs),
        out_shape=(S((rows, cols), f32),) * 2,
        grid_spec=pltpu.PrefetchScalarGridSpec(
            num_scalar_prefetch=1, grid=(1,), in_specs=[ANY] * (parts + len(more)), out_specs=(spec,) * 2,
            scratch_shapes=[pltpu.VMEM((D, cols), bf16), pltpu.VMEM((D, D), f32), pltpu.VMEM((2 * rows, cols), f32),
                            pltpu.SemaphoreType.DMA((parts,))]),
        compiler_params=pltpu.CompilerParams(vmem_limit_bytes=VMEM_LIMIT),
        cost_estimate=pl.CostEstimate(flops=8_000_000_000, bytes_accessed=4_000_000, transcendentals=0))(me, *pieces, *more)


def swap(v, axis, k):
    return lax.ppermute(v, axis, [(i, i ^ k) for i in range(lax.axis_size(axis))])


def bits(axis):
    return range(lax.axis_size(axis).bit_length() - 1)


def bit(axis, b):
    return (lax.axis_index(axis) >> b) & 1


def all_pieces(v, axis):
    pieces = {0: v}
    for b in reversed(bits(axis)):
        pieces.update({k ^ (1 << b): swap(p, axis, 1 << b) for k, p in list(pieces.items())})
    return [pieces[k] for k in range(lax.axis_size(axis))]


def take(v, i):
    return lax.dynamic_index_in_dim(v, i, 0, keepdims=False)


def sum_blocks(send, keep):
    got = swap(send, "fsdp", 1)
    keep, got = (v.reshape((2, -1) + v.shape[1:]) for v in (keep, got))
    for b in reversed(bits("fsdp")[1:]):
        me = bit("fsdp", b)
        sent = (take(keep, 1 - me) + take(got, 1 - me).astype(f32)).astype(bf16)
        own = take(keep, me) + take(got, me).astype(f32)
        got = swap(sent, "fsdp", 1 << b)
        keep = own
        if keep.shape[0] > 1:
            keep, got = (v.reshape((2, -1) + v.shape[1:]) for v in (keep, got))
    return (keep + got.astype(f32)).reshape(keep.shape[-2:])


def halves(v, axis):
    n = v.shape[axis] // 2
    return lax.slice_in_dim(v, 0, n, axis=axis), lax.slice_in_dim(v, n, 2 * n, axis=axis)


def sum_groups(v):
    for b in bits("rep"):
        me = bit("rep", b)
        lo, hi = halves(v, 1 if b == 0 else 0)
        got = swap(jnp.where(me == 0, hi, lo).astype(bf16), "rep", 1 << b)
        v = jnp.where(me == 0, lo, hi) + got.astype(f32)
    v = v.astype(bf16)
    for b in reversed(bits("rep")):
        me = bit("rep", b)
        got = swap(v, "rep", 1 << b)
        v = jnp.concatenate([jnp.where(me == 0, v, got), jnp.where(me == 0, got, v)], axis=1 if b == 0 else 0)
    return v


def sum_groups_whole(v):
    v = v.astype(bf16)
    for b in bits("rep"):
        got = swap(v, "rep", 1 << b)
        v = (v.astype(f32) + got.astype(f32)).astype(bf16)
    return v


def unpool_kernel(slots, n_ref, own_ref, got_ref, o_ref):
    row = pl.program_id(0) * own_ref.shape[0] + lax.broadcasted_iota(jnp.int32, own_ref.shape, 0)
    slot = row & (slots - 1)
    v = jnp.where(slot & 1 == 0, own_ref[...].astype(f32), got_ref[...].astype(f32))
    o_ref[...] = jnp.where(slot < n_ref[0], v, 0.0).astype(bf16)


def unpool_call(count, slots, own, got):
    rows = own.shape[0]
    block = rows // 2 if rows % 16 == 0 else rows
    spec = pl.BlockSpec((block, D), lambda i, n: (i, 0))
    return pl.pallas_call(
        lambda *refs: unpool_kernel(slots, *refs), out_shape=S(own.shape, bf16),
        grid_spec=pltpu.PrefetchScalarGridSpec(
            num_scalar_prefetch=1, grid=(rows // block,), in_specs=[spec, spec], out_specs=spec),
        cost_estimate=pl.CostEstimate(flops=1_000_000, bytes_accessed=7_000_000, transcendentals=0))(count, own, got)


def adam_kernel(scale, g_ref, *refs):
    ins, outs = refs[:6], refs[6:]
    g = (g_ref[...].astype(f32) * scale).T
    for k, (lo, hi) in enumerate(((0, 2), (2, NV))):
        gradient, parameter = g[lo:hi], ins[k][...]
        first = ADAM_FIRST * ins[2 + 2 * k][...] + (1.0 - ADAM_FIRST) * gradient
        second = ADAM_SECOND * ins[3 + 2 * k][...] + (1.0 - ADAM_SECOND) * gradient * gradient
        first_hat = first / (1.0 - ADAM_FIRST**ADAM_STEP)
        second_hat = second / (1.0 - ADAM_SECOND**ADAM_STEP)
        outs[k][...] = gradient
        outs[2 + k][...] = parameter - ADAM_RATE * (
            first_hat / (jnp.sqrt(second_hat) + ADAM_EPSILON) + ADAM_DECAY * parameter)
        outs[4 + 2 * k][...] = first
        outs[5 + 2 * k][...] = second


def adam(last, devices, *states):
    full = [pl.BlockSpec(v.shape, lambda i: (0, 0)) for v in states]
    one, two = S(states[0].shape, f32), S(states[1].shape, f32)
    return pl.pallas_call(
        lambda *refs: adam_kernel(1.0 / devices, *refs),
        grid=(1,), out_shape=(one, two, one, two, one, one, two, two),
        in_specs=[pl.BlockSpec((last.shape[0], 128), lambda i: (0, 3 * D // 128))] + full,
        out_specs=tuple(full[k] for k in (0, 1, 0, 1, 2, 3, 4, 5)), name="adam")(last, *states)


def muon_factor(row_total, column_total):
    return math.sqrt(max(1.0, row_total / column_total))


def body(images, cotangent, counts, w_qkv, w_proj, w_fc1, w_fc2, gains, biases,
         mom_qkv, mom_proj, mom_fc1, mom_fc2, gains_first, gains_second, biases_first, biases_second):
    slots = images.shape[0]
    rows = w_qkv.shape[0]
    devices = lax.axis_size("rep") * lax.axis_size("fsdp")
    me = lax.axis_index("fsdp").astype(jnp.int32)

    first = pl.pallas_call(pack_first_kernel, out_shape=S((rows, Q_COLS), bf16), name="pack_first")(w_qkv, gains, biases)
    q_pieces = all_pieces(first, "fsdp")

    count = counts[0]
    other = swap(counts, "fsdp", 1)[0]
    x_own = images.transpose(1, 0, 2).reshape(-1, D)
    x_got = swap(x_own, "fsdp", 1)
    c_own = cotangent.transpose(1, 0, 2).reshape(-1, D)
    c_got = swap(c_own, "fsdp", 1)
    n_own, n_got = (count + 1) >> 1, other >> 1
    n = jnp.stack([n_own + n_got, n_own, me]).astype(jnp.int32)

    def unpool(v):
        full = unpool_call(count.reshape(1), slots, v, swap(v, "fsdp", 1))
        return full.reshape(-1, slots, D).transpose(1, 0, 2)

    rest = pl.pallas_call(pack_rest_kernel, out_shape=S((rows, R_COLS), bf16), name="pack_rest")(w_proj, w_fc1, w_fc2.T)
    r_pieces = all_pieces(rest, "fsdp")

    x, qkv, o, lse, vec = attn_fwd(n, slots, x_own, x_got, q_pieces)
    out, dh, do, r_send, r_keep, vb = mlp(n, slots, x, c_own, c_got, o, vec, r_pieces)
    mid = sum_blocks(r_send, r_keep)
    in_grad, q_send, q_keep = attn_bwd(n, slots, x, qkv, lse, do, dh, vec, vb, q_pieces, x_own.shape[0])
    mid = sum_groups(mid)
    last = sum_groups_whole(sum_blocks(q_send, q_keep))
    block_out = unpool(out)
    input_grad = unpool(in_grad)

    vectors = adam(last, devices, gains, biases, gains_first, gains_second, biases_first, biases_second)
    last = last.astype(f32) * (1.0 / devices)
    grad_qkv = last[:, : 3 * D]
    next_qkv = MUON_MOMENTUM * mom_qkv + grad_qkv
    qkv_pieces = all_pieces(next_qkv.astype(bf16), "fsdp")
    mid = mid.astype(f32) * (1.0 / devices)
    mom_mid = jnp.concatenate([mom_proj, mom_fc1, mom_fc2.T], axis=1)
    next_mid = MUON_MOMENTUM * mom_mid + mid[:, : D + 2 * F]
    mid_pieces = all_pieces(next_mid.astype(bf16), "fsdp")
    grad_proj, grad_fc1, grad_fc2t = mid[:, :D], mid[:, D : D + F], mid[:, D + F : D + 2 * F]
    next_proj, next_fc1, next_fc2t = next_mid[:, :D], next_mid[:, D : D + F], next_mid[:, D + F :]

    core = me & 1
    mine, theirs = orth_call(orth_mlp_kernel, me.reshape(1), mid_pieces, [], F)
    got = swap(theirs, "fsdp", 1)
    orth_fc1, orth_fc2t = jnp.where(core == 0, mine, got), jnp.where(core == 0, got, mine)
    mine, theirs = orth_call(orth_attn_kernel, me.reshape(1), qkv_pieces, mid_pieces, 3 * D)
    got = swap(theirs, "fsdp", 1)
    orth_qkv, orth_proj = jnp.where(core == 0, mine, got), jnp.where(core == 0, got, mine)[:, :D]
    new_qkv = w_qkv - MUON_RATE * muon_factor(D, 3 * D) * orth_qkv
    new_proj = w_proj - MUON_RATE * muon_factor(D, D) * orth_proj
    new_fc1 = w_fc1 - MUON_RATE * muon_factor(D, F) * orth_fc1
    new_fc2t = w_fc2.T - MUON_RATE * muon_factor(F, D) * orth_fc2t
    grad_gains, grad_biases, new_gains, new_biases = vectors[:4]
    return (block_out, input_grad, grad_qkv, grad_proj, grad_fc1, grad_fc2t.T, grad_gains, grad_biases,
            new_qkv, new_proj, new_fc1, new_fc2t.T, new_gains, new_biases,
            next_qkv, next_proj, next_fc1, next_fc2t.T) + tuple(vectors[4:])


def solution(mesh):
    in_specs = (
        P(("rep", "fsdp"), None, None),
        P(("rep", "fsdp"), None, None),
        P(("rep", "fsdp")),
        P("fsdp", None),
        P("fsdp", None),
        P("fsdp", None),
        P(None, "fsdp"),
        P(None, "fsdp"),
        P(None, "fsdp"),
        P("fsdp", None),
        P("fsdp", None),
        P("fsdp", None),
        P(None, "fsdp"),
        P(None, "fsdp"),
        P(None, "fsdp"),
        P(None, "fsdp"),
        P(None, "fsdp"),
    )
    out_specs = (
        P(("rep", "fsdp"), None, None),
        P(("rep", "fsdp"), None, None),
        P("fsdp", None),
        P("fsdp", None),
        P("fsdp", None),
        P(None, "fsdp"),
        P(None, "fsdp"),
        P(None, "fsdp"),
        P("fsdp", None),
        P("fsdp", None),
        P("fsdp", None),
        P(None, "fsdp"),
        P(None, "fsdp"),
        P(None, "fsdp"),
        P("fsdp", None),
        P("fsdp", None),
        P("fsdp", None),
        P(None, "fsdp"),
        P(None, "fsdp"),
        P(None, "fsdp"),
        P(None, "fsdp"),
        P(None, "fsdp"),
    )
    return jax.shard_map(body, mesh=mesh, in_specs=in_specs, out_specs=out_specs, check_vma=False)
```

```python
import math

import jax
import jax.numpy as jnp
from jax import lax
from jax.experimental import pallas as pl
from jax.experimental.pallas import tpu as pltpu
from jax.sharding import PartitionSpec as P


NS_ITERS = 5
ADAM_STEP = 3
ORTHO_EPSILON = 1e-07
COEFF_FIRST = 3.4445
COEFF_SECOND = -4.775
COEFF_THIRD = 2.0315
MUON_RATE = 0.3
MUON_MOMENTUM = 0.95
ADAM_RATE = 0.2
ADAM_FIRST = 0.9
ADAM_SECOND = 0.95
ADAM_EPSILON = 1e-08
ADAM_DECAY = 0.25

D = 384
H = 6
HD = 64
F = 1536
T = 197
TP = 208
TC = T // 16 * 16
EPS = 1e-6
NV = 12
Q_COLS = 3 * D + 128
R_COLS = D + 2 * F + 128
f32 = jnp.float32
bf16 = jnp.bfloat16
SCALE = 1.0 / math.sqrt(HD)
SCALE_LOG2E = SCALE * math.log2(math.e)
VMEM_LIMIT = 60 * 1024 * 1024
S = jax.ShapeDtypeStruct
ANY = pl.BlockSpec(memory_space=pl.ANY)


def dot(a, b):
    return jnp.dot(a, b, preferred_element_type=f32)


def dot_nt(a, b):
    return lax.dot_general(a, b, (((1,), (1,)), ((), ())), preferred_element_type=f32)


def dot_tn(a, b):
    return lax.dot_general(a, b, (((0,), (0,)), ((), ())), preferred_element_type=f32)


def norm(x):
    xc = x - jnp.mean(x, axis=-1, keepdims=True)
    r = lax.rsqrt(jnp.mean(xc * xc, axis=-1, keepdims=True) + EPS)
    return xc * r, r


def norm_back(e, n, r):
    return r * (e - jnp.mean(e, axis=-1, keepdims=True) - n * jnp.mean(e * n, axis=-1, keepdims=True))


def col8(v):
    return jnp.sum(v.reshape(v.shape[0] // 8, 8, v.shape[1]), axis=0)


def total(v):
    return jnp.sum(v, axis=0, keepdims=True)


PHI_T = 0.28
PHI_C = (0.11652077999788102, 0.06749674653879187, 0.2689101818992952,
         -0.2369935012534717, 0.38987403003604115, -0.10580824648054844)
HALF_LOG2E = -0.5 * math.log2(math.e)
DENSITY = 1.0 / math.sqrt(2.0 * math.pi)


def gelu_parts(z):
    t = 1.0 / (1.0 + PHI_T * jnp.abs(z))
    bell = jnp.exp2((z * z) * HALF_LOG2E)
    poly = PHI_C[5] * t + PHI_C[4]
    for k in (3, 2, 1, 0):
        poly = poly * t + PHI_C[k]
    tail = (poly * t) * bell
    cdf = jnp.where(z < 0.0, tail, 1.0 - tail)
    return z * cdf, cdf + (z * DENSITY) * bell


MOVED = 2
N_ITEMS, N_OWN, ME, N_POOL, OWN_GAP, OWN_JUMP, GOT_GAP, GOT_JUMP, FROM_X, TO_X, TO_Z, COUNT = range(12)


def make_plan(me_ref, *refs):
    v, o_ref = [ref[k] for ref in refs[:4] for k in range(2)], refs[4]
    core = me_ref[0] & 1
    loads = [v[2 * k] + v[2 * k + 1] for k in range(4)]

    def flow(a, b):
        return jnp.minimum((a - b) >> 1, 2 * MOVED), jnp.minimum((b - a) >> 1, 2 * MOVED)

    def share(amount, spare, k):
        return jnp.clip(jnp.minimum((amount + 1 - k) >> 1, spare), 0, MOVED)

    def both(amount, pair, kept):
        return [share(amount, c - kept, k) for c, k in zip(pair, (core, 1 - core))]

    def edge(a, b, load_a, load_b, kept):
        out, back = flow(load_a, load_b)
        s, r = both(out, a, kept), both(back, b, kept)
        return s, r, load_a + r[0] + r[1] - s[0] - s[1], load_b + s[0] + s[1] - r[0] - r[1]

    sx, rx, load, _ = edge(v[0:2], v[2:4], loads[0], loads[1], 1)
    _, _, load_z, _ = edge(v[4:6], v[6:8], loads[2], loads[3], 1)
    sz, rz, _, _ = edge(v[0:2], v[4:6], load, load_z, MOVED + 1)

    def kept(c, x, z, odd):
        hi = jnp.maximum(c - MOVED, 0)
        below, jump, top = ((t + 1 - odd) >> 1 for t in (hi - z, hi, c - x))
        return below + jnp.maximum(top - jump, 0), below, jump

    n_own, own_gap, own_jump = kept(v[0], sx[0], sz[0], 0)
    n_got, got_gap, got_jump = kept(v[1], sx[1], sz[1], 1)
    for k, value in enumerate((n_own + n_got + rx[0] + rz[0], n_own, me_ref[0], n_own + n_got, own_gap, own_jump,
                               got_gap, got_jump, rx[0], sx[0], sz[0], v[0])):
        o_ref[k] = value


def first_row(n_ref, i, slots):
    j, k = i - n_ref[N_OWN], i - n_ref[N_POOL]
    own = 2 * jnp.where(i < n_ref[OWN_GAP], i, i - n_ref[OWN_GAP] + n_ref[OWN_JUMP])
    got = 2 * jnp.where(j < n_ref[GOT_GAP], j, j - n_ref[GOT_GAP] + n_ref[GOT_JUMP]) + 1
    moved = TP * slots + jnp.where(k < n_ref[FROM_X], k, k - n_ref[FROM_X] + MOVED)
    return jnp.where(j < 0, own, jnp.where(k < 0, got, moved))


def item_copy(flow, k, i, out=False):
    ref, buf, sem = flow[k]
    here, there = buf.at[i & 1], ref.at[i]
    return pltpu.make_async_copy(here, there, sem.at[i & 1]) if out else pltpu.make_async_copy(there, here, sem.at[i & 1])


def start_all(copies):
    for c in copies:
        c.start()
    return copies


def wait_all(copies):
    for c in copies:
        c.wait()


def first_items(ins):
    return start_all([item_copy(ins, k, 0) for k in range(len(ins))])


def stream(count, ins, outs, body):
    def turn(i, carry):
        @pl.when(i + 1 < count)
        def _():
            start_all([item_copy(ins, k, i + 1) for k in range(len(ins))])

        wait_all([item_copy(ins, k, i) for k in range(len(ins))])

        @pl.when(i >= 2)
        def _():
            wait_all([item_copy(outs, k, i - 2, True) for k in range(len(outs))])

        body(i, i & 1)
        start_all([item_copy(outs, k, i, True) for k in range(len(outs))])
        return carry

    lax.fori_loop(0, count, turn, 0)

    @pl.when(count >= 2)
    def _():
        wait_all([item_copy(outs, k, count - 2, True) for k in range(len(outs))])

    wait_all([item_copy(outs, k, count - 1, True) for k in range(len(outs))])


def native_copies(refs, bufs, sems):
    return [pltpu.make_async_copy(src, dst, sems.at[k]) for k, (src, dst) in enumerate(zip(refs, bufs))]


def fill_pool(own_ref, got_ref, pool, slots):
    rows = own_ref.shape[0]
    odd = lax.broadcasted_iota(jnp.int32, (rows, 128), 0) & 1
    for j in range(D // 128):
        cols = slice(128 * j, 128 * j + 128)
        pool[j, :rows] = jnp.where(odd == 0, own_ref[:, cols].astype(f32), got_ref[:, cols].astype(f32))
        pool[j, rows : TP * slots] = jnp.zeros((TP * slots - rows, 128), f32)


def read_rows(pool, at, slots):
    rows = pl.ds(at, TP, stride=slots)
    return jnp.concatenate([pool[j, rows, :] for j in range(D // 128)], axis=1)


def write_rows(pool, at, slots, value):
    rows = pl.ds(at, TP, stride=slots)
    for j in range(D // 128):
        pool[j, rows, :] = value[:, 128 * j : 128 * j + 128]


def fill_moved(x_ref, z_ref, pool, slots):
    for k, ref in enumerate((x_ref, z_ref)):
        for j in range(MOVED):
            write_rows(pool, TP * slots + k * MOVED + j, slots, ref[j].astype(f32))


def empty_pool(pool, slots, out_ref, x_ref, z_ref):
    for j in range(D // 128):
        out_ref[:, 128 * j : 128 * j + 128] = pool[j, : out_ref.shape[0]].astype(bf16)
    for k, ref in enumerate((x_ref, z_ref)):
        for j in range(MOVED):
            ref[j] = read_rows(pool, TP * slots + k * MOVED + j, slots).astype(bf16)


def fetch(n_ref, pieces, buf, sems):
    rows = pieces[0].shape[0]
    copies = []
    for k, piece in enumerate(pieces):
        at = pl.multiple_of((n_ref[ME] ^ k) * rows, 32)
        copies.append(pltpu.make_async_copy(piece, buf.at[pl.ds(at, rows)], sems.at[k]))
    return start_all(copies)


def finish(n_ref, acc, send_s, send_ref, keep_ref, pool, slots, natives, outs, sems):
    pairs, rows = send_s.shape[0], send_s.shape[1]
    me = n_ref[ME] & 1
    copies = []
    for y in range(pairs):
        mine = pl.multiple_of((2 * y + me) * rows, 32)
        copies.append(pltpu.make_async_copy(acc.at[pl.ds(mine, rows)], keep_ref.at[y], sems.at[y]))
    start_all(copies)
    for y in range(pairs):
        theirs = pl.multiple_of((2 * y + 1 - me) * rows, 32)
        send_s[y] = acc[pl.ds(theirs, rows), :].astype(bf16)
    copies += start_all([pltpu.make_async_copy(send_s, send_ref, sems.at[pairs])])
    out, x, z = natives
    empty_pool(pool, slots, out, x, z)
    copies += start_all([pltpu.make_async_copy(src, dst, sems.at[pairs + 1 + k]) for k, (src, dst) in enumerate(zip(natives, outs))])
    wait_all(copies)


def attn_fwd_kernel(parts, slots, n_ref, *rest):
    sources, pieces, rest = rest[:4], rest[4 : 4 + parts], rest[4 + parts :]
    hbm, vec_ref, w, pool, natives, (native_sems, w_sems) = rest[:4], rest[4], rest[5], rest[6], rest[7:11], rest[11:13]
    bufs, sems = rest[13:17], rest[17:]
    given = start_all(native_copies(sources, natives, native_sems))
    weights = fetch(n_ref, pieces, w, w_sems)
    wait_all(given)
    fill_pool(natives[0], natives[1], pool, slots)
    fill_moved(natives[2], natives[3], pool, slots)
    wait_all(weights)
    vec_ref[...] = w[:, 3 * D :].astype(f32).T[:16]

    def step(i, slot):
        x_ref, qkv_ref, o_ref, lse_ref = (v.at[slot] for v in bufs)
        x = read_rows(pool, first_row(n_ref, i, slots), slots)
        x_ref[...] = x.astype(bf16)
        n1, _ = norm(x)
        a = (n1 * vec_ref[0:1] + vec_ref[2:3]).astype(bf16)
        qb = jnp.concatenate([vec_ref[3:4], jnp.zeros((1, D), f32), vec_ref[4:5]], axis=1)
        qkv = (dot(a, w[:, : 3 * D]) + qb).astype(bf16)
        real = lax.broadcasted_iota(jnp.int32, (TP - TC, 3 * D), 0) < T - TC
        qkv_ref[:TC] = qkv[:TC]
        qkv_ref[TC:] = jnp.where(real, qkv[TC:], jnp.zeros_like(qkv[TC:]))
        lane = lax.broadcasted_iota(jnp.int32, (TP, 128), 1)
        low = lane < HD
        key = lax.broadcasted_iota(jnp.int32, (TP, TP), 1) < T
        lse = jnp.zeros((TP, 128), f32)
        for pair in range(H // 2):
            at = pair * 128
            q, k, v = (qkv_ref[:, off + at : off + at + 128] for off in (0, D, 2 * D))
            zero = jnp.zeros_like(q)
            o = None
            for side in range(2):
                sel = low if side == 0 else jnp.logical_not(low)
                s = jnp.where(key, dot_nt(jnp.where(sel, q, zero), k) * SCALE_LOG2E, -1e30)
                l2 = jnp.log2(jnp.sum(jnp.exp2(s), axis=-1, keepdims=True))
                p = jnp.exp2(s - l2).astype(bf16)
                part = dot(p, jnp.where(sel, v, zero))
                o = part if o is None else o + part
                lse = jnp.where(lane == pair * 2 + side, l2, lse)
            o_ref[:, at : at + 128] = o.astype(bf16)
        lse_ref[...] = lse

    stream(n_ref[N_ITEMS], (), tuple(zip(hbm, bufs, sems)), step)


FC = 256


def mlp_kernel(parts, slots, n_ref, xb_ref, ob_ref, *rest):
    sources, vec_ref, pieces, rest = rest[:4], rest[4], rest[5 : 5 + parts], rest[5 + parts :]
    dhb_ref, dob_ref, out_ref, ox_ref, oz_ref, send_ref, keep_ref, vb_ref = rest[:8]
    (w, acc, vg, gbu, cpool, opool, bu_s, c_s, dy_s, ct_s, dyt_s, zb, db, ub, eb, out_s, dc_s, send_s) = rest[8:26]
    natives, (native_sems, w_sems, out_sems), bufs, sems = rest[26:30], rest[30:33], rest[33:37], rest[37:]
    flow = tuple(zip((xb_ref, ob_ref, dhb_ref, dob_ref), bufs, sems))
    given = start_all(native_copies(sources, natives, native_sems))
    weights = fetch(n_ref, pieces, w, w_sems)
    first_items(flow[:2])
    acc[...] = jnp.zeros_like(acc)
    vg[...] = jnp.zeros_like(vg)
    gbu[...] = jnp.zeros_like(gbu)
    bu_s[...] = jnp.concatenate([vec_ref[8 + j : 9 + j] for j in range(F // D)], axis=1)
    wait_all(given)
    fill_pool(natives[0], natives[1], cpool, slots)
    fill_moved(natives[2], natives[3], cpool, slots)
    wait_all(weights)

    def step(i, slot):
        x_ref, o_ref, dh_ref, do_ref = (v.at[slot] for v in bufs)
        at = first_row(n_ref, i, slots)
        g2, b2, bo, bd = vec_ref[1:2], vec_ref[6:7], vec_ref[5:6], vec_ref[7:8]
        x = x_ref[...].astype(f32)
        o = o_ref[...]
        h = x + dot(o, w[:, :D]) + bo
        n2, r2 = norm(h)
        c = (n2 * g2 + b2).astype(bf16)
        dyf = read_rows(cpool, at, slots)
        dy = dyf.astype(bf16)
        steps = F // FC
        c_s[...] = c
        dy_s[...] = dy
        ct_s[...] = c.T
        dyt_s[...] = dy.T

        def cols(base, j):
            return slice(base + j * FC, base + j * FC + FC)

        def produce(j, slot):
            zb[slot] = dot(c_s[...], w[:, cols(D, j)])
            db[slot] = dot(dy_s[...], w[:, cols(D + F, j)])

        def middle(j, slot):
            u, slope = gelu_parts(zb[slot] + bu_s[:, cols(0, j)])
            dz = db[slot] * slope
            gbu[:, cols(0, j)] += col8(dz)
            ub[slot] = u.astype(bf16)
            eb[slot] = dz.astype(bf16)

        def consume(j, slot, first=False):
            u, dzb = ub[slot], eb[slot]
            o1, d1 = dot_nt(u, w[:, cols(D + F, j)]), dot_nt(dzb, w[:, cols(D, j)])
            out_s[...] = o1 if first else out_s[...] + o1
            dc_s[...] = d1 if first else dc_s[...] + d1
            acc[:, cols(D, j)] += dot(ct_s[...], dzb)
            acc[:, cols(D + F, j)] += dot(dyt_s[...], u)

        produce(0, 0)
        produce(1, 1)
        middle(0, 0)
        for j in range(1, steps):
            if j + 1 < steps:
                produce(j + 1, (j + 1) % 3)
            consume(j - 1, (j - 1) % 3, j == 1)
            middle(j, j % 3)
        consume(steps - 1, (steps - 1) % 3)
        out, dc = out_s[...], dc_s[...]
        write_rows(opool, at, slots, h + out + bd)
        dh = dyf + norm_back(dc * g2, n2, r2)
        dh_ref[...] = dh
        dhb = dh.astype(bf16)
        acc[:, :D] += dot(o.T, dhb)
        do_ref[...] = dot_nt(dhb, w[:, :D]).astype(bf16)
        vg[0:8] += col8(dc * n2)
        vg[8:16] += col8(dh)
        vg[16:24] += col8(dc)
        vg[24:32] += col8(dyf)

    stream(n_ref[N_ITEMS], flow[:2], flow[2:], step)
    rows = [total(vg[8 * k : 8 * k + 8]) for k in range(4)]
    rows += [total(gbu[:, k * D : (k + 1) * D]) for k in range(F // D)]
    vb_ref[...] = jnp.concatenate(rows, axis=0)
    finish(n_ref, acc, send_s, send_ref, keep_ref, opool, slots, (natives[0], natives[2], natives[3]),
           (out_ref, ox_ref, oz_ref), out_sems)


def attn_bwd_kernel(parts, slots, n_ref, xb_ref, qkvb_ref, lseb_ref, dob_ref, dhb_ref, vec_ref, vb_ref, *rest):
    pieces, rest = rest[:parts], rest[parts:]
    out_ref, ox_ref, oz_ref, send_ref, keep_ref, w, acc, vg, dqkv, opool, sb, db, pb, gb, tb, send_s = rest[:16]
    natives, (w_sems, out_sems), bufs, sems = rest[16:19], rest[19:21], rest[21:26], rest[26:]
    flow = tuple(zip((xb_ref, qkvb_ref, lseb_ref, dob_ref, dhb_ref), bufs, sems))
    first_items(flow)
    weights = fetch(n_ref, pieces, w, w_sems)
    acc[...] = jnp.zeros_like(acc)
    vg[...] = jnp.zeros_like(vg)
    wait_all(weights)

    def step(i, slot):
        x_ref, qkv_ref, lse_ref, do_ref, dh_ref = (v.at[slot] for v in bufs)
        g1, b1 = vec_ref[0:1], vec_ref[2:3]
        x = x_ref[...].astype(f32)
        n1, r1 = norm(x)
        at_ = (n1 * g1 + b1).astype(bf16).T
        low = lax.broadcasted_iota(jnp.int32, (TP, 128), 1) < HD
        real = lax.broadcasted_iota(jnp.int32, (TP - TC, 128), 0) < T - TC

        def mask(h, v):
            return jnp.where(low if h % 2 == 0 else jnp.logical_not(low), v, jnp.zeros_like(v))

        def lanes(h, off=0):
            return slice(off + (h // 2) * 128, off + (h // 2) * 128 + 128)

        def produce(h):
            sb[h % 3] = dot_nt(mask(h, qkv_ref[:, lanes(h)]), qkv_ref[:, lanes(h, D)])
            db[h % 3] = dot_nt(mask(h, do_ref[:, lanes(h)]), qkv_ref[:, lanes(h, 2 * D)])

        def middle(h):
            p = jnp.exp2(sb[h % 3] * SCALE_LOG2E - lse_ref[:, h : h + 1])
            dp = db[h % 3]
            pb[h % 2] = p.astype(bf16)
            delta = jnp.sum(p * dp, axis=-1, keepdims=True)
            gb[h % 2] = (p * (dp - delta) * SCALE).astype(bf16)

        def consume(h):
            ds = gb[h % 2]
            part = (dot(ds, mask(h, qkv_ref[:, lanes(h, D)])),
                    dot_tn(ds, mask(h, qkv_ref[:, lanes(h)])),
                    dot_tn(pb[h % 2], mask(h, do_ref[:, lanes(h)])))
            if h % 2 == 0:
                for k in range(3):
                    tb[k] = part[k]
                return
            dq, dk, dv = (tb[k] + part[k] for k in range(3))
            dqkv[:, lanes(h)] = dq.astype(bf16)
            for v, off in ((dk, D), (dv, 2 * D)):
                v_b = v.astype(bf16)
                dqkv[:TC, lanes(h, off)] = v_b[:TC]
                dqkv[TC:, lanes(h, off)] = jnp.where(real, v_b[TC:], jnp.zeros_like(v_b[TC:]))
            vg[16:24, lanes(h)] += col8(dq)
            vg[24:32, lanes(h)] += col8(dv[:TC]) + col8(jnp.where(real, dv[TC:], 0.0))

        produce(0)
        produce(1)
        middle(0)
        for h in range(1, H):
            if h + 1 < H:
                produce(h + 1)
            consume(h - 1)
            middle(h)
        consume(H - 1)
        dqkv_b = dqkv[...]
        acc[:, : 3 * D] += dot(at_, dqkv_b)
        da = dot_nt(dqkv_b, w[:, : 3 * D])
        write_rows(opool, first_row(n_ref, i, slots), slots, dh_ref[...] + norm_back(da * g1, n1, r1))
        vg[0:8] += col8(da * n1)
        vg[8:16] += col8(da)

    stream(n_ref[N_ITEMS], flow, (), step)
    mine = [total(vg[8 * k : 8 * k + 8]) for k in range(4)]
    vb = vb_ref[...]
    rows = jnp.concatenate([mine[0], vb[0:1], mine[1], mine[2], mine[3], vb[1:8], jnp.zeros((116, D), f32)], axis=0)
    acc[:, 3 * D :] = rows.T
    finish(n_ref, acc, send_s, send_ref, keep_ref, opool, slots, natives, (out_ref, ox_ref, oz_ref), out_sems)


def once(shape):
    return pl.BlockSpec(shape, lambda i, *n: (0,) * len(shape), pipeline_mode=pl.Buffered(1))


PLAN = pltpu.SMEM((12,), jnp.int32)


def planned(kernel):
    def run(*refs):
        make_plan(*refs[:5], refs[-1])
        kernel(refs[-1], *refs[5:-1])

    return run


def layer_call(kernel, n, slots, streams, ins, pieces, left, outs, scratch, sems, flow, flops):
    parts = len(pieces)
    items = [S((slots + 2 * MOVED,) + v.shape, v.dtype) for v in flow[len(streams):]]
    return pl.pallas_call(
        planned(lambda *refs: kernel(parts, slots, *refs)),
        out_shape=tuple(items) + tuple(left) + tuple(outs),
        grid_spec=pltpu.PrefetchScalarGridSpec(
            num_scalar_prefetch=5, grid=(1,),
            in_specs=[ANY] * len(streams) + [once(v.shape) if v.size <= 16 * D else ANY for v in ins] + [ANY] * parts,
            out_specs=tuple([ANY] * (len(items) + len(left)) + [once(v.shape) for v in outs]),
            scratch_shapes=list(scratch) + [pltpu.SemaphoreType.DMA((k,)) for k in sems]
            + [pltpu.VMEM((2,) + v.shape, v.dtype) for v in flow] + [pltpu.SemaphoreType.DMA((2,)) for _ in flow]
            + [PLAN]),
        compiler_params=pltpu.CompilerParams(
            dimension_semantics=("arbitrary",), vmem_limit_bytes=VMEM_LIMIT),
        cost_estimate=pl.CostEstimate(flops=flops, bytes_accessed=20_000_000, transcendentals=0))(*n, *streams, *ins, *pieces)


FEW = S((MOVED, TP, D), bf16)
WIDE = S((TP, D), f32)
SLIM = S((TP, D), bf16)
QKV = S((TP, 3 * D), bf16)
LSE = S((TP, 128), f32)


def pool_of(slots):
    return pltpu.VMEM((D // 128, 2 * TP * slots, 128), f32)


def reduced(parts, cols):
    shape = (parts // 2, D // parts, cols)
    return S(shape, bf16), S(shape, f32)


def vmem(v):
    return pltpu.VMEM(v.shape, v.dtype)


def attn_fwd(n, slots, own, got, x, z, pieces):
    native = S(own.shape, bf16)
    return layer_call(
        attn_fwd_kernel, n, slots, (), (own, got, x, z), pieces, (), (S((16, D), f32),),
        (pltpu.VMEM((D, Q_COLS), bf16), pool_of(slots)) + tuple(vmem(v) for v in (native, native, FEW, FEW)),
        (4, len(pieces)), (SLIM, QKV, SLIM, LSE), 10_000_000_000)


def mlp(n, slots, x, o, c_own, c_got, c_x, c_z, vec, pieces):
    native, sums = S(c_own.shape, bf16), reduced(len(pieces), R_COLS)
    return layer_call(
        mlp_kernel, n, slots, (x, o), (c_own, c_got, c_x, c_z, vec), pieces, (native, FEW, FEW) + sums, (S((8, D), f32),),
        (pltpu.VMEM((D, R_COLS), bf16), pltpu.VMEM((D, R_COLS), f32), pltpu.VMEM((32, D), f32),
         pltpu.VMEM((8, F), f32), pool_of(slots), pool_of(slots),
         pltpu.VMEM((1, F), f32), pltpu.VMEM((TP, D), bf16), pltpu.VMEM((TP, D), bf16), pltpu.VMEM((D, TP), bf16),
         pltpu.VMEM((D, TP), bf16), pltpu.VMEM((3, TP, FC), f32), pltpu.VMEM((3, TP, FC), f32),
         pltpu.VMEM((3, TP, FC), bf16), pltpu.VMEM((3, TP, FC), bf16), pltpu.VMEM((TP, D), f32),
         pltpu.VMEM((TP, D), f32), vmem(sums[0])) + tuple(vmem(v) for v in (native, native, FEW, FEW)),
        (4, len(pieces), len(pieces) // 2 + 4), (SLIM, SLIM, WIDE, SLIM), 25_000_000_000)


def attn_bwd(n, slots, x, qkv, lse, do, dh, vec, vb, pieces, rows):
    native, sums = S((rows, D), bf16), reduced(len(pieces), Q_COLS)
    return layer_call(
        attn_bwd_kernel, n, slots, (x, qkv, lse, do, dh), (vec, vb), pieces, (native, FEW, FEW) + sums, (),
        (pltpu.VMEM((D, Q_COLS), bf16), pltpu.VMEM((D, Q_COLS), f32), pltpu.VMEM((32, D), f32),
         pltpu.VMEM((TP, 3 * D), bf16), pool_of(slots), pltpu.VMEM((3, TP, TP), f32),
         pltpu.VMEM((3, TP, TP), f32), pltpu.VMEM((2, TP, TP), bf16), pltpu.VMEM((2, TP, TP), bf16),
         pltpu.VMEM((3, TP, 128), f32), vmem(sums[0])) + tuple(vmem(v) for v in (native, FEW, FEW)),
        (len(pieces), len(pieces) // 2 + 4), (SLIM, QKV, LSE, SLIM, WIDE), 20_000_000_000)


def pack_first_kernel(w_ref, g_ref, b_ref, o_ref):
    rows = w_ref.shape[0]
    vec = jnp.concatenate([g_ref[...], b_ref[...], jnp.zeros((128 - NV, rows), f32)], axis=0)
    o_ref[:, : 3 * D] = w_ref[...].astype(bf16)
    o_ref[:, 3 * D :] = vec.T.astype(bf16)


def pack_rest_kernel(p_ref, a_ref, b_ref, o_ref):
    o_ref[:, :D] = p_ref[...].astype(bf16)
    o_ref[:, D : D + F] = a_ref[...].astype(bf16)
    o_ref[:, D + F : D + 2 * F] = b_ref[...].astype(bf16)
    o_ref[:, D + 2 * F :] = jnp.zeros((o_ref.shape[0], R_COLS - D - 2 * F), bf16)


def split3(a):
    hi = a.astype(bf16)
    return hi, (a - hi.astype(f32)).astype(bf16)


def dot3(a, b):
    return dot(jnp.concatenate([a[0], a[1], a[0]], axis=1), jnp.concatenate([b[0], b[0], b[1]], axis=0))


def dot3_sym(a, b):
    left = jnp.concatenate([a[0], a[1], a[0]], axis=1)
    right = jnp.concatenate([b[0], b[0], b[1]], axis=0)
    wide = dot(left, right[:, :256])
    corner = dot(left[256:], right[:, 256:])
    return jnp.concatenate([wide, jnp.concatenate([wide[256:].T, corner], axis=0)], axis=1)


def orth_rows(m, q_s, at, rows):
    a = dot_nt(m, m)
    diag = lax.broadcasted_iota(jnp.int32, (D, D), 0) == lax.broadcasted_iota(jnp.int32, (D, D), 1)
    ssq = jnp.sum(jnp.where(diag, a, 0.0), axis=(0, 1), keepdims=True)
    s = 1.0 / (jnp.sqrt(ssq) + ORTHO_EPSILON)
    a = a * (s * s)
    eye = jnp.where(diag, COEFF_FIRST, 0.0)
    q = None
    for k in range(NS_ITERS - 1):
        a_s = split3(a)
        p = eye + COEFF_SECOND * a + COEFF_THIRD * dot3_sym(a_s, a_s)
        p_s = split3(p)
        if k == 0:
            q_s[...] = p
            q = q_s[pl.ds(at, rows), :]
        else:
            q = dot3(split3(q), p_s)
        if k < NS_ITERS - 2:
            a = dot3_sym(split3(dot3_sym(p_s, a_s)), p_s)

    def times_last(v):
        return dot3(split3(dot3(split3(dot3(split3(v), p_s)), a_s)), p_s)

    qa = times_last(q)
    q = COEFF_FIRST * q + COEFF_SECOND * qa + COEFF_THIRD * times_last(qa)
    hi, lo = split3(q * s)
    return dot(hi, m) + dot(lo, m)


def fetch_cols(n_ref, pieces, buf, sems, at_col, cols):
    rows = pieces[0].shape[0]
    copies = []
    for k, piece in enumerate(pieces):
        at = pl.multiple_of((n_ref[0] ^ k) * rows, 32)
        copies.append(pltpu.make_async_copy(
            piece.at[:, pl.ds(at_col, cols)], buf.at[pl.ds(at, rows), pl.ds(0, cols)], sems.at[k]))
    for c in copies:
        c.start()
    for c in copies:
        c.wait()


def orth_both(n_ref, mine_ref, theirs_ref, m, q_s, o_s):
    rows = mine_ref.shape[0]
    core = n_ref[0] & 1
    at = pl.multiple_of((n_ref[0] - core) * rows, 32)
    o_s[...] = orth_rows(m[...], q_s, at, 2 * rows)
    mine_ref[...] = o_s[pl.ds(pl.multiple_of(core * rows, 32), rows), :]
    theirs_ref[...] = o_s[pl.ds(pl.multiple_of((1 - core) * rows, 32), rows), :]


def orth_mlp_kernel(parts, n_ref, *rest):
    pieces = rest[:parts]
    mine_ref, theirs_ref, m, q_s, o_s, sems = rest[parts:]
    fetch_cols(n_ref, pieces, m, sems, pl.multiple_of((n_ref[0] & 1) * F, 128), F)
    orth_both(n_ref, mine_ref, theirs_ref, m, q_s, o_s)


def orth_attn_kernel(parts, n_ref, *rest):
    pieces = rest[:parts]
    mine_ref, theirs_ref, m, q_s, o_s, sems = rest[parts:]

    @pl.when(n_ref[0] & 1 == 0)
    def _():
        fetch_cols(n_ref, pieces, m, sems, 0, 3 * D)

    @pl.when(n_ref[0] & 1 == 1)
    def _():
        m[:, D:] = jnp.zeros((D, 2 * D), bf16)
        fetch_cols(n_ref, pieces, m, sems, 3 * D, D)

    orth_both(n_ref, mine_ref, theirs_ref, m, q_s, o_s)


def orth_call(kernel, me, pieces, cols):
    parts = len(pieces)
    rows = pieces[0].shape[0]
    spec = pl.BlockSpec((rows, cols), lambda i, n: (0, 0))
    return pl.pallas_call(
        lambda *refs: kernel(parts, *refs),
        out_shape=(S((rows, cols), f32),) * 2,
        grid_spec=pltpu.PrefetchScalarGridSpec(
            num_scalar_prefetch=1, grid=(1,), in_specs=[ANY] * parts, out_specs=(spec,) * 2,
            scratch_shapes=[pltpu.VMEM((D, cols), bf16), pltpu.VMEM((D, D), f32), pltpu.VMEM((2 * rows, cols), f32),
                            pltpu.SemaphoreType.DMA((parts,))]),
        compiler_params=pltpu.CompilerParams(vmem_limit_bytes=VMEM_LIMIT),
        cost_estimate=pl.CostEstimate(flops=8_000_000_000, bytes_accessed=4_000_000, transcendentals=0))(me, *pieces)


def swap(v, axis, k):
    return lax.ppermute(v, axis, [(i, i ^ k) for i in range(lax.axis_size(axis))])


def bits(axis):
    return range(lax.axis_size(axis).bit_length() - 1)


def bit(axis, b):
    return (lax.axis_index(axis) >> b) & 1


def all_pieces(v, axis):
    pieces = {0: v}
    for b in reversed(bits(axis)):
        pieces.update({k ^ (1 << b): swap(p, axis, 1 << b) for k, p in list(pieces.items())})
    return [pieces[k] for k in range(lax.axis_size(axis))]


def take(v, i):
    return lax.dynamic_index_in_dim(v, i, 0, keepdims=False)


def sum_blocks(send, keep):
    got = swap(send, "fsdp", 1)
    keep, got = (v.reshape((2, -1) + v.shape[1:]) for v in (keep, got))
    for b in reversed(bits("fsdp")[1:]):
        me = bit("fsdp", b)
        sent = (take(keep, 1 - me) + take(got, 1 - me).astype(f32)).astype(bf16)
        own = take(keep, me) + take(got, me).astype(f32)
        got = swap(sent, "fsdp", 1 << b)
        keep = own
        if keep.shape[0] > 1:
            keep, got = (v.reshape((2, -1) + v.shape[1:]) for v in (keep, got))
    return (keep + got.astype(f32)).reshape(keep.shape[-2:])


def halves(v, axis):
    n = v.shape[axis] // 2
    return lax.slice_in_dim(v, 0, n, axis=axis), lax.slice_in_dim(v, n, 2 * n, axis=axis)


def sum_groups(v):
    for b in bits("rep"):
        me = bit("rep", b)
        lo, hi = halves(v, 1 if b == 0 else 0)
        got = swap(jnp.where(me == 0, hi, lo).astype(bf16), "rep", 1 << b)
        v = jnp.where(me == 0, lo, hi) + got.astype(f32)
    v = v.astype(bf16)
    for b in reversed(bits("rep")):
        me = bit("rep", b)
        got = swap(v, "rep", 1 << b)
        v = jnp.concatenate([jnp.where(me == 0, v, got), jnp.where(me == 0, got, v)], axis=1 if b == 0 else 0)
    return v


def sum_groups_whole(v):
    v = v.astype(bf16)
    for b in bits("rep"):
        got = swap(v, "rep", 1 << b)
        v = (v.astype(f32) + got.astype(f32)).astype(bf16)
    return v


def pick_kernel(slots, count_ref, a_ref, b_ref, ax_ref, az_ref, bx_ref, bz_ref, pool):
    for ref, x_ref, z_ref in ((a_ref, ax_ref, az_ref), (b_ref, bx_ref, bz_ref)):
        fill_pool(ref, ref, pool, slots)
        for j in range(MOVED):
            x_ref[j] = read_rows(pool, jnp.maximum(count_ref[0] - 1 - j, 0), slots).astype(bf16)
            z_ref[j] = read_rows(pool, jnp.maximum(count_ref[0] - MOVED - 1 - j, 0), slots).astype(bf16)


def pool_call(kernel, scalars, slots, ins, outs, scratch):
    return pl.pallas_call(
        kernel, out_shape=outs,
        grid_spec=pltpu.PrefetchScalarGridSpec(
            num_scalar_prefetch=len(scalars), grid=(1,), in_specs=[once(v.shape) for v in ins],
            out_specs=tuple(once(v.shape) for v in outs),
            scratch_shapes=[pltpu.VMEM((D // 128, TP * slots, 128), f32)] + list(scratch)),
        compiler_params=pltpu.CompilerParams(vmem_limit_bytes=VMEM_LIMIT),
        cost_estimate=pl.CostEstimate(flops=1_000_000, bytes_accessed=7_000_000, transcendentals=0))(*scalars, *ins)


def unpool_kernel(slots, n_ref, own_ref, got_ref, x_ref, z_ref, o_ref, pool):
    fill_pool(own_ref, got_ref, pool, slots)
    for j in range(MOVED):
        for ref, given, at in ((x_ref, TO_X, 1), (z_ref, TO_Z, MOVED + 1)):
            @pl.when(j < n_ref[given])
            def _(ref=ref, at=at):
                write_rows(pool, n_ref[COUNT] - at - j, slots, ref[j].astype(f32))
    rows = o_ref.shape[0]
    live = (lax.broadcasted_iota(jnp.int32, (rows, 128), 0) & (slots - 1)) < n_ref[COUNT]
    for j in range(D // 128):
        o_ref[:, 128 * j : 128 * j + 128] = jnp.where(live, pool[j, :rows], 0.0).astype(bf16)


def adam_kernel(scale, g_ref, *refs):
    ins, outs = refs[:6], refs[6:]
    g = (g_ref[...].astype(f32) * scale).T
    for k, (lo, hi) in enumerate(((0, 2), (2, NV))):
        gradient, parameter = g[lo:hi], ins[k][...]
        first = ADAM_FIRST * ins[2 + 2 * k][...] + (1.0 - ADAM_FIRST) * gradient
        second = ADAM_SECOND * ins[3 + 2 * k][...] + (1.0 - ADAM_SECOND) * gradient * gradient
        first_hat = first / (1.0 - ADAM_FIRST**ADAM_STEP)
        second_hat = second / (1.0 - ADAM_SECOND**ADAM_STEP)
        outs[k][...] = gradient
        outs[2 + k][...] = parameter - ADAM_RATE * (
            first_hat / (jnp.sqrt(second_hat) + ADAM_EPSILON) + ADAM_DECAY * parameter)
        outs[4 + 2 * k][...] = first
        outs[5 + 2 * k][...] = second


def adam(last, devices, *states):
    full = [pl.BlockSpec(v.shape, lambda i: (0, 0)) for v in states]
    one, two = S(states[0].shape, f32), S(states[1].shape, f32)
    return pl.pallas_call(
        lambda *refs: adam_kernel(1.0 / devices, *refs),
        grid=(1,), out_shape=(one, two, one, two, one, one, two, two),
        in_specs=[pl.BlockSpec((last.shape[0], 128), lambda i: (0, 3 * D // 128))] + full,
        out_specs=tuple(full[k] for k in (0, 1, 0, 1, 2, 3, 4, 5)), name="adam")(last, *states)


def muon_factor(row_total, column_total):
    return math.sqrt(max(1.0, row_total / column_total))


def body(images, cotangent, counts, w_qkv, w_proj, w_fc1, w_fc2, gains, biases,
         mom_qkv, mom_proj, mom_fc1, mom_fc2, gains_first, gains_second, biases_first, biases_second):
    slots = images.shape[0]
    rows = w_qkv.shape[0]
    devices = lax.axis_size("rep") * lax.axis_size("fsdp")
    me = lax.axis_index("fsdp").astype(jnp.int32)

    first = pl.pallas_call(pack_first_kernel, out_shape=S((rows, Q_COLS), bf16), name="pack_first")(w_qkv, gains, biases)
    q_pieces = all_pieces(first, "fsdp")

    pair = jnp.concatenate([counts, swap(counts, "fsdp", 1)])
    n = (me.reshape(1), pair) + tuple(swap(pair, "rep", k) for k in (1, 2, 3))

    own = [v.transpose(1, 0, 2).reshape(-1, D) for v in (images, cotangent)]
    offers = pool_call(lambda *refs: pick_kernel(slots, *refs), (counts,), slots, own, (FEW,) * 4, ())

    def spread(v, to_x, to_z):
        return v, swap(v, "fsdp", 1), swap(to_x, "rep", 1), swap(to_z, "rep", 2)

    x_in = spread(own[0], *offers[:2])
    c_in = spread(own[1], *offers[2:])

    def unpool(v, to_x, to_z):
        ins = (v, swap(v, "fsdp", 1), swap(to_x, "rep", 1), swap(to_z, "rep", 2))
        (full,) = pool_call(planned(lambda *refs: unpool_kernel(slots, *refs)), n, slots, ins, (S(v.shape, bf16),), (PLAN,))
        return full.reshape(-1, slots, D).transpose(1, 0, 2)

    rest = pl.pallas_call(pack_rest_kernel, out_shape=S((rows, R_COLS), bf16), name="pack_rest")(w_proj, w_fc1, w_fc2.T)
    r_pieces = all_pieces(rest, "fsdp")

    x, qkv, o, lse, vec = attn_fwd(n, slots, *x_in, q_pieces)
    dh, do, *out, r_send, r_keep, vb = mlp(n, slots, x, o, *c_in, vec, r_pieces)
    mid = sum_blocks(r_send, r_keep)
    *in_grad, q_send, q_keep = attn_bwd(n, slots, x, qkv, lse, do, dh, vec, vb, q_pieces, x_in[0].shape[0])
    mid = sum_groups(mid)
    last = sum_groups_whole(sum_blocks(q_send, q_keep))
    block_out = unpool(*out)
    input_grad = unpool(*in_grad)

    vectors = adam(last, devices, gains, biases, gains_first, gains_second, biases_first, biases_second)
    scale = 1.0 / devices
    grad_qkv = last[:, : 3 * D].astype(f32) * scale
    grad_proj, grad_fc1, grad_fc2t = (
        mid[:, lo:hi].astype(f32) * scale for lo, hi in ((0, D), (D, D + F), (D + F, D + 2 * F)))
    next_qkv = MUON_MOMENTUM * mom_qkv + grad_qkv
    next_proj = MUON_MOMENTUM * mom_proj + grad_proj
    next_fc1 = MUON_MOMENTUM * mom_fc1 + grad_fc1
    next_fc2t = MUON_MOMENTUM * mom_fc2.T + grad_fc2t
    attn_pieces = all_pieces(jnp.concatenate([next_qkv.astype(bf16), next_proj.astype(bf16)], axis=1), "fsdp")
    mlp_pieces = all_pieces(jnp.concatenate([next_fc1.astype(bf16), next_fc2t.astype(bf16)], axis=1), "fsdp")

    core = me & 1
    mine, theirs = orth_call(orth_attn_kernel, me.reshape(1), attn_pieces, 3 * D)
    got = swap(theirs, "fsdp", 1)
    orth_qkv, orth_proj = jnp.where(core == 0, mine, got), jnp.where(core == 0, got, mine)[:, :D]
    mine, theirs = orth_call(orth_mlp_kernel, me.reshape(1), mlp_pieces, F)
    got = swap(theirs, "fsdp", 1)
    orth_fc1, orth_fc2t = jnp.where(core == 0, mine, got), jnp.where(core == 0, got, mine)
    new_qkv = w_qkv - MUON_RATE * muon_factor(D, 3 * D) * orth_qkv
    new_proj = w_proj - MUON_RATE * muon_factor(D, D) * orth_proj
    new_fc1 = w_fc1 - MUON_RATE * muon_factor(D, F) * orth_fc1
    new_fc2t = w_fc2.T - MUON_RATE * muon_factor(F, D) * orth_fc2t
    grad_gains, grad_biases, new_gains, new_biases = vectors[:4]
    return (block_out, input_grad, grad_qkv, grad_proj, grad_fc1, grad_fc2t.T, grad_gains, grad_biases,
            new_qkv, new_proj, new_fc1, new_fc2t.T, new_gains, new_biases,
            next_qkv, next_proj, next_fc1, next_fc2t.T) + tuple(vectors[4:])


def solution(mesh):
    in_specs = (
        P(("rep", "fsdp"), None, None),
        P(("rep", "fsdp"), None, None),
        P(("rep", "fsdp")),
        P("fsdp", None),
        P("fsdp", None),
        P("fsdp", None),
        P(None, "fsdp"),
        P(None, "fsdp"),
        P(None, "fsdp"),
        P("fsdp", None),
        P("fsdp", None),
        P("fsdp", None),
        P(None, "fsdp"),
        P(None, "fsdp"),
        P(None, "fsdp"),
        P(None, "fsdp"),
        P(None, "fsdp"),
    )
    out_specs = (
        P(("rep", "fsdp"), None, None),
        P(("rep", "fsdp"), None, None),
        P("fsdp", None),
        P("fsdp", None),
        P("fsdp", None),
        P(None, "fsdp"),
        P(None, "fsdp"),
        P(None, "fsdp"),
        P("fsdp", None),
        P("fsdp", None),
        P("fsdp", None),
        P(None, "fsdp"),
        P(None, "fsdp"),
        P(None, "fsdp"),
        P("fsdp", None),
        P("fsdp", None),
        P("fsdp", None),
        P(None, "fsdp"),
        P(None, "fsdp"),
        P(None, "fsdp"),
        P(None, "fsdp"),
        P(None, "fsdp"),
    )
    return jax.shard_map(body, mesh=mesh, in_specs=in_specs, out_specs=out_specs, check_vma=False)
```

```python
import math

import jax
import jax.numpy as jnp
from jax import lax
from jax.experimental import pallas as pl
from jax.experimental.pallas import tpu as pltpu
from jax.sharding import PartitionSpec as P


NS_ITERS = 5
ADAM_STEP = 3
ORTHO_EPSILON = 1e-07
COEFF_FIRST = 3.4445
COEFF_SECOND = -4.775
COEFF_THIRD = 2.0315
MUON_RATE = 0.3
MUON_MOMENTUM = 0.95
ADAM_RATE = 0.2
ADAM_FIRST = 0.9
ADAM_SECOND = 0.95
ADAM_EPSILON = 1e-08
ADAM_DECAY = 0.25

D = 384
H = 6
HD = 64
F = 1536
T = 197
TP = 208
TC = T // 16 * 16
EPS = 1e-6
NV = 12
Q_COLS = 3 * D + 128
R_COLS = D + 2 * F + 128
f32 = jnp.float32
bf16 = jnp.bfloat16
SCALE = 1.0 / math.sqrt(HD)
SCALE_LOG2E = SCALE * math.log2(math.e)
VMEM_LIMIT = 60 * 1024 * 1024
S = jax.ShapeDtypeStruct
ANY = pl.BlockSpec(memory_space=pl.ANY)


def dot(a, b):
    return jnp.dot(a, b, preferred_element_type=f32)


def dot_nt(a, b):
    return lax.dot_general(a, b, (((1,), (1,)), ((), ())), preferred_element_type=f32)


def norm(x):
    xc = x - jnp.mean(x, axis=-1, keepdims=True)
    r = lax.rsqrt(jnp.mean(xc * xc, axis=-1, keepdims=True) + EPS)
    return xc * r, r


def norm_back(e, n, r):
    return r * (e - jnp.mean(e, axis=-1, keepdims=True) - n * jnp.mean(e * n, axis=-1, keepdims=True))


def col8(v):
    return jnp.sum(v.reshape(v.shape[0] // 8, 8, v.shape[1]), axis=0)


def total(v):
    return jnp.sum(v, axis=0, keepdims=True)


PHI_T = 0.28
PHI_C = (0.11652077999788102, 0.06749674653879187, 0.2689101818992952,
         -0.2369935012534717, 0.38987403003604115, -0.10580824648054844)
HALF_LOG2E = -0.5 * math.log2(math.e)
DENSITY = 1.0 / math.sqrt(2.0 * math.pi)


def gelu_parts(z):
    t = 1.0 / (1.0 + PHI_T * jnp.abs(z))
    bell = jnp.exp2((z * z) * HALF_LOG2E)
    poly = PHI_C[5] * t + PHI_C[4]
    for k in (3, 2, 1, 0):
        poly = poly * t + PHI_C[k]
    tail = (poly * t) * bell
    cdf = jnp.where(z < 0.0, tail, 1.0 - tail)
    return z * cdf, cdf + (z * DENSITY) * bell


MOVED = 2
N_ITEMS, N_OWN, ME, N_POOL, OWN_GAP, OWN_JUMP, GOT_GAP, GOT_JUMP, FROM_X, TO_X, TO_Z, COUNT = range(12)


def make_plan(me_ref, *refs):
    v, o_ref = [ref[k] for ref in refs[:4] for k in range(2)], refs[4]
    core = me_ref[0] & 1
    loads = [v[2 * k] + v[2 * k + 1] for k in range(4)]

    def flow(a, b):
        return jnp.minimum((a - b) >> 1, 2 * MOVED), jnp.minimum((b - a) >> 1, 2 * MOVED)

    def share(amount, spare, k):
        return jnp.clip(jnp.minimum((amount + 1 - k) >> 1, spare), 0, MOVED)

    def both(amount, pair, kept):
        return [share(amount, c - kept, k) for c, k in zip(pair, (core, 1 - core))]

    def edge(a, b, load_a, load_b, kept):
        out, back = flow(load_a, load_b)
        s, r = both(out, a, kept), both(back, b, kept)
        return s, r, load_a + r[0] + r[1] - s[0] - s[1], load_b + s[0] + s[1] - r[0] - r[1]

    sx, rx, load, _ = edge(v[0:2], v[2:4], loads[0], loads[1], 1)
    _, _, load_z, _ = edge(v[4:6], v[6:8], loads[2], loads[3], 1)
    sz, rz, _, _ = edge(v[0:2], v[4:6], load, load_z, MOVED + 1)

    def kept(c, x, z, odd):
        hi = jnp.maximum(c - MOVED, 0)
        below, jump, top = ((t + 1 - odd) >> 1 for t in (hi - z, hi, c - x))
        return below + jnp.maximum(top - jump, 0), below, jump

    n_own, own_gap, own_jump = kept(v[0], sx[0], sz[0], 0)
    n_got, got_gap, got_jump = kept(v[1], sx[1], sz[1], 1)
    for k, value in enumerate((n_own + n_got + rx[0] + rz[0], n_own, me_ref[0], n_own + n_got, own_gap, own_jump,
                               got_gap, got_jump, rx[0], sx[0], sz[0], v[0])):
        o_ref[k] = value


def first_row(n_ref, i, slots):
    j, k = i - n_ref[N_OWN], i - n_ref[N_POOL]
    own = 2 * jnp.where(i < n_ref[OWN_GAP], i, i - n_ref[OWN_GAP] + n_ref[OWN_JUMP])
    got = 2 * jnp.where(j < n_ref[GOT_GAP], j, j - n_ref[GOT_GAP] + n_ref[GOT_JUMP]) + 1
    moved = TP * slots + jnp.where(k < n_ref[FROM_X], k, k - n_ref[FROM_X] + MOVED)
    return jnp.where(j < 0, own, jnp.where(k < 0, got, moved))


def item_copy(flow, k, i, out=False):
    ref, buf, sem = flow[k]
    here, there = buf.at[i & 1], ref.at[i]
    return pltpu.make_async_copy(here, there, sem.at[i & 1]) if out else pltpu.make_async_copy(there, here, sem.at[i & 1])


def start_all(copies):
    for c in copies:
        c.start()
    return copies


def wait_all(copies):
    for c in copies:
        c.wait()


def first_items(ins):
    return start_all([item_copy(ins, k, 0) for k in range(len(ins))])


def stream(count, ins, outs, body):
    def turn(i, carry):
        @pl.when(i + 1 < count)
        def _():
            start_all([item_copy(ins, k, i + 1) for k in range(len(ins))])

        wait_all([item_copy(ins, k, i) for k in range(len(ins))])

        @pl.when(i >= 2)
        def _():
            wait_all([item_copy(outs, k, i - 2, True) for k in range(len(outs))])

        body(i, i & 1)
        start_all([item_copy(outs, k, i, True) for k in range(len(outs))])
        return carry

    lax.fori_loop(0, count, turn, 0)

    @pl.when(count >= 2)
    def _():
        wait_all([item_copy(outs, k, count - 2, True) for k in range(len(outs))])

    wait_all([item_copy(outs, k, count - 1, True) for k in range(len(outs))])


def native_copies(refs, bufs, sems):
    return [pltpu.make_async_copy(src, dst, sems.at[k]) for k, (src, dst) in enumerate(zip(refs, bufs))]


def by_rows(rows, step, body):
    def turn(k, carry):
        body(pl.multiple_of(k * step, 16), step)
        return carry

    lax.fori_loop(0, rows // step, turn, 0)
    if rows % step:
        body(rows - rows % step, rows % step)


def clear(ref):
    def part(at, rows):
        ref[pl.ds(at, rows), :] = jnp.zeros((rows, ref.shape[1]), ref.dtype)

    by_rows(ref.shape[0], 16, part)


def fill_pool(own_ref, got_ref, pool, slots):
    rows = own_ref.shape[0]

    def part(at, count):
        odd = lax.broadcasted_iota(jnp.int32, (count, 128), 0) & 1
        for j in range(D // 128):
            own, got = (ref[pl.ds(at, count), 128 * j : 128 * j + 128].astype(f32) for ref in (own_ref, got_ref))
            pool[j, pl.ds(at, count)] = jnp.where(odd == 0, own, got)

    by_rows(rows, TP, part)
    for j in range(D // 128):
        pool[j, rows : TP * slots] = jnp.zeros((TP * slots - rows, 128), f32)


def read_rows(pool, at, slots):
    rows = pl.ds(at, TP, stride=slots)
    return jnp.concatenate([pool[j, rows, :] for j in range(D // 128)], axis=1)


def write_rows(pool, at, slots, value):
    rows = pl.ds(at, TP, stride=slots)
    for j in range(D // 128):
        pool[j, rows, :] = value[:, 128 * j : 128 * j + 128]


def fill_moved(x_ref, z_ref, pool, slots):
    for k, ref in enumerate((x_ref, z_ref)):
        for j in range(MOVED):
            write_rows(pool, TP * slots + k * MOVED + j, slots, ref[j].astype(f32))


def empty_pool(pool, slots, out_ref, x_ref, z_ref):
    def part(at, count):
        for j in range(D // 128):
            out_ref[pl.ds(at, count), 128 * j : 128 * j + 128] = pool[j, pl.ds(at, count)].astype(bf16)

    by_rows(out_ref.shape[0], TP, part)
    for k, ref in enumerate((x_ref, z_ref)):
        for j in range(MOVED):
            ref[j] = read_rows(pool, TP * slots + k * MOVED + j, slots).astype(bf16)


def fetch(n_ref, pieces, buf, sems):
    rows = pieces[0].shape[0]
    copies = []
    for k, piece in enumerate(pieces):
        at = pl.multiple_of((n_ref[ME] ^ k) * rows, 32)
        copies.append(pltpu.make_async_copy(piece, buf.at[pl.ds(at, rows)], sems.at[k]))
    return start_all(copies)


def finish(n_ref, acc, send_s, send_ref, keep_ref, pool, slots, natives, outs, sems):
    pairs, rows = send_s.shape[0], send_s.shape[1]
    me = n_ref[ME] & 1
    copies = []
    for y in range(pairs):
        mine = pl.multiple_of((2 * y + me) * rows, 32)
        copies.append(pltpu.make_async_copy(acc.at[pl.ds(mine, rows)], keep_ref.at[y], sems.at[y]))
    start_all(copies)
    for y in range(pairs):
        theirs = pl.multiple_of((2 * y + 1 - me) * rows, 32)

        def part(at, count, y=y, theirs=theirs):
            send_s[y, pl.ds(at, count), :] = acc[pl.ds(pl.multiple_of(theirs + at, 16), count), :].astype(bf16)

        by_rows(rows, 16, part)
    copies += start_all([pltpu.make_async_copy(send_s, send_ref, sems.at[pairs])])
    out, x, z = natives
    empty_pool(pool, slots, out, x, z)
    copies += start_all([pltpu.make_async_copy(src, dst, sems.at[pairs + 1 + k]) for k, (src, dst) in enumerate(zip(natives, outs))])
    wait_all(copies)


def attn_fwd_kernel(parts, slots, n_ref, *rest):
    sources, pieces, rest = rest[:4], rest[4 : 4 + parts], rest[4 + parts :]
    hbm, vec_ref, w, pool, natives, (native_sems, w_sems) = rest[:4], rest[4], rest[5], rest[6], rest[7:11], rest[11:13]
    bufs, sems = rest[13:17], rest[17:]
    given = start_all(native_copies(sources, natives, native_sems))
    weights = fetch(n_ref, pieces, w, w_sems)
    wait_all(given)
    fill_pool(natives[0], natives[1], pool, slots)
    fill_moved(natives[2], natives[3], pool, slots)
    wait_all(weights)
    vec_ref[...] = w[:, 3 * D :].astype(f32).T[:16]

    def step(i, slot):
        x_ref, qkv_ref, o_ref, lse_ref = (v.at[slot] for v in bufs)
        x = read_rows(pool, first_row(n_ref, i, slots), slots)
        x_ref[...] = x.astype(bf16)
        n1, _ = norm(x)
        a = (n1 * vec_ref[0:1] + vec_ref[2:3]).astype(bf16)
        qb = jnp.concatenate([vec_ref[3:4], jnp.zeros((1, D), f32), vec_ref[4:5]], axis=1)
        qkv = (dot(a, w[:, : 3 * D]) + qb).astype(bf16)
        real = lax.broadcasted_iota(jnp.int32, (TP - TC, 3 * D), 0) < T - TC
        qkv_ref[:TC] = qkv[:TC]
        qkv_ref[TC:] = jnp.where(real, qkv[TC:], jnp.zeros_like(qkv[TC:]))
        lane = lax.broadcasted_iota(jnp.int32, (TP, 128), 1)
        low = lane < HD
        key = lax.broadcasted_iota(jnp.int32, (TP, TP), 1) < T
        lse = jnp.zeros((TP, 128), f32)
        for pair in range(H // 2):
            at = pair * 128
            q, k, v = (qkv_ref[:, off + at : off + at + 128] for off in (0, D, 2 * D))
            zero = jnp.zeros_like(q)
            o = None
            for side in range(2):
                sel = low if side == 0 else jnp.logical_not(low)
                s = jnp.where(key, dot_nt(jnp.where(sel, q, zero), k) * SCALE_LOG2E, -1e30)
                l2 = jnp.log2(jnp.sum(jnp.exp2(s), axis=-1, keepdims=True))
                p = jnp.exp2(s - l2).astype(bf16)
                part = dot(p, jnp.where(sel, v, zero))
                o = part if o is None else o + part
                lse = jnp.where(lane == pair * 2 + side, l2, lse)
            o_ref[:, at : at + 128] = o.astype(bf16)
        lse_ref[...] = lse

    stream(n_ref[N_ITEMS], (), tuple(zip(hbm, bufs, sems)), step)


FC = 256


def mlp_kernel(parts, slots, n_ref, xb_ref, ob_ref, *rest):
    sources, vec_ref, pieces, rest = rest[:4], rest[4], rest[5 : 5 + parts], rest[5 + parts :]
    dhb_ref, dob_ref, out_ref, ox_ref, oz_ref, send_ref, keep_ref, vb_ref = rest[:8]
    (w, acc, vg, gbu, cpool, opool, bu_s, c_s, dy_s, ct_s, dyt_s, zb, db, ub, eb, out_s, dc_s, send_s) = rest[8:26]
    natives, (native_sems, w_sems, out_sems), bufs, sems = rest[26:30], rest[30:33], rest[33:37], rest[37:]
    flow = tuple(zip((xb_ref, ob_ref, dhb_ref, dob_ref), bufs, sems))
    given = start_all(native_copies(sources, natives, native_sems))
    weights = fetch(n_ref, pieces, w, w_sems)
    first_items(flow[:2])
    clear(acc)
    vg[...] = jnp.zeros_like(vg)
    gbu[...] = jnp.zeros_like(gbu)
    bu_s[...] = jnp.concatenate([vec_ref[8 + j : 9 + j] for j in range(F // D)], axis=1)
    wait_all(given)
    fill_pool(natives[0], natives[1], cpool, slots)
    fill_moved(natives[2], natives[3], cpool, slots)
    wait_all(weights)

    def step(i, slot):
        x_ref, o_ref, dh_ref, do_ref = (v.at[slot] for v in bufs)
        at = first_row(n_ref, i, slots)
        g2, b2, bo, bd = vec_ref[1:2], vec_ref[6:7], vec_ref[5:6], vec_ref[7:8]
        x = x_ref[...].astype(f32)
        o = o_ref[...]
        h = x + dot(o, w[:, :D]) + bo
        n2, r2 = norm(h)
        c = (n2 * g2 + b2).astype(bf16)
        dyf = read_rows(cpool, at, slots)
        dy = dyf.astype(bf16)
        steps = F // FC
        c_s[...] = c
        dy_s[...] = dy
        ct_s[...] = c.T
        dyt_s[...] = dy.T

        def cols(base, j):
            return slice(base + j * FC, base + j * FC + FC)

        def produce(j, slot):
            zb[slot] = dot(c_s[...], w[:, cols(D, j)])
            db[slot] = dot(dy_s[...], w[:, cols(D + F, j)])

        def middle(j, slot):
            u, slope = gelu_parts(zb[slot] + bu_s[:, cols(0, j)])
            dz = db[slot] * slope
            gbu[:, cols(0, j)] += col8(dz)
            ub[slot] = u.astype(bf16)
            eb[slot] = dz.astype(bf16)

        def consume(j, slot, first=False):
            u, dzb = ub[slot], eb[slot]
            o1, d1 = dot_nt(u, w[:, cols(D + F, j)]), dot_nt(dzb, w[:, cols(D, j)])
            out_s[...] = o1 if first else out_s[...] + o1
            dc_s[...] = d1 if first else dc_s[...] + d1
            acc[:, cols(D, j)] += dot(ct_s[...], dzb)
            acc[:, cols(D + F, j)] += dot(dyt_s[...], u)

        produce(0, 0)
        produce(1, 1)
        middle(0, 0)
        for j in range(1, steps):
            if j + 1 < steps:
                produce(j + 1, (j + 1) % 3)
            consume(j - 1, (j - 1) % 3, j == 1)
            middle(j, j % 3)
        consume(steps - 1, (steps - 1) % 3)
        out, dc = out_s[...], dc_s[...]
        write_rows(opool, at, slots, h + out + bd)
        dh = dyf + norm_back(dc * g2, n2, r2)
        dh_ref[...] = dh
        dhb = dh.astype(bf16)
        acc[:, :D] += dot(o.T, dhb)
        do_ref[...] = dot_nt(dhb, w[:, :D]).astype(bf16)
        vg[0:8] += col8(dc * n2)
        vg[8:16] += col8(dh)
        vg[16:24] += col8(dc)
        vg[24:32] += col8(dyf)

    stream(n_ref[N_ITEMS], flow[:2], flow[2:], step)
    rows = [total(vg[8 * k : 8 * k + 8]) for k in range(4)]
    rows += [total(gbu[:, k * D : (k + 1) * D]) for k in range(F // D)]
    vb_ref[...] = jnp.concatenate(rows, axis=0)
    finish(n_ref, acc, send_s, send_ref, keep_ref, opool, slots, (natives[0], natives[2], natives[3]),
           (out_ref, ox_ref, oz_ref), out_sems)


def attn_bwd_kernel(parts, slots, n_ref, xb_ref, qkvb_ref, lseb_ref, dob_ref, dhb_ref, vec_ref, vb_ref, *rest):
    pieces, rest = rest[:parts], rest[parts:]
    (out_ref, ox_ref, oz_ref, send_ref, keep_ref, w, acc, vg, dqkv, opool, sb, db, pb, gb, tb, qt, dot_, kt, vt, vsum,
     send_s) = rest[:21]
    natives, (w_sems, out_sems), bufs, sems = rest[21:24], rest[24:26], rest[26:31], rest[31:]
    flow = tuple(zip((xb_ref, qkvb_ref, lseb_ref, dob_ref, dhb_ref), bufs, sems))
    first_items(flow)
    weights = fetch(n_ref, pieces, w, w_sems)
    clear(acc)
    vg[...] = jnp.zeros_like(vg)
    vsum[...] = jnp.zeros_like(vsum)
    wait_all(weights)

    def step(i, slot):
        x_ref, qkv_ref, lse_ref, do_ref, dh_ref = (v.at[slot] for v in bufs)
        g1, b1 = vec_ref[0:1], vec_ref[2:3]
        x = x_ref[...].astype(f32)
        n1, r1 = norm(x)
        at_ = (n1 * g1 + b1).astype(bf16).T
        low = lax.broadcasted_iota(jnp.int32, (TP, 128), 1) < HD
        real = lax.broadcasted_iota(jnp.int32, (TP - TC, D), 0) < T - TC

        def mask(h, v):
            return jnp.where(low if h % 2 == 0 else jnp.logical_not(low), v, jnp.zeros_like(v))

        def lanes(h, off=0):
            return slice(off + (h // 2) * 128, off + (h // 2) * 128 + 128)

        def produce(h):
            sb[h % 3] = dot_nt(mask(h, qkv_ref[:, lanes(h)]), qkv_ref[:, lanes(h, D)])
            db[h % 3] = dot_nt(mask(h, do_ref[:, lanes(h)]), qkv_ref[:, lanes(h, 2 * D)])

        def middle(h):
            p = jnp.exp2(sb[h % 3] * SCALE_LOG2E - lse_ref[:, h : h + 1])
            dp = db[h % 3]
            pb[h % 2] = p.astype(bf16)
            delta = jnp.sum(p * dp, axis=-1, keepdims=True)
            gb[h % 2] = (p * (dp - delta) * SCALE).astype(bf16)

        def rows_of(h):
            return slice(h * HD, h * HD + HD)

        qt[...] = qkv_ref[:, :D].T
        dot_[...] = do_ref[...].T

        def consume(h):
            ds = gb[h % 2]
            kt[rows_of(h), :] = dot(qt[rows_of(h), :], ds).astype(bf16)
            dv = dot(dot_[rows_of(h), :], pb[h % 2])
            vt[rows_of(h), :] = dv.astype(bf16)
            vsum[rows_of(h), :] += dv
            dq = dot(ds, mask(h, qkv_ref[:, lanes(h, D)]))
            if h % 2 == 0:
                tb[...] = dq
                return
            dq = tb[...] + dq
            dqkv[:, lanes(h)] = dq.astype(bf16)
            vg[16:24, lanes(h)] += col8(dq)

        produce(0)
        produce(1)
        middle(0)
        for h in range(1, H):
            if h + 1 < H:
                produce(h + 1)
            consume(h - 1)
            middle(h)
        consume(H - 1)
        for ref, off in ((kt, D), (vt, 2 * D)):
            v = ref[...].T
            dqkv[:TC, off : off + D] = v[:TC]
            dqkv[TC:, off : off + D] = jnp.where(real, v[TC:], jnp.zeros_like(v[TC:]))
        dqkv_b = dqkv[...]
        acc[:, : 3 * D] += dot(at_, dqkv_b)
        da = dot_nt(dqkv_b, w[:, : 3 * D])
        write_rows(opool, first_row(n_ref, i, slots), slots, dh_ref[...] + norm_back(da * g1, n1, r1))
        vg[0:8] += col8(da * n1)
        vg[8:16] += col8(da)

    stream(n_ref[N_ITEMS], flow, (), step)
    token = lax.broadcasted_iota(jnp.int32, (D, TP), 1) < T
    dv = jnp.sum(jnp.where(token, vsum[...], 0.0), axis=1, keepdims=True)
    mine = [total(vg[8 * k : 8 * k + 8]) for k in range(3)] + [jnp.broadcast_to(dv, (D, 128)).T[:1]]
    vb = vb_ref[...]
    rows = jnp.concatenate([mine[0], vb[0:1], mine[1], mine[2], mine[3], vb[1:8], jnp.zeros((116, D), f32)], axis=0)
    acc[:, 3 * D :] = rows.T
    finish(n_ref, acc, send_s, send_ref, keep_ref, opool, slots, natives, (out_ref, ox_ref, oz_ref), out_sems)


def once(shape):
    return pl.BlockSpec(shape, lambda i, *n: (0,) * len(shape), pipeline_mode=pl.Buffered(1))


PLAN = pltpu.SMEM((12,), jnp.int32)


def planned(kernel):
    def run(*refs):
        make_plan(*refs[:5], refs[-1])
        kernel(refs[-1], *refs[5:-1])

    return run


def layer_call(kernel, n, slots, streams, ins, pieces, left, outs, scratch, sems, flow, flops):
    parts = len(pieces)
    items = [S((slots + 2 * MOVED,) + v.shape, v.dtype) for v in flow[len(streams):]]
    return pl.pallas_call(
        planned(lambda *refs: kernel(parts, slots, *refs)),
        out_shape=tuple(items) + tuple(left) + tuple(outs),
        grid_spec=pltpu.PrefetchScalarGridSpec(
            num_scalar_prefetch=5, grid=(1,),
            in_specs=[ANY] * len(streams) + [once(v.shape) if v.size <= 16 * D else ANY for v in ins] + [ANY] * parts,
            out_specs=tuple([ANY] * (len(items) + len(left)) + [once(v.shape) for v in outs]),
            scratch_shapes=list(scratch) + [pltpu.SemaphoreType.DMA((k,)) for k in sems]
            + [pltpu.VMEM((2,) + v.shape, v.dtype) for v in flow] + [pltpu.SemaphoreType.DMA((2,)) for _ in flow]
            + [PLAN]),
        compiler_params=pltpu.CompilerParams(
            dimension_semantics=("arbitrary",), vmem_limit_bytes=VMEM_LIMIT),
        cost_estimate=pl.CostEstimate(flops=flops, bytes_accessed=20_000_000, transcendentals=0))(*n, *streams, *ins, *pieces)


FEW = S((MOVED, TP, D), bf16)
WIDE = S((TP, D), f32)
SLIM = S((TP, D), bf16)
QKV = S((TP, 3 * D), bf16)
LSE = S((TP, 128), f32)


def pool_of(slots):
    return pltpu.VMEM((D // 128, 2 * TP * slots, 128), f32)


def reduced(parts, cols):
    shape = (parts // 2, D // parts, cols)
    return S(shape, bf16), S(shape, f32)


def vmem(v):
    return pltpu.VMEM(v.shape, v.dtype)


def attn_fwd(n, slots, own, got, x, z, pieces):
    native = S(own.shape, bf16)
    return layer_call(
        attn_fwd_kernel, n, slots, (), (own, got, x, z), pieces, (), (S((16, D), f32),),
        (pltpu.VMEM((D, Q_COLS), bf16), pool_of(slots)) + tuple(vmem(v) for v in (native, native, FEW, FEW)),
        (4, len(pieces)), (SLIM, QKV, SLIM, LSE), 10_000_000_000)


def mlp(n, slots, x, o, c_own, c_got, c_x, c_z, vec, pieces):
    native, sums = S(c_own.shape, bf16), reduced(len(pieces), R_COLS)
    return layer_call(
        mlp_kernel, n, slots, (x, o), (c_own, c_got, c_x, c_z, vec), pieces, (native, FEW, FEW) + sums, (S((8, D), f32),),
        (pltpu.VMEM((D, R_COLS), bf16), pltpu.VMEM((D, R_COLS), f32), pltpu.VMEM((32, D), f32),
         pltpu.VMEM((8, F), f32), pool_of(slots), pool_of(slots),
         pltpu.VMEM((1, F), f32), pltpu.VMEM((TP, D), bf16), pltpu.VMEM((TP, D), bf16), pltpu.VMEM((D, TP), bf16),
         pltpu.VMEM((D, TP), bf16), pltpu.VMEM((3, TP, FC), f32), pltpu.VMEM((3, TP, FC), f32),
         pltpu.VMEM((3, TP, FC), bf16), pltpu.VMEM((3, TP, FC), bf16), pltpu.VMEM((TP, D), f32),
         pltpu.VMEM((TP, D), f32), vmem(sums[0])) + tuple(vmem(v) for v in (native, native, FEW, FEW)),
        (4, len(pieces), len(pieces) // 2 + 4), (SLIM, SLIM, WIDE, SLIM), 25_000_000_000)


def attn_bwd(n, slots, x, qkv, lse, do, dh, vec, vb, pieces, rows):
    native, sums = S((rows, D), bf16), reduced(len(pieces), Q_COLS)
    return layer_call(
        attn_bwd_kernel, n, slots, (x, qkv, lse, do, dh), (vec, vb), pieces, (native, FEW, FEW) + sums, (),
        (pltpu.VMEM((D, Q_COLS), bf16), pltpu.VMEM((D, Q_COLS), f32), pltpu.VMEM((32, D), f32),
         pltpu.VMEM((TP, 3 * D), bf16), pool_of(slots), pltpu.VMEM((3, TP, TP), f32),
         pltpu.VMEM((3, TP, TP), f32), pltpu.VMEM((2, TP, TP), bf16), pltpu.VMEM((2, TP, TP), bf16),
         pltpu.VMEM((TP, 128), f32)) + (pltpu.VMEM((D, TP), bf16),) * 4 + (pltpu.VMEM((D, TP), f32), vmem(sums[0]))
        + tuple(vmem(v) for v in (native, FEW, FEW)),
        (len(pieces), len(pieces) // 2 + 4), (SLIM, QKV, LSE, SLIM, WIDE), 20_000_000_000)


def pack_first_kernel(w_ref, g_ref, b_ref, o_ref):
    rows = w_ref.shape[0]
    vec = jnp.concatenate([g_ref[...], b_ref[...], jnp.zeros((128 - NV, rows), f32)], axis=0)
    o_ref[:, : 3 * D] = w_ref[...].astype(bf16)
    o_ref[:, 3 * D :] = vec.T.astype(bf16)


def pack_rest_kernel(p_ref, a_ref, b_ref, o_ref):
    o_ref[:, :D] = p_ref[...].astype(bf16)
    o_ref[:, D : D + F] = a_ref[...].astype(bf16)
    o_ref[:, D + F : D + 2 * F] = b_ref[...].astype(bf16)
    o_ref[:, D + 2 * F :] = jnp.zeros((o_ref.shape[0], R_COLS - D - 2 * F), bf16)


def split3(a):
    hi = a.astype(bf16)
    return hi, (a - hi.astype(f32)).astype(bf16)


def dot3(a, b):
    return dot(jnp.concatenate([a[0], a[1], a[0]], axis=1), jnp.concatenate([b[0], b[0], b[1]], axis=0))


def dot3_sym(a, b):
    left = jnp.concatenate([a[0], a[1], a[0]], axis=1)
    right = jnp.concatenate([b[0], b[0], b[1]], axis=0)
    wide = dot(left, right[:, :256])
    corner = dot(left[256:], right[:, 256:])
    return jnp.concatenate([wide, jnp.concatenate([wide[256:].T, corner], axis=0)], axis=1)


def orth_rows(m, a_s, q_s, at):
    wide, corner = dot_nt(m, m[:256]), dot_nt(m[256:], m[256:])
    a = jnp.concatenate([wide, jnp.concatenate([wide[256:].T, corner], axis=0)], axis=1)
    row, col = (lax.broadcasted_iota(jnp.int32, (D, D), k) for k in range(2))
    ssq = jnp.sum(jnp.where(row == col, a, 0.0), axis=(0, 1), keepdims=True)
    s = 1.0 / (jnp.sqrt(ssq) + ORTHO_EPSILON)
    a_s[...] = a * (s * s)
    row, col = (lax.broadcasted_iota(jnp.int32, q_s.shape, k) for k in range(2))
    q_s[...] = jnp.where(row + at == col, 1.0, 0.0)

    def turn(k, carry):
        a = a_s[...]
        parts = split3(a)
        row, col = (lax.broadcasted_iota(jnp.int32, (D, D), k) for k in range(2))
        p = split3(jnp.where(row == col, COEFF_FIRST, 0.0) + COEFF_SECOND * a + COEFF_THIRD * dot3_sym(parts, parts))
        q_s[...] = dot3(split3(q_s[...]), p)
        a_s[...] = dot3_sym(split3(dot3_sym(p, parts)), p)
        return carry

    lax.fori_loop(0, NS_ITERS - 1, turn, 0)
    parts, q = split3(a_s[...]), q_s[...]
    qa = dot3(split3(q), parts)
    q = COEFF_FIRST * q + COEFF_SECOND * qa + COEFF_THIRD * dot3(split3(qa), parts)
    hi, lo = split3(q * s)
    return dot(hi, m) + dot(lo, m)


def fetch_cols(n_ref, pieces, buf, sems, at_col, cols):
    rows = pieces[0].shape[0]
    copies = []
    for k, piece in enumerate(pieces):
        at = pl.multiple_of((n_ref[0] ^ k) * rows, 32)
        copies.append(pltpu.make_async_copy(
            piece.at[:, pl.ds(at_col, cols)], buf.at[pl.ds(at, rows), pl.ds(0, cols)], sems.at[k]))
    for c in copies:
        c.start()
    for c in copies:
        c.wait()


def orth_both(n_ref, mine_ref, theirs_ref, m, a_s, q_s, o_s):
    rows = mine_ref.shape[0]
    core = n_ref[0] & 1
    at = pl.multiple_of((n_ref[0] - core) * rows, 32)
    o_s[...] = orth_rows(m[...], a_s, q_s, at)
    mine_ref[...] = o_s[pl.ds(pl.multiple_of(core * rows, 32), rows), :]
    theirs_ref[...] = o_s[pl.ds(pl.multiple_of((1 - core) * rows, 32), rows), :]


def orth_mlp_kernel(parts, n_ref, *rest):
    pieces = rest[:parts]
    mine_ref, theirs_ref, m, a_s, q_s, o_s, sems = rest[parts:]
    fetch_cols(n_ref, pieces, m, sems, pl.multiple_of((n_ref[0] & 1) * F, 128), F)
    orth_both(n_ref, mine_ref, theirs_ref, m, a_s, q_s, o_s)


def orth_attn_kernel(parts, n_ref, *rest):
    pieces = rest[:parts]
    mine_ref, theirs_ref, m, a_s, q_s, o_s, sems = rest[parts:]

    @pl.when(n_ref[0] & 1 == 0)
    def _():
        fetch_cols(n_ref, pieces, m, sems, 0, 3 * D)

    @pl.when(n_ref[0] & 1 == 1)
    def _():
        m[:, D:] = jnp.zeros((D, 2 * D), bf16)
        fetch_cols(n_ref, pieces, m, sems, 3 * D, D)

    orth_both(n_ref, mine_ref, theirs_ref, m, a_s, q_s, o_s)


def orth_call(kernel, me, pieces, cols):
    parts = len(pieces)
    rows = pieces[0].shape[0]
    spec = pl.BlockSpec((rows, cols), lambda i, n: (0, 0))
    return pl.pallas_call(
        lambda *refs: kernel(parts, *refs),
        out_shape=(S((rows, cols), f32),) * 2,
        grid_spec=pltpu.PrefetchScalarGridSpec(
            num_scalar_prefetch=1, grid=(1,), in_specs=[ANY] * parts, out_specs=(spec,) * 2,
            scratch_shapes=[pltpu.VMEM((D, cols), bf16), pltpu.VMEM((D, D), f32), pltpu.VMEM((2 * rows, D), f32), pltpu.VMEM((2 * rows, cols), f32),
                            pltpu.SemaphoreType.DMA((parts,))]),
        compiler_params=pltpu.CompilerParams(vmem_limit_bytes=VMEM_LIMIT),
        cost_estimate=pl.CostEstimate(flops=8_000_000_000, bytes_accessed=4_000_000, transcendentals=0))(me, *pieces)


def swap(v, axis, k):
    return lax.ppermute(v, axis, [(i, i ^ k) for i in range(lax.axis_size(axis))])


def bits(axis):
    return range(lax.axis_size(axis).bit_length() - 1)


def bit(axis, b):
    return (lax.axis_index(axis) >> b) & 1


def all_pieces(v, axis):
    pieces = {0: v}
    for b in reversed(bits(axis)):
        pieces.update({k ^ (1 << b): swap(p, axis, 1 << b) for k, p in list(pieces.items())})
    return [pieces[k] for k in range(lax.axis_size(axis))]


def take(v, i):
    return lax.dynamic_index_in_dim(v, i, 0, keepdims=False)


def sum_blocks(send, keep):
    got = swap(send, "fsdp", 1)
    keep, got = (v.reshape((2, -1) + v.shape[1:]) for v in (keep, got))
    for b in reversed(bits("fsdp")[1:]):
        me = bit("fsdp", b)
        sent = (take(keep, 1 - me) + take(got, 1 - me).astype(f32)).astype(bf16)
        own = take(keep, me) + take(got, me).astype(f32)
        got = swap(sent, "fsdp", 1 << b)
        keep = own
        if keep.shape[0] > 1:
            keep, got = (v.reshape((2, -1) + v.shape[1:]) for v in (keep, got))
    return (keep + got.astype(f32)).reshape(keep.shape[-2:])


def halves(v, axis):
    n = v.shape[axis] // 2
    return lax.slice_in_dim(v, 0, n, axis=axis), lax.slice_in_dim(v, n, 2 * n, axis=axis)


def sum_groups(v):
    for b in bits("rep"):
        me = bit("rep", b)
        lo, hi = halves(v, 1 if b == 0 else 0)
        got = swap(jnp.where(me == 0, hi, lo).astype(bf16), "rep", 1 << b)
        v = jnp.where(me == 0, lo, hi) + got.astype(f32)
    v = v.astype(bf16)
    for b in reversed(bits("rep")):
        me = bit("rep", b)
        got = swap(v, "rep", 1 << b)
        v = jnp.concatenate([jnp.where(me == 0, v, got), jnp.where(me == 0, got, v)], axis=1 if b == 0 else 0)
    return v


def sum_groups_whole(v):
    v = v.astype(bf16)
    for b in bits("rep"):
        got = swap(v, "rep", 1 << b)
        v = (v.astype(f32) + got.astype(f32)).astype(bf16)
    return v


def pick_kernel(slots, count_ref, a_ref, b_ref, ax_ref, az_ref, bx_ref, bz_ref, pool):
    for ref, x_ref, z_ref in ((a_ref, ax_ref, az_ref), (b_ref, bx_ref, bz_ref)):
        fill_pool(ref, ref, pool, slots)
        for j in range(MOVED):
            x_ref[j] = read_rows(pool, jnp.maximum(count_ref[0] - 1 - j, 0), slots).astype(bf16)
            z_ref[j] = read_rows(pool, jnp.maximum(count_ref[0] - MOVED - 1 - j, 0), slots).astype(bf16)


def pool_call(kernel, scalars, slots, ins, outs, scratch):
    return pl.pallas_call(
        kernel, out_shape=outs,
        grid_spec=pltpu.PrefetchScalarGridSpec(
            num_scalar_prefetch=len(scalars), grid=(1,), in_specs=[once(v.shape) for v in ins],
            out_specs=tuple(once(v.shape) for v in outs),
            scratch_shapes=[pltpu.VMEM((D // 128, TP * slots, 128), f32)] + list(scratch)),
        compiler_params=pltpu.CompilerParams(vmem_limit_bytes=VMEM_LIMIT),
        cost_estimate=pl.CostEstimate(flops=1_000_000, bytes_accessed=7_000_000, transcendentals=0))(*scalars, *ins)


def unpool_kernel(slots, n_ref, own_ref, got_ref, x_ref, z_ref, o_ref, pool):
    fill_pool(own_ref, got_ref, pool, slots)
    for j in range(MOVED):
        for ref, given, at in ((x_ref, TO_X, 1), (z_ref, TO_Z, MOVED + 1)):
            @pl.when(j < n_ref[given])
            def _(ref=ref, at=at):
                write_rows(pool, n_ref[COUNT] - at - j, slots, ref[j].astype(f32))

    def part(at, count):
        live = (lax.broadcasted_iota(jnp.int32, (count, 128), 0) & (slots - 1)) < n_ref[COUNT]
        for j in range(D // 128):
            o_ref[pl.ds(at, count), 128 * j : 128 * j + 128] = jnp.where(live, pool[j, pl.ds(at, count)], 0.0).astype(bf16)

    by_rows(o_ref.shape[0], TP, part)


def adam_kernel(scale, g_ref, *refs):
    ins, outs = refs[:6], refs[6:]
    g = (g_ref[...].astype(f32) * scale).T
    for k, (lo, hi) in enumerate(((0, 2), (2, NV))):
        gradient, parameter = g[lo:hi], ins[k][...]
        first = ADAM_FIRST * ins[2 + 2 * k][...] + (1.0 - ADAM_FIRST) * gradient
        second = ADAM_SECOND * ins[3 + 2 * k][...] + (1.0 - ADAM_SECOND) * gradient * gradient
        first_hat = first / (1.0 - ADAM_FIRST**ADAM_STEP)
        second_hat = second / (1.0 - ADAM_SECOND**ADAM_STEP)
        outs[k][...] = gradient
        outs[2 + k][...] = parameter - ADAM_RATE * (
            first_hat / (jnp.sqrt(second_hat) + ADAM_EPSILON) + ADAM_DECAY * parameter)
        outs[4 + 2 * k][...] = first
        outs[5 + 2 * k][...] = second


def adam(last, devices, *states):
    full = [pl.BlockSpec(v.shape, lambda i: (0, 0)) for v in states]
    one, two = S(states[0].shape, f32), S(states[1].shape, f32)
    return pl.pallas_call(
        lambda *refs: adam_kernel(1.0 / devices, *refs),
        grid=(1,), out_shape=(one, two, one, two, one, one, two, two),
        in_specs=[pl.BlockSpec((last.shape[0], 128), lambda i: (0, 3 * D // 128))] + full,
        out_specs=tuple(full[k] for k in (0, 1, 0, 1, 2, 3, 4, 5)), name="adam")(last, *states)


def muon_factor(row_total, column_total):
    return math.sqrt(max(1.0, row_total / column_total))


def body(images, cotangent, counts, w_qkv, w_proj, w_fc1, w_fc2, gains, biases,
         mom_qkv, mom_proj, mom_fc1, mom_fc2, gains_first, gains_second, biases_first, biases_second):
    slots = images.shape[0]
    rows = w_qkv.shape[0]
    devices = lax.axis_size("rep") * lax.axis_size("fsdp")
    me = lax.axis_index("fsdp").astype(jnp.int32)

    first = pl.pallas_call(pack_first_kernel, out_shape=S((rows, Q_COLS), bf16), name="pack_first")(w_qkv, gains, biases)
    q_pieces = all_pieces(first, "fsdp")

    pair = jnp.concatenate([counts, swap(counts, "fsdp", 1)])
    n = (me.reshape(1), pair) + tuple(swap(pair, "rep", k) for k in (1, 2, 3))

    own = [v.transpose(1, 0, 2).reshape(-1, D) for v in (images, cotangent)]
    offers = pool_call(lambda *refs: pick_kernel(slots, *refs), (counts,), slots, own, (FEW,) * 4, ())

    def spread(v, to_x, to_z):
        return v, swap(v, "fsdp", 1), swap(to_x, "rep", 1), swap(to_z, "rep", 2)

    x_in = spread(own[0], *offers[:2])
    c_in = spread(own[1], *offers[2:])

    def unpool(v, to_x, to_z):
        ins = (v, swap(v, "fsdp", 1), swap(to_x, "rep", 1), swap(to_z, "rep", 2))
        (full,) = pool_call(planned(lambda *refs: unpool_kernel(slots, *refs)), n, slots, ins, (S(v.shape, bf16),), (PLAN,))
        return full.reshape(-1, slots, D).transpose(1, 0, 2)

    rest = pl.pallas_call(pack_rest_kernel, out_shape=S((rows, R_COLS), bf16), name="pack_rest")(w_proj, w_fc1, w_fc2.T)
    r_pieces = all_pieces(rest, "fsdp")

    x, qkv, o, lse, vec = attn_fwd(n, slots, *x_in, q_pieces)
    dh, do, *out, r_send, r_keep, vb = mlp(n, slots, x, o, *c_in, vec, r_pieces)
    mid = sum_blocks(r_send, r_keep)
    *in_grad, q_send, q_keep = attn_bwd(n, slots, x, qkv, lse, do, dh, vec, vb, q_pieces, x_in[0].shape[0])
    mid = sum_groups(mid)
    last = sum_groups_whole(sum_blocks(q_send, q_keep))
    block_out = unpool(*out)
    input_grad = unpool(*in_grad)

    vectors = adam(last, devices, gains, biases, gains_first, gains_second, biases_first, biases_second)
    scale = 1.0 / devices
    grad_qkv = last[:, : 3 * D].astype(f32) * scale
    grad_proj, grad_fc1, grad_fc2t = (
        mid[:, lo:hi].astype(f32) * scale for lo, hi in ((0, D), (D, D + F), (D + F, D + 2 * F)))
    next_qkv = MUON_MOMENTUM * mom_qkv + grad_qkv
    next_proj = MUON_MOMENTUM * mom_proj + grad_proj
    next_fc1 = MUON_MOMENTUM * mom_fc1 + grad_fc1
    next_fc2t = MUON_MOMENTUM * mom_fc2.T + grad_fc2t
    attn_pieces = all_pieces(jnp.concatenate([next_qkv.astype(bf16), next_proj.astype(bf16)], axis=1), "fsdp")
    mlp_pieces = all_pieces(jnp.concatenate([next_fc1.astype(bf16), next_fc2t.astype(bf16)], axis=1), "fsdp")

    core = me & 1
    mine, theirs = orth_call(orth_attn_kernel, me.reshape(1), attn_pieces, 3 * D)
    got = swap(theirs, "fsdp", 1)
    orth_qkv, orth_proj = jnp.where(core == 0, mine, got), jnp.where(core == 0, got, mine)[:, :D]
    mine, theirs = orth_call(orth_mlp_kernel, me.reshape(1), mlp_pieces, F)
    got = swap(theirs, "fsdp", 1)
    orth_fc1, orth_fc2t = jnp.where(core == 0, mine, got), jnp.where(core == 0, got, mine)
    new_qkv = w_qkv - MUON_RATE * muon_factor(D, 3 * D) * orth_qkv
    new_proj = w_proj - MUON_RATE * muon_factor(D, D) * orth_proj
    new_fc1 = w_fc1 - MUON_RATE * muon_factor(D, F) * orth_fc1
    new_fc2t = w_fc2.T - MUON_RATE * muon_factor(F, D) * orth_fc2t
    grad_gains, grad_biases, new_gains, new_biases = vectors[:4]
    return (block_out, input_grad, grad_qkv, grad_proj, grad_fc1, grad_fc2t.T, grad_gains, grad_biases,
            new_qkv, new_proj, new_fc1, new_fc2t.T, new_gains, new_biases,
            next_qkv, next_proj, next_fc1, next_fc2t.T) + tuple(vectors[4:])


def solution(mesh):
    in_specs = (
        P(("rep", "fsdp"), None, None),
        P(("rep", "fsdp"), None, None),
        P(("rep", "fsdp")),
        P("fsdp", None),
        P("fsdp", None),
        P("fsdp", None),
        P(None, "fsdp"),
        P(None, "fsdp"),
        P(None, "fsdp"),
        P("fsdp", None),
        P("fsdp", None),
        P("fsdp", None),
        P(None, "fsdp"),
        P(None, "fsdp"),
        P(None, "fsdp"),
        P(None, "fsdp"),
        P(None, "fsdp"),
    )
    out_specs = (
        P(("rep", "fsdp"), None, None),
        P(("rep", "fsdp"), None, None),
        P("fsdp", None),
        P("fsdp", None),
        P("fsdp", None),
        P(None, "fsdp"),
        P(None, "fsdp"),
        P(None, "fsdp"),
        P("fsdp", None),
        P("fsdp", None),
        P("fsdp", None),
        P(None, "fsdp"),
        P(None, "fsdp"),
        P(None, "fsdp"),
        P("fsdp", None),
        P("fsdp", None),
        P("fsdp", None),
        P(None, "fsdp"),
        P(None, "fsdp"),
        P(None, "fsdp"),
        P(None, "fsdp"),
        P(None, "fsdp"),
    )
    return jax.shard_map(body, mesh=mesh, in_specs=in_specs, out_specs=out_specs, check_vma=False)
```

```python
import math

import jax
import jax.numpy as jnp
from jax import lax
from jax.experimental import pallas as pl
from jax.experimental.pallas import tpu as pltpu
from jax.sharding import PartitionSpec as P


NS_ITERS = 5
ADAM_STEP = 3
ORTHO_EPSILON = 1e-07
COEFF_FIRST = 3.4445
COEFF_SECOND = -4.775
COEFF_THIRD = 2.0315
MUON_RATE = 0.3
MUON_MOMENTUM = 0.95
ADAM_RATE = 0.2
ADAM_FIRST = 0.9
ADAM_SECOND = 0.95
ADAM_EPSILON = 1e-08
ADAM_DECAY = 0.25

D = 384
H = 6
HD = 64
F = 1536
T = 197
TP = 208
TC = T // 16 * 16
EPS = 1e-6
NV = 12
Q_COLS = 3 * D + 128
R_COLS = D + 2 * F + 128
f32 = jnp.float32
bf16 = jnp.bfloat16
SCALE = 1.0 / math.sqrt(HD)
SCALE_LOG2E = SCALE * math.log2(math.e)
VMEM_LIMIT = 60 * 1024 * 1024
S = jax.ShapeDtypeStruct
ANY = pl.BlockSpec(memory_space=pl.ANY)


def dot(a, b):
    return jnp.dot(a, b, preferred_element_type=f32)


def dot_nt(a, b):
    return lax.dot_general(a, b, (((1,), (1,)), ((), ())), preferred_element_type=f32)


def norm(x):
    xc = x - jnp.mean(x, axis=-1, keepdims=True)
    r = lax.rsqrt(jnp.mean(xc * xc, axis=-1, keepdims=True) + EPS)
    return xc * r, r


def norm_back(e, n, r):
    return r * (e - jnp.mean(e, axis=-1, keepdims=True) - n * jnp.mean(e * n, axis=-1, keepdims=True))


def col8(v):
    return jnp.sum(v.reshape(v.shape[0] // 8, 8, v.shape[1]), axis=0)


def total(v):
    return jnp.sum(v, axis=0, keepdims=True)


PHI_T = 0.28
PHI_C = (0.11652077999788102, 0.06749674653879187, 0.2689101818992952,
         -0.2369935012534717, 0.38987403003604115, -0.10580824648054844)
HALF_LOG2E = -0.5 * math.log2(math.e)
DENSITY = 1.0 / math.sqrt(2.0 * math.pi)


def gelu_parts(z):
    t = 1.0 / (1.0 + PHI_T * jnp.abs(z))
    bell = jnp.exp2((z * z) * HALF_LOG2E)
    poly = PHI_C[5] * t + PHI_C[4]
    for k in (3, 2, 1, 0):
        poly = poly * t + PHI_C[k]
    tail = (poly * t) * bell
    cdf = jnp.where(z < 0.0, tail, 1.0 - tail)
    return z * cdf, cdf + (z * DENSITY) * bell


MOVED = 2
N_ITEMS, N_OWN, ME, N_POOL, OWN_GAP, OWN_JUMP, GOT_GAP, GOT_JUMP, FROM_X, TO_X, TO_Z, COUNT = range(12)


def make_plan(me_ref, *refs):
    v, o_ref = [ref[k] for ref in refs[:4] for k in range(2)], refs[4]
    core = me_ref[0] & 1
    loads = [v[2 * k] + v[2 * k + 1] for k in range(4)]

    def flow(a, b):
        return jnp.minimum((a - b) >> 1, 2 * MOVED), jnp.minimum((b - a) >> 1, 2 * MOVED)

    def share(amount, spare, k):
        return jnp.clip(jnp.minimum((amount + 1 - k) >> 1, spare), 0, MOVED)

    def both(amount, pair, kept):
        return [share(amount, c - kept, k) for c, k in zip(pair, (core, 1 - core))]

    def edge(a, b, load_a, load_b, kept):
        out, back = flow(load_a, load_b)
        s, r = both(out, a, kept), both(back, b, kept)
        return s, r, load_a + r[0] + r[1] - s[0] - s[1], load_b + s[0] + s[1] - r[0] - r[1]

    sx, rx, load, _ = edge(v[0:2], v[2:4], loads[0], loads[1], 1)
    _, _, load_z, _ = edge(v[4:6], v[6:8], loads[2], loads[3], 1)
    sz, rz, _, _ = edge(v[0:2], v[4:6], load, load_z, MOVED + 1)

    def kept(c, x, z, odd):
        hi = jnp.maximum(c - MOVED, 0)
        below, jump, top = ((t + 1 - odd) >> 1 for t in (hi - z, hi, c - x))
        return below + jnp.maximum(top - jump, 0), below, jump

    n_own, own_gap, own_jump = kept(v[0], sx[0], sz[0], 0)
    n_got, got_gap, got_jump = kept(v[1], sx[1], sz[1], 1)
    for k, value in enumerate((n_own + n_got + rx[0] + rz[0], n_own, me_ref[0], n_own + n_got, own_gap, own_jump,
                               got_gap, got_jump, rx[0], sx[0], sz[0], v[0])):
        o_ref[k] = value


def first_row(n_ref, i, slots):
    j, k = i - n_ref[N_OWN], i - n_ref[N_POOL]
    own = 2 * jnp.where(i < n_ref[OWN_GAP], i, i - n_ref[OWN_GAP] + n_ref[OWN_JUMP])
    got = 2 * jnp.where(j < n_ref[GOT_GAP], j, j - n_ref[GOT_GAP] + n_ref[GOT_JUMP]) + 1
    moved = TP * slots + jnp.where(k < n_ref[FROM_X], k, k - n_ref[FROM_X] + MOVED)
    return jnp.where(j < 0, own, jnp.where(k < 0, got, moved))


def item_copy(flow, k, i, out=False):
    ref, buf, sem = flow[k]
    here, there = buf.at[i & 1], ref.at[i]
    return pltpu.make_async_copy(here, there, sem.at[i & 1]) if out else pltpu.make_async_copy(there, here, sem.at[i & 1])


def start_all(copies):
    for c in copies:
        c.start()
    return copies


def wait_all(copies):
    for c in copies:
        c.wait()


def first_items(ins):
    return start_all([item_copy(ins, k, 0) for k in range(len(ins))])


def stream(count, ins, outs, body):
    def turn(i, carry):
        @pl.when(i + 1 < count)
        def _():
            start_all([item_copy(ins, k, i + 1) for k in range(len(ins))])

        wait_all([item_copy(ins, k, i) for k in range(len(ins))])

        @pl.when(i >= 2)
        def _():
            wait_all([item_copy(outs, k, i - 2, True) for k in range(len(outs))])

        body(i, i & 1)
        start_all([item_copy(outs, k, i, True) for k in range(len(outs))])
        return carry

    lax.fori_loop(0, count, turn, 0)

    @pl.when(count >= 2)
    def _():
        wait_all([item_copy(outs, k, count - 2, True) for k in range(len(outs))])

    wait_all([item_copy(outs, k, count - 1, True) for k in range(len(outs))])


def natives_in(refs, bufs, sems):
    own, got, x, z = zip(refs, bufs)
    wide = [(v[1], start_all(in_pieces(*v, sems.at[k]))) for k, v in enumerate((own, got))]
    few = start_all([pltpu.make_async_copy(*v, sems.at[2, k]) for k, v in enumerate((x, z))])
    return wide, few


def by_rows(rows, step, body, first=0):
    def turn(k, carry):
        body(pl.multiple_of(first + k * step, 16), step)
        return carry

    lax.fori_loop(0, rows // step, turn, 0)
    if rows % step:
        body(first + rows - rows % step, rows % step)


def clear(ref):
    def part(at, rows):
        ref[pl.ds(at, rows), :] = jnp.zeros((rows, ref.shape[1]), ref.dtype)

    by_rows(ref.shape[0], 16, part)


PIECES = 4


def cut(rows):
    step = (rows // PIECES + TP) // 16 * 16
    return [(k, min(step, rows - k)) for k in range(0, rows, step)]


def in_pieces(src, dst, sems):
    return [pltpu.make_async_copy(src.at[pl.ds(at, count)], dst.at[pl.ds(at, count)], sems.at[k])
            for k, (at, count) in enumerate(cut(src.shape[0]))]


def fill_pool(own, got, pool, slots):
    rows = own[0].shape[0]

    def part(at, count):
        odd = lax.broadcasted_iota(jnp.int32, (count, 128), 0) & 1
        for j in range(D // 128):
            a, b = (v[0][pl.ds(at, count), 128 * j : 128 * j + 128].astype(f32) for v in (own, got))
            pool[j, pl.ds(at, count)] = jnp.where(odd == 0, a, b)

    for k, (at, count) in enumerate(cut(rows)):
        wait_all([own[1][k]] + ([got[1][k]] if got is not own else []))
        by_rows(count, TP, part, at)
    for j in range(D // 128):
        pool[j, rows : TP * slots] = jnp.zeros((TP * slots - rows, 128), f32)


def send_pool(buf, dst, sems, value):
    copies = in_pieces(buf, dst, sems)

    def part(at, count):
        for j in range(D // 128):
            buf[pl.ds(at, count), 128 * j : 128 * j + 128] = value(j, at, count).astype(bf16)

    for k, (at, count) in enumerate(cut(buf.shape[0])):
        by_rows(count, TP, part, at)
        copies[k].start()
    return copies


def read_rows(pool, at, slots):
    rows = pl.ds(at, TP, stride=slots)
    return jnp.concatenate([pool[j, rows, :] for j in range(D // 128)], axis=1)


def write_rows(pool, at, slots, value):
    rows = pl.ds(at, TP, stride=slots)
    for j in range(D // 128):
        pool[j, rows, :] = value[:, 128 * j : 128 * j + 128]


def fill_moved(x_ref, z_ref, pool, slots):
    for k, ref in enumerate((x_ref, z_ref)):
        for j in range(MOVED):
            write_rows(pool, TP * slots + k * MOVED + j, slots, ref[j].astype(f32))


def empty_moved(pool, slots, x_ref, z_ref):
    for k, ref in enumerate((x_ref, z_ref)):
        for j in range(MOVED):
            ref[j] = read_rows(pool, TP * slots + k * MOVED + j, slots).astype(bf16)


def fetch(n_ref, pieces, buf, sems):
    rows = pieces[0].shape[0]
    copies = []
    for k, piece in enumerate(pieces):
        at = pl.multiple_of((n_ref[ME] ^ k) * rows, 32)
        copies.append(pltpu.make_async_copy(piece, buf.at[pl.ds(at, rows)], sems.at[k]))
    return start_all(copies)


def finish(n_ref, acc, send_s, send_ref, keep_ref, pool, slots, natives, outs, sems, out_sems):
    pairs, rows = send_s.shape[0], send_s.shape[1]
    me = n_ref[ME] & 1
    copies = []
    for y in range(pairs):
        mine = pl.multiple_of((2 * y + me) * rows, 32)
        copies.append(pltpu.make_async_copy(acc.at[pl.ds(mine, rows)], keep_ref.at[y], sems.at[y]))
    start_all(copies)
    for y in range(pairs):
        theirs = pl.multiple_of((2 * y + 1 - me) * rows, 32)

        def part(at, count, y=y, theirs=theirs):
            send_s[y, pl.ds(at, count), :] = acc[pl.ds(pl.multiple_of(theirs + at, 16), count), :].astype(bf16)

        by_rows(rows, 16, part)
    copies += start_all([pltpu.make_async_copy(send_s, send_ref, sems.at[pairs])])
    copies += send_pool(natives[0], outs[0], out_sems, lambda j, at, count: pool[j, pl.ds(at, count)])
    empty_moved(pool, slots, *natives[1:])
    copies += start_all([pltpu.make_async_copy(natives[k], outs[k], sems.at[pairs + k]) for k in (1, 2)])
    wait_all(copies)


def attn_fwd_kernel(parts, slots, n_ref, *rest):
    sources, pieces, rest = rest[:4], rest[4 : 4 + parts], rest[4 + parts :]
    hbm, vec_ref, w, pool, natives, (native_sems, w_sems) = rest[:4], rest[4], rest[5], rest[6], rest[7:11], rest[11:13]
    bufs, sems = rest[13:17], rest[17:]
    wide, few = natives_in(sources, natives, native_sems)
    weights = fetch(n_ref, pieces, w, w_sems)
    fill_pool(*wide, pool, slots)
    wait_all(few)
    fill_moved(natives[2], natives[3], pool, slots)
    wait_all(weights)
    vec_ref[...] = w[:, 3 * D :].astype(f32).T[:16]

    def step(i, slot):
        x_ref, qkv_ref, o_ref, lse_ref = (v.at[slot] for v in bufs)
        x = read_rows(pool, first_row(n_ref, i, slots), slots)
        x_ref[...] = x.astype(bf16)
        n1, _ = norm(x)
        a = (n1 * vec_ref[0:1] + vec_ref[2:3]).astype(bf16)
        qb = jnp.concatenate([vec_ref[3:4], jnp.zeros((1, D), f32), vec_ref[4:5]], axis=1)
        qkv = (dot(a, w[:, : 3 * D]) + qb).astype(bf16)
        real = lax.broadcasted_iota(jnp.int32, (TP - TC, 3 * D), 0) < T - TC
        qkv_ref[:TC] = qkv[:TC]
        qkv_ref[TC:] = jnp.where(real, qkv[TC:], jnp.zeros_like(qkv[TC:]))
        lane = lax.broadcasted_iota(jnp.int32, (TP, 128), 1)
        low = lane < HD
        key = lax.broadcasted_iota(jnp.int32, (TP, TP), 1) < T
        for pair in range(H // 2):
            at = pair * 128
            q, k, v = (qkv_ref[:, off + at : off + at + 128] for off in (0, D, 2 * D))
            zero = jnp.zeros_like(q)
            o = None
            for side in range(2):
                sel = low if side == 0 else jnp.logical_not(low)
                s = jnp.where(key, dot_nt(jnp.where(sel, q, zero), k) * SCALE_LOG2E, -1e30)
                l2 = jnp.log2(jnp.sum(jnp.exp2(s), axis=-1, keepdims=True))
                p = jnp.exp2(s - l2).astype(bf16)
                part = dot(p, jnp.where(sel, v, zero))
                o = part if o is None else o + part
                lse_ref[:, pair * 2 + side : pair * 2 + side + 1] = l2
            o_ref[:, at : at + 128] = o.astype(bf16)

    stream(n_ref[N_ITEMS], (), tuple(zip(hbm, bufs, sems)), step)


FC = 256


def mlp_kernel(parts, slots, n_ref, xb_ref, ob_ref, *rest):
    sources, vec_ref, pieces, rest = rest[:4], rest[4], rest[5 : 5 + parts], rest[5 + parts :]
    dhb_ref, dob_ref, out_ref, ox_ref, oz_ref, send_ref, keep_ref, vb_ref = rest[:8]
    (w, acc, vg, gbu, cpool, opool, bu_s, c_s, dy_s, ct_s, dyt_s, zb, db, ub, eb, out_s, dc_s, send_s) = rest[8:26]
    natives, (native_sems, w_sems, end_sems, out_sems), bufs, sems = rest[26:30], rest[30:34], rest[34:38], rest[38:]
    flow = tuple(zip((xb_ref, ob_ref, dhb_ref, dob_ref), bufs, sems))
    wide, few = natives_in(sources, natives, native_sems)
    weights = fetch(n_ref, pieces, w, w_sems)
    first_items(flow[:2])
    clear(acc)
    vg[...] = jnp.zeros_like(vg)
    gbu[...] = jnp.zeros_like(gbu)
    bu_s[...] = jnp.concatenate([vec_ref[8 + j : 9 + j] for j in range(F // D)], axis=1)
    fill_pool(*wide, cpool, slots)
    wait_all(few)
    fill_moved(natives[2], natives[3], cpool, slots)
    wait_all(weights)

    def step(i, slot):
        x_ref, o_ref, dh_ref, do_ref = (v.at[slot] for v in bufs)
        at = first_row(n_ref, i, slots)
        g2, b2, bo, bd = vec_ref[1:2], vec_ref[6:7], vec_ref[5:6], vec_ref[7:8]
        x = x_ref[...].astype(f32)
        o = o_ref[...]
        h = x + dot(o, w[:, :D]) + bo
        n2, r2 = norm(h)
        c = (n2 * g2 + b2).astype(bf16)
        dyf = read_rows(cpool, at, slots)
        dy = dyf.astype(bf16)
        steps = F // FC
        c_s[...] = c
        dy_s[...] = dy
        ct_s[...] = c.T
        dyt_s[...] = dy.T

        def cols(base, j):
            return slice(base + j * FC, base + j * FC + FC)

        def produce(j, slot):
            zb[slot] = dot(c_s[...], w[:, cols(D, j)])
            db[slot] = dot(dy_s[...], w[:, cols(D + F, j)])

        def middle(j, slot):
            u, slope = gelu_parts(zb[slot] + bu_s[:, cols(0, j)])
            dz = db[slot] * slope
            gbu[:, cols(0, j)] += col8(dz)
            ub[slot] = u.astype(bf16)
            eb[slot] = dz.astype(bf16)

        def consume(j, slot, first=False):
            u, dzb = ub[slot], eb[slot]
            o1, d1 = dot_nt(u, w[:, cols(D + F, j)]), dot_nt(dzb, w[:, cols(D, j)])
            out_s[...] = o1 if first else out_s[...] + o1
            dc_s[...] = d1 if first else dc_s[...] + d1
            acc[:, cols(D, j)] += dot(ct_s[...], dzb)
            acc[:, cols(D + F, j)] += dot(dyt_s[...], u)

        produce(0, 0)
        produce(1, 1)
        middle(0, 0)
        for j in range(1, steps):
            if j + 1 < steps:
                produce(j + 1, (j + 1) % 3)
            consume(j - 1, (j - 1) % 3, j == 1)
            middle(j, j % 3)
        consume(steps - 1, (steps - 1) % 3)
        out, dc = out_s[...], dc_s[...]
        write_rows(opool, at, slots, h + out + bd)
        dh = dyf + norm_back(dc * g2, n2, r2)
        dh_ref[...] = dh
        dhb = dh.astype(bf16)
        acc[:, :D] += dot(o.T, dhb)
        do_ref[...] = dot_nt(dhb, w[:, :D]).astype(bf16)
        vg[0:8] += col8(dc * n2)
        vg[8:16] += col8(dh)
        vg[16:24] += col8(dc)
        vg[24:32] += col8(dyf)

    stream(n_ref[N_ITEMS], flow[:2], flow[2:], step)
    rows = [total(vg[8 * k : 8 * k + 8]) for k in range(4)]
    rows += [total(gbu[:, k * D : (k + 1) * D]) for k in range(F // D)]
    vb_ref[...] = jnp.concatenate(rows, axis=0)
    finish(n_ref, acc, send_s, send_ref, keep_ref, opool, slots, (natives[0], natives[2], natives[3]),
           (out_ref, ox_ref, oz_ref), end_sems, out_sems)


def attn_bwd_kernel(parts, slots, n_ref, xb_ref, qkvb_ref, lseb_ref, dob_ref, dhb_ref, vec_ref, vb_ref, *rest):
    pieces, rest = rest[:parts], rest[parts:]
    (out_ref, ox_ref, oz_ref, send_ref, keep_ref, w, acc, vg, dqkv, opool, sb, db, pb, gb, tb, qt, dot_, kt, vt, vsum,
     send_s) = rest[:21]
    natives, (w_sems, end_sems, out_sems), bufs, sems = rest[21:24], rest[24:27], rest[27:32], rest[32:]
    flow = tuple(zip((xb_ref, qkvb_ref, lseb_ref, dob_ref, dhb_ref), bufs, sems))
    first_items(flow)
    weights = fetch(n_ref, pieces, w, w_sems)
    clear(acc)
    vg[...] = jnp.zeros_like(vg)
    vsum[...] = jnp.zeros_like(vsum)
    wait_all(weights)

    def step(i, slot):
        x_ref, qkv_ref, lse_ref, do_ref, dh_ref = (v.at[slot] for v in bufs)
        g1, b1 = vec_ref[0:1], vec_ref[2:3]
        x = x_ref[...].astype(f32)
        n1, r1 = norm(x)
        at_ = (n1 * g1 + b1).astype(bf16).T
        low = lax.broadcasted_iota(jnp.int32, (TP, 128), 1) < HD
        real = lax.broadcasted_iota(jnp.int32, (TP - TC, D), 0) < T - TC

        def mask(h, v):
            return jnp.where(low if h % 2 == 0 else jnp.logical_not(low), v, jnp.zeros_like(v))

        def lanes(h, off=0):
            return slice(off + (h // 2) * 128, off + (h // 2) * 128 + 128)

        def produce(h):
            sb[h % 3] = dot_nt(mask(h, qkv_ref[:, lanes(h)]), qkv_ref[:, lanes(h, D)])
            db[h % 3] = dot_nt(mask(h, do_ref[:, lanes(h)]), qkv_ref[:, lanes(h, 2 * D)])

        def middle(h):
            p = jnp.exp2(sb[h % 3] * SCALE_LOG2E - lse_ref[:, h : h + 1])
            dp = db[h % 3]
            pb[h % 2] = p.astype(bf16)
            delta = jnp.sum(p * dp, axis=-1, keepdims=True)
            gb[h % 2] = (p * (dp - delta) * SCALE).astype(bf16)

        def rows_of(h):
            return slice(h * HD, h * HD + HD)

        qt[...] = qkv_ref[:, :D].T
        dot_[...] = do_ref[...].T

        def consume(h):
            ds = gb[h % 2]
            kt[rows_of(h), :] = dot(qt[rows_of(h), :], ds).astype(bf16)
            dv = dot(dot_[rows_of(h), :], pb[h % 2])
            vt[rows_of(h), :] = dv.astype(bf16)
            vsum[rows_of(h), :] += dv
            dq = dot(ds, mask(h, qkv_ref[:, lanes(h, D)]))
            if h % 2 == 0:
                tb[...] = dq
                return
            dq = tb[...] + dq
            dqkv[:, lanes(h)] = dq.astype(bf16)
            vg[16:24, lanes(h)] += col8(dq)

        produce(0)
        produce(1)
        middle(0)
        for h in range(1, H):
            if h + 1 < H:
                produce(h + 1)
            consume(h - 1)
            middle(h)
        consume(H - 1)
        for ref, off in ((kt, D), (vt, 2 * D)):
            v = ref[...].T
            dqkv[:TC, off : off + D] = v[:TC]
            dqkv[TC:, off : off + D] = jnp.where(real, v[TC:], jnp.zeros_like(v[TC:]))
        dqkv_b = dqkv[...]
        acc[:, : 3 * D] += dot(at_, dqkv_b)
        da = dot_nt(dqkv_b, w[:, : 3 * D])
        write_rows(opool, first_row(n_ref, i, slots), slots, dh_ref[...] + norm_back(da * g1, n1, r1))
        vg[0:8] += col8(da * n1)
        vg[8:16] += col8(da)

    stream(n_ref[N_ITEMS], flow, (), step)
    token = lax.broadcasted_iota(jnp.int32, (D, TP), 1) < T
    dv = jnp.sum(jnp.where(token, vsum[...], 0.0), axis=1, keepdims=True)
    mine = [total(vg[8 * k : 8 * k + 8]) for k in range(3)] + [jnp.broadcast_to(dv, (D, 128)).T[:1]]
    vb = vb_ref[...]
    rows = jnp.concatenate([mine[0], vb[0:1], mine[1], mine[2], mine[3], vb[1:8], jnp.zeros((116, D), f32)], axis=0)
    acc[:, 3 * D :] = rows.T
    finish(n_ref, acc, send_s, send_ref, keep_ref, opool, slots, natives, (out_ref, ox_ref, oz_ref), end_sems,
           out_sems)


def once(shape):
    return pl.BlockSpec(shape, lambda i, *n: (0,) * len(shape), pipeline_mode=pl.Buffered(1))


PLAN = pltpu.SMEM((12,), jnp.int32)


def planned(kernel):
    def run(*refs):
        make_plan(*refs[:5], refs[-1])
        kernel(refs[-1], *refs[5:-1])

    return run


def layer_call(kernel, n, slots, streams, ins, pieces, left, outs, scratch, sems, flow, flops):
    parts = len(pieces)
    items = [S((slots + 2 * MOVED,) + v.shape, v.dtype) for v in flow[len(streams):]]
    return pl.pallas_call(
        planned(lambda *refs: kernel(parts, slots, *refs)),
        out_shape=tuple(items) + tuple(left) + tuple(outs),
        grid_spec=pltpu.PrefetchScalarGridSpec(
            num_scalar_prefetch=5, grid=(1,),
            in_specs=[ANY] * len(streams) + [once(v.shape) if v.size <= 16 * D else ANY for v in ins] + [ANY] * parts,
            out_specs=tuple([ANY] * (len(items) + len(left)) + [once(v.shape) for v in outs]),
            scratch_shapes=list(scratch) + [pltpu.SemaphoreType.DMA(k if isinstance(k, tuple) else (k,)) for k in sems]
            + [pltpu.VMEM((2,) + v.shape, v.dtype) for v in flow] + [pltpu.SemaphoreType.DMA((2,)) for _ in flow]
            + [PLAN]),
        compiler_params=pltpu.CompilerParams(
            dimension_semantics=("arbitrary",), vmem_limit_bytes=VMEM_LIMIT),
        cost_estimate=pl.CostEstimate(flops=flops, bytes_accessed=20_000_000, transcendentals=0))(*n, *streams, *ins, *pieces)


FEW = S((MOVED, TP, D), bf16)
WIDE = S((TP, D), f32)
SLIM = S((TP, D), bf16)
QKV = S((TP, 3 * D), bf16)
LSE = S((TP, 128), f32)


def pool_of(slots):
    return pltpu.VMEM((D // 128, 2 * TP * slots, 128), f32)


def reduced(parts, cols):
    shape = (parts // 2, D // parts, cols)
    return S(shape, bf16), S(shape, f32)


def vmem(v):
    return pltpu.VMEM(v.shape, v.dtype)


def attn_fwd(n, slots, own, got, x, z, pieces):
    native = S(own.shape, bf16)
    return layer_call(
        attn_fwd_kernel, n, slots, (), (own, got, x, z), pieces, (), (S((16, D), f32),),
        (pltpu.VMEM((D, Q_COLS), bf16), pool_of(slots)) + tuple(vmem(v) for v in (native, native, FEW, FEW)),
        ((3, PIECES), len(pieces)), (SLIM, QKV, SLIM, LSE), 10_000_000_000)


def mlp(n, slots, x, o, c_own, c_got, c_x, c_z, vec, pieces):
    native, sums = S(c_own.shape, bf16), reduced(len(pieces), R_COLS)
    return layer_call(
        mlp_kernel, n, slots, (x, o), (c_own, c_got, c_x, c_z, vec), pieces, (native, FEW, FEW) + sums, (S((8, D), f32),),
        (pltpu.VMEM((D, R_COLS), bf16), pltpu.VMEM((D, R_COLS), f32), pltpu.VMEM((32, D), f32),
         pltpu.VMEM((8, F), f32), pool_of(slots), pool_of(slots),
         pltpu.VMEM((1, F), f32), pltpu.VMEM((TP, D), bf16), pltpu.VMEM((TP, D), bf16), pltpu.VMEM((D, TP), bf16),
         pltpu.VMEM((D, TP), bf16), pltpu.VMEM((3, TP, FC), f32), pltpu.VMEM((3, TP, FC), f32),
         pltpu.VMEM((3, TP, FC), bf16), pltpu.VMEM((3, TP, FC), bf16), pltpu.VMEM((TP, D), f32),
         pltpu.VMEM((TP, D), f32), vmem(sums[0])) + tuple(vmem(v) for v in (native, native, FEW, FEW)),
        ((3, PIECES), len(pieces), len(pieces) // 2 + 3, PIECES), (SLIM, SLIM, WIDE, SLIM), 25_000_000_000)


def attn_bwd(n, slots, x, qkv, lse, do, dh, vec, vb, pieces, rows):
    native, sums = S((rows, D), bf16), reduced(len(pieces), Q_COLS)
    return layer_call(
        attn_bwd_kernel, n, slots, (x, qkv, lse, do, dh), (vec, vb), pieces, (native, FEW, FEW) + sums, (),
        (pltpu.VMEM((D, Q_COLS), bf16), pltpu.VMEM((D, Q_COLS), f32), pltpu.VMEM((32, D), f32),
         pltpu.VMEM((TP, 3 * D), bf16), pool_of(slots), pltpu.VMEM((3, TP, TP), f32),
         pltpu.VMEM((3, TP, TP), f32), pltpu.VMEM((2, TP, TP), bf16), pltpu.VMEM((2, TP, TP), bf16),
         pltpu.VMEM((TP, 128), f32)) + (pltpu.VMEM((D, TP), bf16),) * 4 + (pltpu.VMEM((D, TP), f32), vmem(sums[0]))
        + tuple(vmem(v) for v in (native, FEW, FEW)),
        (len(pieces), len(pieces) // 2 + 3, PIECES), (SLIM, QKV, LSE, SLIM, WIDE), 20_000_000_000)


def pack_first_kernel(w_ref, g_ref, b_ref, o_ref):
    rows = w_ref.shape[0]
    vec = jnp.concatenate([g_ref[...], b_ref[...], jnp.zeros((128 - NV, rows), f32)], axis=0)
    o_ref[:, : 3 * D] = w_ref[...].astype(bf16)
    o_ref[:, 3 * D :] = vec.T.astype(bf16)


def pack_rest_kernel(p_ref, a_ref, b_ref, o_ref):
    o_ref[:, :D] = p_ref[...].astype(bf16)
    o_ref[:, D : D + F] = a_ref[...].astype(bf16)
    o_ref[:, D + F : D + 2 * F] = b_ref[...].astype(bf16)
    o_ref[:, D + 2 * F :] = jnp.zeros((o_ref.shape[0], R_COLS - D - 2 * F), bf16)


def split3(a):
    hi = a.astype(bf16)
    return hi, (a - hi.astype(f32)).astype(bf16)


def dot3(a, b):
    return dot(jnp.concatenate([a[0], a[1], a[0]], axis=1), jnp.concatenate([b[0], b[0], b[1]], axis=0))


def dot3_sym(a, b):
    left = jnp.concatenate([a[0], a[1], a[0]], axis=1)
    right = jnp.concatenate([b[0], b[0], b[1]], axis=0)
    wide = dot(left, right[:, :256])
    corner = dot(left[256:], right[:, 256:])
    return jnp.concatenate([wide, jnp.concatenate([wide[256:].T, corner], axis=0)], axis=1)


def orth_rows(m, a_s, q_s, at):
    wide, corner = dot_nt(m, m[:256]), dot_nt(m[256:], m[256:])
    a = jnp.concatenate([wide, jnp.concatenate([wide[256:].T, corner], axis=0)], axis=1)
    row, col = (lax.broadcasted_iota(jnp.int32, (D, D), k) for k in range(2))
    ssq = jnp.sum(jnp.where(row == col, a, 0.0), axis=(0, 1), keepdims=True)
    s = 1.0 / (jnp.sqrt(ssq) + ORTHO_EPSILON)
    a_s[...] = a * (s * s)
    row, col = (lax.broadcasted_iota(jnp.int32, q_s.shape, k) for k in range(2))
    q_s[...] = jnp.where(row + at == col, 1.0, 0.0)

    def turn(k, carry):
        a = a_s[...]
        parts = split3(a)
        row, col = (lax.broadcasted_iota(jnp.int32, (D, D), k) for k in range(2))
        p = split3(jnp.where(row == col, COEFF_FIRST, 0.0) + COEFF_SECOND * a + COEFF_THIRD * dot3_sym(parts, parts))
        q_s[...] = dot3(split3(q_s[...]), p)
        a_s[...] = dot3_sym(split3(dot3_sym(p, parts)), p)
        return carry

    lax.fori_loop(0, NS_ITERS - 1, turn, 0)
    parts, q = split3(a_s[...]), q_s[...]
    qa = dot3(split3(q), parts)
    q = COEFF_FIRST * q + COEFF_SECOND * qa + COEFF_THIRD * dot3(split3(qa), parts)
    hi, lo = split3(q * s)
    return dot(hi, m) + dot(lo, m)


def fetch_cols(n_ref, pieces, buf, sems, at_col, cols):
    rows = pieces[0].shape[0]
    copies = []
    for k, piece in enumerate(pieces):
        at = pl.multiple_of((n_ref[0] ^ k) * rows, 32)
        copies.append(pltpu.make_async_copy(
            piece.at[:, pl.ds(at_col, cols)], buf.at[pl.ds(at, rows), pl.ds(0, cols)], sems.at[k]))
    for c in copies:
        c.start()
    for c in copies:
        c.wait()


def orth_both(n_ref, mine_ref, theirs_ref, m, a_s, q_s, o_s):
    rows = mine_ref.shape[0]
    core = n_ref[0] & 1
    at = pl.multiple_of((n_ref[0] - core) * rows, 32)
    o_s[...] = orth_rows(m[...], a_s, q_s, at)
    mine_ref[...] = o_s[pl.ds(pl.multiple_of(core * rows, 32), rows), :]
    theirs_ref[...] = o_s[pl.ds(pl.multiple_of((1 - core) * rows, 32), rows), :]


def orth_mlp_kernel(parts, n_ref, *rest):
    pieces = rest[:parts]
    mine_ref, theirs_ref, m, a_s, q_s, o_s, sems = rest[parts:]
    fetch_cols(n_ref, pieces, m, sems, pl.multiple_of((n_ref[0] & 1) * F, 128), F)
    orth_both(n_ref, mine_ref, theirs_ref, m, a_s, q_s, o_s)


def orth_attn_kernel(parts, n_ref, *rest):
    pieces = rest[:parts]
    mine_ref, theirs_ref, m, a_s, q_s, o_s, sems = rest[parts:]

    @pl.when(n_ref[0] & 1 == 0)
    def _():
        fetch_cols(n_ref, pieces, m, sems, 0, 3 * D)

    @pl.when(n_ref[0] & 1 == 1)
    def _():
        m[:, D:] = jnp.zeros((D, 2 * D), bf16)
        fetch_cols(n_ref, pieces, m, sems, 3 * D, D)

    orth_both(n_ref, mine_ref, theirs_ref, m, a_s, q_s, o_s)


def orth_call(kernel, me, pieces, cols):
    parts = len(pieces)
    rows = pieces[0].shape[0]
    spec = pl.BlockSpec((rows, cols), lambda i, n: (0, 0))
    return pl.pallas_call(
        lambda *refs: kernel(parts, *refs),
        out_shape=(S((rows, cols), f32),) * 2,
        grid_spec=pltpu.PrefetchScalarGridSpec(
            num_scalar_prefetch=1, grid=(1,), in_specs=[ANY] * parts, out_specs=(spec,) * 2,
            scratch_shapes=[pltpu.VMEM((D, cols), bf16), pltpu.VMEM((D, D), f32), pltpu.VMEM((2 * rows, D), f32), pltpu.VMEM((2 * rows, cols), f32),
                            pltpu.SemaphoreType.DMA((parts,))]),
        compiler_params=pltpu.CompilerParams(vmem_limit_bytes=VMEM_LIMIT),
        cost_estimate=pl.CostEstimate(flops=8_000_000_000, bytes_accessed=4_000_000, transcendentals=0))(me, *pieces)


def swap(v, axis, k):
    return lax.ppermute(v, axis, [(i, i ^ k) for i in range(lax.axis_size(axis))])


def bits(axis):
    return range(lax.axis_size(axis).bit_length() - 1)


def bit(axis, b):
    return (lax.axis_index(axis) >> b) & 1


def all_pieces(v, axis):
    pieces = {0: v}
    for b in reversed(bits(axis)):
        pieces.update({k ^ (1 << b): swap(p, axis, 1 << b) for k, p in list(pieces.items())})
    return [pieces[k] for k in range(lax.axis_size(axis))]


def take(v, i):
    return lax.dynamic_index_in_dim(v, i, 0, keepdims=False)


def sum_blocks(send, keep):
    got = swap(send, "fsdp", 1)
    keep, got = (v.reshape((2, -1) + v.shape[1:]) for v in (keep, got))
    for b in reversed(bits("fsdp")[1:]):
        me = bit("fsdp", b)
        sent = (take(keep, 1 - me) + take(got, 1 - me).astype(f32)).astype(bf16)
        own = take(keep, me) + take(got, me).astype(f32)
        got = swap(sent, "fsdp", 1 << b)
        keep = own
        if keep.shape[0] > 1:
            keep, got = (v.reshape((2, -1) + v.shape[1:]) for v in (keep, got))
    return (keep + got.astype(f32)).reshape(keep.shape[-2:])


def halves(v, axis):
    n = v.shape[axis] // 2
    return lax.slice_in_dim(v, 0, n, axis=axis), lax.slice_in_dim(v, n, 2 * n, axis=axis)


def sum_groups(v):
    for b in bits("rep"):
        me = bit("rep", b)
        lo, hi = halves(v, 1 if b == 0 else 0)
        got = swap(jnp.where(me == 0, hi, lo).astype(bf16), "rep", 1 << b)
        v = jnp.where(me == 0, lo, hi) + got.astype(f32)
    v = v.astype(bf16)
    for b in reversed(bits("rep")):
        me = bit("rep", b)
        got = swap(v, "rep", 1 << b)
        v = jnp.concatenate([jnp.where(me == 0, v, got), jnp.where(me == 0, got, v)], axis=1 if b == 0 else 0)
    return v


def sum_groups_whole(v):
    v = v.astype(bf16)
    for b in bits("rep"):
        got = swap(v, "rep", 1 << b)
        v = (v.astype(f32) + got.astype(f32)).astype(bf16)
    return v


def pick_kernel(slots, count_ref, a_ref, b_ref, ax_ref, az_ref, bx_ref, bz_ref, pool, *rest):
    bufs, sems = rest[:2], rest[2]
    both = [(buf, start_all(in_pieces(ref, buf, sems.at[k]))) for k, (ref, buf) in enumerate(zip((a_ref, b_ref), bufs))]
    for v, x_ref, z_ref in zip(both, (ax_ref, bx_ref), (az_ref, bz_ref)):
        fill_pool(v, v, pool, slots)
        for j in range(MOVED):
            x_ref[j] = read_rows(pool, jnp.maximum(count_ref[0] - 1 - j, 0), slots).astype(bf16)
            z_ref[j] = read_rows(pool, jnp.maximum(count_ref[0] - MOVED - 1 - j, 0), slots).astype(bf16)


def pool_call(kernel, scalars, slots, ins, outs, scratch):
    native = ins[0].shape
    spec = lambda v: ANY if v.shape == native else once(v.shape)
    return pl.pallas_call(
        kernel, out_shape=outs,
        grid_spec=pltpu.PrefetchScalarGridSpec(
            num_scalar_prefetch=len(scalars), grid=(1,), in_specs=[spec(v) for v in ins],
            out_specs=tuple(spec(v) for v in outs),
            scratch_shapes=[pltpu.VMEM((D // 128, TP * slots, 128), f32), pltpu.VMEM(native, bf16), pltpu.VMEM(native, bf16),
                            pltpu.SemaphoreType.DMA((3, PIECES))] + list(scratch)),
        compiler_params=pltpu.CompilerParams(vmem_limit_bytes=VMEM_LIMIT),
        cost_estimate=pl.CostEstimate(flops=1_000_000, bytes_accessed=7_000_000, transcendentals=0))(*scalars, *ins)


def unpool_kernel(slots, n_ref, own_ref, got_ref, x_ref, z_ref, o_ref, pool, own, got, sems):
    wide = [(buf, start_all(in_pieces(ref, buf, sems.at[k]))) for k, (ref, buf) in enumerate(((own_ref, own), (got_ref, got)))]
    fill_pool(*wide, pool, slots)
    for j in range(MOVED):
        for ref, given, at in ((x_ref, TO_X, 1), (z_ref, TO_Z, MOVED + 1)):
            @pl.when(j < n_ref[given])
            def _(ref=ref, at=at):
                write_rows(pool, n_ref[COUNT] - at - j, slots, ref[j].astype(f32))

    def live(j, at, count):
        slot = lax.broadcasted_iota(jnp.int32, (count, 128), 0) & (slots - 1)
        return jnp.where(slot < n_ref[COUNT], pool[j, pl.ds(at, count)], 0.0)

    wait_all(send_pool(own, o_ref, sems.at[2], live))


def adam_kernel(scale, g_ref, *refs):
    ins, outs = refs[:6], refs[6:]
    g = (g_ref[...].astype(f32) * scale).T
    for k, (lo, hi) in enumerate(((0, 2), (2, NV))):
        gradient, parameter = g[lo:hi], ins[k][...]
        first = ADAM_FIRST * ins[2 + 2 * k][...] + (1.0 - ADAM_FIRST) * gradient
        second = ADAM_SECOND * ins[3 + 2 * k][...] + (1.0 - ADAM_SECOND) * gradient * gradient
        first_hat = first / (1.0 - ADAM_FIRST**ADAM_STEP)
        second_hat = second / (1.0 - ADAM_SECOND**ADAM_STEP)
        outs[k][...] = gradient
        outs[2 + k][...] = parameter - ADAM_RATE * (
            first_hat / (jnp.sqrt(second_hat) + ADAM_EPSILON) + ADAM_DECAY * parameter)
        outs[4 + 2 * k][...] = first
        outs[5 + 2 * k][...] = second


def adam(last, devices, *states):
    full = [pl.BlockSpec(v.shape, lambda i: (0, 0)) for v in states]
    one, two = S(states[0].shape, f32), S(states[1].shape, f32)
    return pl.pallas_call(
        lambda *refs: adam_kernel(1.0 / devices, *refs),
        grid=(1,), out_shape=(one, two, one, two, one, one, two, two),
        in_specs=[pl.BlockSpec((last.shape[0], 128), lambda i: (0, 3 * D // 128))] + full,
        out_specs=tuple(full[k] for k in (0, 1, 0, 1, 2, 3, 4, 5)), name="adam")(last, *states)


def muon_factor(row_total, column_total):
    return math.sqrt(max(1.0, row_total / column_total))


def body(images, cotangent, counts, w_qkv, w_proj, w_fc1, w_fc2, gains, biases,
         mom_qkv, mom_proj, mom_fc1, mom_fc2, gains_first, gains_second, biases_first, biases_second):
    slots = images.shape[0]
    rows = w_qkv.shape[0]
    devices = lax.axis_size("rep") * lax.axis_size("fsdp")
    me = lax.axis_index("fsdp").astype(jnp.int32)

    first = pl.pallas_call(pack_first_kernel, out_shape=S((rows, Q_COLS), bf16), name="pack_first")(w_qkv, gains, biases)
    q_pieces = all_pieces(first, "fsdp")

    pair = jnp.concatenate([counts, swap(counts, "fsdp", 1)])
    n = (me.reshape(1), pair) + tuple(swap(pair, "rep", k) for k in (1, 2, 3))

    own = [v.transpose(1, 0, 2).reshape(-1, D) for v in (images, cotangent)]
    offers = pool_call(lambda *refs: pick_kernel(slots, *refs), (counts,), slots, own, (FEW,) * 4, ())

    def spread(v, to_x, to_z):
        return v, swap(v, "fsdp", 1), swap(to_x, "rep", 1), swap(to_z, "rep", 2)

    x_in = spread(own[0], *offers[:2])
    c_in = spread(own[1], *offers[2:])

    def unpool(v, to_x, to_z):
        ins = (v, swap(v, "fsdp", 1), swap(to_x, "rep", 1), swap(to_z, "rep", 2))
        (full,) = pool_call(planned(lambda *refs: unpool_kernel(slots, *refs)), n, slots, ins, (S(v.shape, bf16),), (PLAN,))
        return full.reshape(-1, slots, D).transpose(1, 0, 2)

    rest = pl.pallas_call(pack_rest_kernel, out_shape=S((rows, R_COLS), bf16), name="pack_rest")(w_proj, w_fc1, w_fc2.T)
    r_pieces = all_pieces(rest, "fsdp")

    x, qkv, o, lse, vec = attn_fwd(n, slots, *x_in, q_pieces)
    dh, do, *out, r_send, r_keep, vb = mlp(n, slots, x, o, *c_in, vec, r_pieces)
    mid = sum_blocks(r_send, r_keep)
    *in_grad, q_send, q_keep = attn_bwd(n, slots, x, qkv, lse, do, dh, vec, vb, q_pieces, x_in[0].shape[0])
    mid = sum_groups(mid)
    last = sum_groups_whole(sum_blocks(q_send, q_keep))
    block_out = unpool(*out)
    input_grad = unpool(*in_grad)

    vectors = adam(last, devices, gains, biases, gains_first, gains_second, biases_first, biases_second)
    scale = 1.0 / devices
    grad_qkv = last[:, : 3 * D].astype(f32) * scale
    grad_proj, grad_fc1, grad_fc2t = (
        mid[:, lo:hi].astype(f32) * scale for lo, hi in ((0, D), (D, D + F), (D + F, D + 2 * F)))
    next_qkv = MUON_MOMENTUM * mom_qkv + grad_qkv
    next_proj = MUON_MOMENTUM * mom_proj + grad_proj
    next_fc1 = MUON_MOMENTUM * mom_fc1 + grad_fc1
    next_fc2t = MUON_MOMENTUM * mom_fc2.T + grad_fc2t
    attn_pieces = all_pieces(jnp.concatenate([next_qkv.astype(bf16), next_proj.astype(bf16)], axis=1), "fsdp")
    mlp_pieces = all_pieces(jnp.concatenate([next_fc1.astype(bf16), next_fc2t.astype(bf16)], axis=1), "fsdp")

    core = me & 1
    mine, theirs = orth_call(orth_attn_kernel, me.reshape(1), attn_pieces, 3 * D)
    got = swap(theirs, "fsdp", 1)
    orth_qkv, orth_proj = jnp.where(core == 0, mine, got), jnp.where(core == 0, got, mine)[:, :D]
    mine, theirs = orth_call(orth_mlp_kernel, me.reshape(1), mlp_pieces, F)
    got = swap(theirs, "fsdp", 1)
    orth_fc1, orth_fc2t = jnp.where(core == 0, mine, got), jnp.where(core == 0, got, mine)
    new_qkv = w_qkv - MUON_RATE * muon_factor(D, 3 * D) * orth_qkv
    new_proj = w_proj - MUON_RATE * muon_factor(D, D) * orth_proj
    new_fc1 = w_fc1 - MUON_RATE * muon_factor(D, F) * orth_fc1
    new_fc2t = w_fc2.T - MUON_RATE * muon_factor(F, D) * orth_fc2t
    grad_gains, grad_biases, new_gains, new_biases = vectors[:4]
    return (block_out, input_grad, grad_qkv, grad_proj, grad_fc1, grad_fc2t.T, grad_gains, grad_biases,
            new_qkv, new_proj, new_fc1, new_fc2t.T, new_gains, new_biases,
            next_qkv, next_proj, next_fc1, next_fc2t.T) + tuple(vectors[4:])


def solution(mesh):
    in_specs = (
        P(("rep", "fsdp"), None, None),
        P(("rep", "fsdp"), None, None),
        P(("rep", "fsdp")),
        P("fsdp", None),
        P("fsdp", None),
        P("fsdp", None),
        P(None, "fsdp"),
        P(None, "fsdp"),
        P(None, "fsdp"),
        P("fsdp", None),
        P("fsdp", None),
        P("fsdp", None),
        P(None, "fsdp"),
        P(None, "fsdp"),
        P(None, "fsdp"),
        P(None, "fsdp"),
        P(None, "fsdp"),
    )
    out_specs = (
        P(("rep", "fsdp"), None, None),
        P(("rep", "fsdp"), None, None),
        P("fsdp", None),
        P("fsdp", None),
        P("fsdp", None),
        P(None, "fsdp"),
        P(None, "fsdp"),
        P(None, "fsdp"),
        P("fsdp", None),
        P("fsdp", None),
        P("fsdp", None),
        P(None, "fsdp"),
        P(None, "fsdp"),
        P(None, "fsdp"),
        P("fsdp", None),
        P("fsdp", None),
        P("fsdp", None),
        P(None, "fsdp"),
        P(None, "fsdp"),
        P(None, "fsdp"),
        P(None, "fsdp"),
        P(None, "fsdp"),
    )
    return jax.shard_map(body, mesh=mesh, in_specs=in_specs, out_specs=out_specs, check_vma=False)
```
